32 devices in a mesh: grp: 4 (over y, x), rep: 8 (over z, core).
Axes of the slice: x: 2, y: 2, z: 4, core: 2. Of those that a mesh axis runs over, the one named last changes fastest.
Arguments:
- inputs: bfloat16 [8, 512, 768], P('rep', 'grp'), may hold values from -6 to 6
- qkv_weight: bfloat16 [768, 2304], P('grp'), may hold values from -0.21650635 to 0.21650635
- qkv_bias: bfloat16 [2304], P('grp'), may hold values from -3 to 3
- out_weight: bfloat16 [768, 768], P('grp'), may hold values from -0.625 to 0.625
- out_bias: bfloat16 [768], P('grp'), may hold values from -3 to 3
- up_weight: bfloat16 [768, 3072], P('grp'), may hold values from -0.21875 to 0.21875
- up_bias: bfloat16 [3072], P('grp'), may hold values from -3 to 3
- down_weight: bfloat16 [3072, 768], P('grp'), may hold values from -0.109375 to 0.109375
- down_bias: bfloat16 [768], P('grp'), may hold values from -3 to 3
- attn_gain: bfloat16 [768], P('grp'), may hold values from 0.5 to 1.5
- attn_shift: bfloat16 [768], P('grp'), may hold values from -2 to 2
- mlp_gain: bfloat16 [768], P('grp'), may hold values from 0.5 to 1.5
- mlp_shift: bfloat16 [768], P('grp'), may hold values from -2 to 2
- cotangent: float32 [8, 512, 768], P('rep', 'grp'), may hold values from -6 to 6
Outputs:
- block_out: float32 [8, 512, 768], P('rep', 'grp')
- input_grad: float32 [8, 512, 768], P('rep', 'grp')
- qkv_weight_grad: float32 [768, 2304], P('grp')
- qkv_bias_grad: float32 [2304], P('grp')
- out_weight_grad: float32 [768, 768], P('grp')
- out_bias_grad: float32 [768], P('grp')
- up_weight_grad: float32 [768, 3072], P('grp')
- up_bias_grad: float32 [3072], P('grp')
- down_weight_grad: float32 [3072, 768], P('grp')
- down_bias_grad: float32 [768], P('grp')
- attn_gain_grad: float32 [768], P('grp')
- attn_shift_grad: float32 [768], P('grp')
- mlp_gain_grad: float32 [768], P('grp')
- mlp_shift_grad: float32 [768], P('grp')
The draws below stay inside these ranges and needn't reach their ends.
All inputs are finite; a program needn't handle non-finite values.
Results may differ from the reference program's by a relative error of at most 0.0093.
Values may be sent and summed in bfloat16 or wider, within the bound.
A program may use at most 128 MiB of HBM per device.

```python
import jax
import jax.numpy as jnp
from jax import lax

D = 768
HEADS = 12
HD = 64
ROT = 16
FF = 3072
SEQ = 512
SEQS = 8


def draw_inputs(key, part):
    base = jnp.clip(jax.random.normal(jax.random.fold_in(key, 11), (SEQS, SEQ, D), jnp.float32), -6.0, 6.0)
    return base.astype(jnp.bfloat16)


def draw_qkv_weight(key, part):
    base = jnp.clip(jax.random.normal(jax.random.fold_in(key, 21), (D, 3 * D), jnp.float32), -6.0, 6.0) * D ** (-0.5)
    return base.astype(jnp.bfloat16)


def block_scale(own_key, dims, cuts, smallest, top_value):
    level, own = 1.0, jax.random.fold_in(own_key, 6)
    for position, shards_of in cuts:
        heights = jnp.exp(jax.random.uniform(jax.random.fold_in(own, position), (shards_of,), jnp.float32, smallest / len(cuts), top_value / len(cuts)))
        level = level * jnp.repeat(heights, dims[position] // shards_of).reshape([-1 if axis == position else 1 for axis in range(len(dims))])
    return level


def normal_values(own_key, dims, spread, most, cuts=(), held_as=jnp.bfloat16):
    array = spread * jax.random.normal(own_key, dims, jnp.float32)
    if cuts:
        array = array * block_scale(own_key, dims, cuts, -0.22, 0.18)
    return jnp.clip(array, -most, most).astype(held_as)


def setup_inputs(seed: int = 0) -> dict:
    keys = jax.random.split(jax.random.key(seed), 15)
    return {
        "inputs": draw_inputs(jax.random.fold_in(keys[14], 71), 0),
        "qkv_weight": draw_qkv_weight(jax.random.fold_in(keys[14], 71), 0),
        "qkv_bias": normal_values(keys[2], (3 * D,), 0.5, 3.0, ((0, 4),)),
        "out_weight": normal_values(keys[3], (D, D), (max(1, D // 8)) ** -0.5, 0.625, ((0, 4),)),
        "out_bias": normal_values(keys[4], (D,), 0.5, 3.0, ((0, 4),)),
        "up_weight": normal_values(keys[5], (D, FF), D ** -0.5, 0.21875, ((0, 4),)),
        "up_bias": normal_values(keys[6], (FF,), 0.5, 3.0, ((0, 4),)),
        "down_weight": normal_values(keys[7], (FF, D), FF ** -0.5, 0.109375, ((0, 4),)),
        "down_bias": normal_values(keys[8], (D,), 0.5, 3.0, ((0, 4),)),
        "attn_gain": jnp.clip(1.0 + 0.1 * jax.random.normal(keys[9], (D,), jnp.float32), 0.5, 1.5).astype(jnp.bfloat16),
        "attn_shift": normal_values(keys[10], (D,), 0.3, 2.0, ((0, 4),)),
        "mlp_gain": jnp.clip(1.0 + 0.1 * jax.random.normal(keys[11], (D,), jnp.float32), 0.5, 1.5).astype(jnp.bfloat16),
        "mlp_shift": normal_values(keys[12], (D,), 0.3, 2.0, ((0, 4),)),
        "cotangent": normal_values(keys[13], (SEQS, SEQ, D), 1.0, 6.0, ((0, 8), (1, 4)), jnp.float32),
    }


eps = 1e-05

def layer_norm(values):
    centered = values - lax.optimization_barrier(jnp.mean(values, axis=-1, keepdims=True))
    variance = lax.optimization_barrier(jnp.mean(centered * centered, axis=-1, keepdims=True))
    inverse = lax.rsqrt(variance + eps)
    return (centered * inverse, inverse)

def gelu_parts(preact):
    normal_cdf = 0.5 * (1.0 + jax.scipy.special.erf(preact * 0.7071067811865476))
    density = jnp.exp(-0.5 * preact * preact) * 0.3989422804014327
    return (preact * normal_cdf, normal_cdf + preact * density)

def angle_tables(positions):
    half_rot = ROT // 2
    frequency = 10000.0 ** (-jnp.arange(half_rot, dtype=jnp.float32) * (2.0 / ROT))
    angles = positions.astype(jnp.float32)[:, None] * frequency[None, :]
    return (jnp.cos(angles)[:, None, :], jnp.sin(angles)[:, None, :])

def rotate(tensor, cos_table, sin_table):
    half_rot = ROT // 2
    lower_part = tensor[..., :half_rot]
    upper_part = tensor[..., half_rot:ROT]
    return jnp.concatenate([lower_part * cos_table - upper_part * sin_table, upper_part * cos_table + lower_part * sin_table, tensor[..., ROT:]], axis=-1)

def unrotate(tensor, cos_table, sin_table):
    half_rot = ROT // 2
    lower_part = tensor[..., :half_rot]
    upper_part = tensor[..., half_rot:ROT]
    return jnp.concatenate([lower_part * cos_table + upper_part * sin_table, upper_part * cos_table - lower_part * sin_table, tensor[..., ROT:]], axis=-1)

def widen(tensor):
    return lax.optimization_barrier(tensor).astype(jnp.float32)

def reference(inputs, qkv_weight, qkv_bias, out_weight, out_bias, up_weight, up_bias, down_weight, down_bias, attn_gain, attn_shift, mlp_gain, mlp_shift, cotangent):
    positions = jnp.arange(SEQ, dtype=jnp.int32)
    cos_table, sin_table = angle_tables(positions)
    visible = positions[None, :] <= positions[:, None]
    score_scale = HD ** (-0.5)
    gain_attn = attn_gain.astype(jnp.float32)
    shift_attn = attn_shift.astype(jnp.float32)
    gain_mlp = mlp_gain.astype(jnp.float32)
    shift_mlp = mlp_shift.astype(jnp.float32)

    def one_sequence(carry, operands):
        sequence, grad_out = operands
        hidden_in = sequence.astype(jnp.float32)
        normed, inverse = layer_norm(hidden_in)
        attn_in = (normed * gain_attn + shift_attn).astype(jnp.bfloat16)
        mlp_in = (normed * gain_mlp + shift_mlp).astype(jnp.bfloat16)
        qkv = jnp.dot(attn_in, qkv_weight, preferred_element_type=jnp.float32) + qkv_bias.astype(jnp.float32)
        query_b = rotate(qkv[:, :D].reshape(SEQ, HEADS, HD), cos_table, sin_table).astype(jnp.bfloat16)
        keys_b = rotate(qkv[:, D:2 * D].reshape(SEQ, HEADS, HD), cos_table, sin_table).astype(jnp.bfloat16)
        values_b = qkv[:, 2 * D:].reshape(SEQ, HEADS, HD).astype(jnp.bfloat16)
        query_w = widen(query_b)
        keys_w = widen(keys_b)
        values_w = widen(values_b)
        scores = jnp.einsum('qhd,khd->hqk', query_w, keys_w) * score_scale
        scores = jnp.where(visible[None], scores, -jnp.inf)
        row_max = lax.optimization_barrier(jnp.max(scores, axis=-1, keepdims=True))
        log_total = row_max + jnp.log(lax.optimization_barrier(jnp.sum(jnp.exp(scores - row_max), axis=-1, keepdims=True)))
        attn_probs = jnp.exp(scores - log_total)
        probs_w = widen(attn_probs.astype(jnp.bfloat16))
        context = jnp.einsum('hqk,khd->qhd', probs_w, values_w).astype(jnp.bfloat16).reshape(SEQ, D)
        attn_out = jnp.dot(context, out_weight, preferred_element_type=jnp.float32) + out_bias.astype(jnp.float32)
        preact = jnp.dot(mlp_in, up_weight, preferred_element_type=jnp.float32) + up_bias.astype(jnp.float32)
        activation, slope = gelu_parts(preact)
        act_b = activation.astype(jnp.bfloat16)
        mlp_out = jnp.dot(act_b, down_weight, preferred_element_type=jnp.float32) + down_bias.astype(jnp.float32)
        block_out = hidden_in + attn_out + mlp_out
        grad_b = grad_out.astype(jnp.bfloat16)
        down_grad = jnp.dot(act_b.T, grad_b, preferred_element_type=jnp.float32)
        out_grad = jnp.dot(context.T, grad_b, preferred_element_type=jnp.float32)
        bias_sum = lax.optimization_barrier(jnp.sum(grad_out, axis=0))
        preact_grad = jnp.dot(grad_b, down_weight.T, preferred_element_type=jnp.float32) * slope
        up_bias_grad = lax.optimization_barrier(jnp.sum(preact_grad, axis=0))
        preact_b = preact_grad.astype(jnp.bfloat16)
        up_grad = jnp.dot(mlp_in.T, preact_b, preferred_element_type=jnp.float32)
        mlp_in_grad = jnp.dot(preact_b, up_weight.T, preferred_element_type=jnp.float32)
        context_grad = jnp.dot(grad_b, out_weight.T, preferred_element_type=jnp.float32).astype(jnp.bfloat16).reshape(SEQ, HEADS, HD)
        context_w = widen(context_grad)
        prob_grad = jnp.einsum('qhd,khd->hqk', context_w, values_w)
        row_dot = lax.optimization_barrier(jnp.sum(attn_probs * prob_grad, axis=-1, keepdims=True))
        score_grad = widen((attn_probs * (prob_grad - row_dot) * score_scale).astype(jnp.bfloat16))
        query_grad = jnp.einsum('hqk,khd->qhd', score_grad, keys_w)
        key_grad = jnp.einsum('hqk,qhd->khd', score_grad, query_w)
        value_grad = jnp.einsum('hqk,qhd->khd', probs_w, context_w)
        qkv_rows = jnp.concatenate([unrotate(query_grad, cos_table, sin_table).reshape(SEQ, D), unrotate(key_grad, cos_table, sin_table).reshape(SEQ, D), value_grad.reshape(SEQ, D)], axis=1)
        qkv_bias_grad = lax.optimization_barrier(jnp.sum(qkv_rows, axis=0))
        qkv_rows_b = qkv_rows.astype(jnp.bfloat16)
        qkv_grad = jnp.dot(attn_in.T, qkv_rows_b, preferred_element_type=jnp.float32)
        attn_in_grad = jnp.dot(qkv_rows_b, qkv_weight.T, preferred_element_type=jnp.float32)
        attn_gain_grad = lax.optimization_barrier(jnp.sum(attn_in_grad * normed, axis=0))
        attn_shift_grad = lax.optimization_barrier(jnp.sum(attn_in_grad, axis=0))
        mlp_gain_grad = lax.optimization_barrier(jnp.sum(mlp_in_grad * normed, axis=0))
        mlp_shift_grad = lax.optimization_barrier(jnp.sum(mlp_in_grad, axis=0))
        normed_grad = attn_in_grad * gain_attn + mlp_in_grad * gain_mlp
        input_grad = grad_out + inverse * (normed_grad - lax.optimization_barrier(jnp.mean(normed_grad, axis=-1, keepdims=True)) - normed * lax.optimization_barrier(jnp.mean(normed_grad * normed, axis=-1, keepdims=True)))
        pieces = (qkv_grad, qkv_bias_grad, out_grad, bias_sum, up_grad, up_bias_grad, down_grad, bias_sum, attn_gain_grad, attn_shift_grad, mlp_gain_grad, mlp_shift_grad)
        updated = tuple((summed + portion for summed, portion in zip(carry, pieces)))
        return (updated, (block_out, input_grad))
    shapes = ((D, 3 * D), (3 * D,), (D, D), (D,), (D, FF), (FF,), (FF, D), (D,), (D,), (D,), (D,), (D,))
    starting = tuple((jnp.zeros(shape_one, jnp.float32) for shape_one in shapes))
    totals, (block_outs, input_grads) = lax.scan(one_sequence, starting, (inputs, cotangent))
    return (block_outs, input_grads, totals[0], totals[1], totals[2], totals[3], totals[4], totals[5], totals[6], totals[7], totals[8], totals[9], totals[10], totals[11])
```

```python
import jax
import jax.numpy as jnp
import numpy as np
from jax import lax
from jax.experimental import pallas as pl
from jax.experimental.pallas import tpu as pltpu
from jax.sharding import PartitionSpec as P

D = 768
HEADS = 12
HD = 64
ROT = 16


eps = 1e-05


def layer_norm(values):
    centered = values - jnp.mean(values, axis=-1, keepdims=True)
    variance = jnp.mean(centered * centered, axis=-1, keepdims=True)
    inverse = lax.rsqrt(variance + eps)
    return (centered * inverse, inverse)


def gelu_parts(preact):
    normal_cdf = 0.5 * (1.0 + jax.scipy.special.erf(preact * 0.7071067811865476))
    density = jnp.exp(-0.5 * preact * preact) * 0.3989422804014327
    return (preact * normal_cdf, normal_cdf + preact * density)


def angle_tables(positions):
    half_rot = ROT // 2
    frequency = 10000.0 ** (-jnp.arange(half_rot, dtype=jnp.float32) * (2.0 / ROT))
    angles = positions.astype(jnp.float32)[:, None] * frequency[None, :]
    return (jnp.cos(angles)[:, None, :], jnp.sin(angles)[:, None, :])


def rotate(tensor, cos_table, sin_table):
    half_rot = ROT // 2
    lower_part = tensor[..., :half_rot]
    upper_part = tensor[..., half_rot:ROT]
    return jnp.concatenate(
        [
            lower_part * cos_table - upper_part * sin_table,
            upper_part * cos_table + lower_part * sin_table,
            tensor[..., ROT:],
        ],
        axis=-1,
    )


def unrotate(tensor, cos_table, sin_table):
    half_rot = ROT // 2
    lower_part = tensor[..., :half_rot]
    upper_part = tensor[..., half_rot:ROT]
    return jnp.concatenate(
        [
            lower_part * cos_table + upper_part * sin_table,
            upper_part * cos_table - lower_part * sin_table,
            tensor[..., ROT:],
        ],
        axis=-1,
    )


def local_by_tokens(
    inputs,
    qkv_weight,
    qkv_bias,
    out_weight,
    out_bias,
    up_weight,
    up_bias,
    down_weight,
    down_bias,
    attn_gain,
    attn_shift,
    mlp_gain,
    mlp_shift,
    cotangent,
):
    tokens = inputs.shape[1]
    (
        full_qkv,
        full_qkv_bias,
        full_out,
        full_out_bias,
        full_up,
        full_up_bias,
        full_down,
        full_down_bias,
        gain_attn,
        shift_attn,
        gain_mlp,
        shift_mlp,
    ) = (
        lax.all_gather(qkv_weight, "grp", axis=0, tiled=True),
        lax.all_gather(qkv_bias, "grp", axis=0, tiled=True),
        lax.all_gather(out_weight, "grp", axis=0, tiled=True),
        lax.all_gather(out_bias, "grp", axis=0, tiled=True),
        lax.all_gather(up_weight, "grp", axis=0, tiled=True),
        lax.all_gather(up_bias, "grp", axis=0, tiled=True),
        lax.all_gather(down_weight, "grp", axis=0, tiled=True),
        lax.all_gather(down_bias, "grp", axis=0, tiled=True),
        lax.all_gather(attn_gain, "grp", axis=0, tiled=True),
        lax.all_gather(attn_shift, "grp", axis=0, tiled=True),
        lax.all_gather(mlp_gain, "grp", axis=0, tiled=True),
        lax.all_gather(mlp_shift, "grp", axis=0, tiled=True),
    )
    first_row = lax.axis_index("grp") * tokens
    positions = first_row + jnp.arange(tokens, dtype=jnp.int32)
    cos_table, sin_table = angle_tables(positions)
    score_scale = HD ** (-0.5)
    hidden_in = inputs[0].astype(jnp.float32)
    normed, inverse = layer_norm(hidden_in)
    attn_in = (normed * gain_attn.astype(jnp.float32) + shift_attn.astype(jnp.float32)).astype(
        jnp.bfloat16
    )
    mlp_in = (normed * gain_mlp.astype(jnp.float32) + shift_mlp.astype(jnp.float32)).astype(
        jnp.bfloat16
    )
    qkv = jnp.dot(attn_in, full_qkv, preferred_element_type=jnp.float32) + full_qkv_bias.astype(
        jnp.float32
    )
    query_b = rotate(qkv[:, :D].reshape(tokens, HEADS, HD), cos_table, sin_table).astype(
        jnp.bfloat16
    )
    keys_local = (
        rotate(qkv[:, D : 2 * D].reshape(tokens, HEADS, HD), cos_table, sin_table)
        .astype(jnp.bfloat16)
        .reshape(tokens, D)
    )
    values_local = qkv[:, 2 * D :].astype(jnp.bfloat16)
    keys_all, values_all = (
        lax.all_gather(keys_local, "grp", axis=0, tiled=True),
        lax.all_gather(values_local, "grp", axis=0, tiled=True),
    )
    length = keys_all.shape[0]
    visible = jnp.arange(length, dtype=jnp.int32)[None, :] <= positions[:, None]
    query_heads = jnp.transpose(query_b, (1, 0, 2))
    key_heads = jnp.transpose(keys_all.reshape(length, HEADS, HD), (1, 0, 2))
    value_heads = jnp.transpose(values_all.reshape(length, HEADS, HD), (1, 0, 2))

    def forward_head(operands):
        query_one, key_one, value_one = operands
        scores = jnp.dot(query_one, key_one.T, preferred_element_type=jnp.float32) * score_scale
        scores = jnp.where(visible, scores, -jnp.inf)
        row_max = jnp.max(scores, axis=-1, keepdims=True)
        log_total = row_max + jnp.log(jnp.sum(jnp.exp(scores - row_max), axis=-1, keepdims=True))
        probs_b = jnp.exp(scores - log_total).astype(jnp.bfloat16)
        context_one = jnp.dot(probs_b, value_one, preferred_element_type=jnp.float32).astype(
            jnp.bfloat16
        )
        return (context_one, log_total)

    context_heads, log_totals = lax.map(forward_head, (query_heads, key_heads, value_heads))
    context = jnp.transpose(context_heads, (1, 0, 2)).reshape(tokens, D)
    attn_out = jnp.dot(
        context, full_out, preferred_element_type=jnp.float32
    ) + full_out_bias.astype(jnp.float32)
    preact = jnp.dot(mlp_in, full_up, preferred_element_type=jnp.float32) + full_up_bias.astype(
        jnp.float32
    )
    activation, slope = gelu_parts(preact)
    act_b = activation.astype(jnp.bfloat16)
    mlp_out = jnp.dot(act_b, full_down, preferred_element_type=jnp.float32) + full_down_bias.astype(
        jnp.float32
    )
    block_out = hidden_in + attn_out + mlp_out
    back_qkv, back_out, back_up, back_down, back_gain_attn, back_gain_mlp = (
        lax.all_gather(qkv_weight, "grp", axis=0, tiled=True),
        lax.all_gather(out_weight, "grp", axis=0, tiled=True),
        lax.all_gather(up_weight, "grp", axis=0, tiled=True),
        lax.all_gather(down_weight, "grp", axis=0, tiled=True),
        lax.all_gather(attn_gain, "grp", axis=0, tiled=True),
        lax.all_gather(mlp_gain, "grp", axis=0, tiled=True),
    )
    grad_out = cotangent[0]
    grad_b = grad_out.astype(jnp.bfloat16)
    down_grad = jnp.dot(act_b.T, grad_b, preferred_element_type=jnp.float32)
    out_grad = jnp.dot(context.T, grad_b, preferred_element_type=jnp.float32)
    bias_sum = jnp.sum(grad_out, axis=0)
    preact_grad = jnp.dot(grad_b, back_down.T, preferred_element_type=jnp.float32) * slope
    up_bias_grad = jnp.sum(preact_grad, axis=0)
    preact_b = preact_grad.astype(jnp.bfloat16)
    up_grad = jnp.dot(mlp_in.T, preact_b, preferred_element_type=jnp.float32)
    mlp_in_grad = jnp.dot(preact_b, back_up.T, preferred_element_type=jnp.float32)
    context_grad = jnp.dot(grad_b, back_out.T, preferred_element_type=jnp.float32).astype(
        jnp.bfloat16
    )
    context_grad_heads = jnp.transpose(context_grad.reshape(tokens, HEADS, HD), (1, 0, 2))

    def backward_head(operands):
        query_one, key_one, value_one, grad_one, log_total = operands
        scores = jnp.dot(query_one, key_one.T, preferred_element_type=jnp.float32) * score_scale
        scores = jnp.where(visible, scores, -jnp.inf)
        attn_probs = jnp.exp(scores - log_total)
        probs_b = attn_probs.astype(jnp.bfloat16)
        prob_grad = jnp.dot(grad_one, value_one.T, preferred_element_type=jnp.float32)
        row_dot = jnp.sum(attn_probs * prob_grad, axis=-1, keepdims=True)
        score_grad = (attn_probs * (prob_grad - row_dot) * score_scale).astype(jnp.bfloat16)
        query_grad = jnp.dot(score_grad, key_one, preferred_element_type=jnp.float32)
        key_grad = jnp.dot(score_grad.T, query_one, preferred_element_type=jnp.float32)
        value_grad = jnp.dot(probs_b.T, grad_one, preferred_element_type=jnp.float32)
        return (query_grad, key_grad, value_grad)

    query_grads, key_grads, value_grads = lax.map(
        backward_head, (query_heads, key_heads, value_heads, context_grad_heads, log_totals)
    )
    key_full = jnp.transpose(key_grads, (1, 0, 2)).reshape(length, D)
    value_full = jnp.transpose(value_grads, (1, 0, 2)).reshape(length, D)
    key_mine, value_mine = (
        lax.psum_scatter(key_full, "grp", scatter_dimension=0, tiled=True),
        lax.psum_scatter(value_full, "grp", scatter_dimension=0, tiled=True),
    )
    query_rows = unrotate(jnp.transpose(query_grads, (1, 0, 2)), cos_table, sin_table).reshape(
        tokens, D
    )
    key_rows = unrotate(key_mine.reshape(tokens, HEADS, HD), cos_table, sin_table).reshape(
        tokens, D
    )
    qkv_rows = jnp.concatenate([query_rows, key_rows, value_mine], axis=1)
    qkv_bias_grad = jnp.sum(qkv_rows, axis=0)
    qkv_rows_b = qkv_rows.astype(jnp.bfloat16)
    qkv_grad = jnp.dot(attn_in.T, qkv_rows_b, preferred_element_type=jnp.float32)
    attn_in_grad = jnp.dot(qkv_rows_b, back_qkv.T, preferred_element_type=jnp.float32)
    attn_gain_grad = jnp.sum(attn_in_grad * normed, axis=0)
    attn_shift_grad = jnp.sum(attn_in_grad, axis=0)
    mlp_gain_grad = jnp.sum(mlp_in_grad * normed, axis=0)
    mlp_shift_grad = jnp.sum(mlp_in_grad, axis=0)
    normed_grad = attn_in_grad * back_gain_attn.astype(
        jnp.float32
    ) + mlp_in_grad * back_gain_mlp.astype(jnp.float32)
    input_grad = grad_out + inverse * (
        normed_grad
        - jnp.mean(normed_grad, axis=-1, keepdims=True)
        - normed * jnp.mean(normed_grad * normed, axis=-1, keepdims=True)
    )
    group_parts = (
        lax.psum_scatter(qkv_grad, "grp", scatter_dimension=0, tiled=True),
        lax.psum_scatter(qkv_bias_grad, "grp", scatter_dimension=0, tiled=True),
        lax.psum_scatter(out_grad, "grp", scatter_dimension=0, tiled=True),
        lax.psum_scatter(bias_sum, "grp", scatter_dimension=0, tiled=True),
        lax.psum_scatter(up_grad, "grp", scatter_dimension=0, tiled=True),
        lax.psum_scatter(up_bias_grad, "grp", scatter_dimension=0, tiled=True),
        lax.psum_scatter(down_grad, "grp", scatter_dimension=0, tiled=True),
        lax.psum_scatter(attn_gain_grad, "grp", scatter_dimension=0, tiled=True),
        lax.psum_scatter(attn_shift_grad, "grp", scatter_dimension=0, tiled=True),
        lax.psum_scatter(mlp_gain_grad, "grp", scatter_dimension=0, tiled=True),
        lax.psum_scatter(mlp_shift_grad, "grp", scatter_dimension=0, tiled=True),
    )
    (
        qkv_part,
        qkv_bias_part,
        out_part,
        bias_part,
        up_part,
        up_bias_part,
        down_part,
        gain_attn_part,
        shift_attn_part,
        gain_mlp_part,
        shift_mlp_part,
    ) = group_parts
    (
        qkv_total,
        qkv_bias_total,
        out_total,
        bias_total,
        up_total,
        up_bias_total,
        down_total,
        gain_attn_total,
        shift_attn_total,
        gain_mlp_total,
        shift_mlp_total,
    ) = lax.psum(
        (
            qkv_part,
            qkv_bias_part,
            out_part,
            bias_part,
            up_part,
            up_bias_part,
            down_part,
            gain_attn_part,
            shift_attn_part,
            gain_mlp_part,
            shift_mlp_part,
        ),
        "rep",
    )
    return (
        block_out[None],
        input_grad[None],
        qkv_total,
        qkv_bias_total,
        out_total,
        bias_total,
        up_total,
        up_bias_total,
        down_total,
        bias_total,
        gain_attn_total,
        shift_attn_total,
        gain_mlp_total,
        shift_mlp_total,
    )


ROWS = 96
SHARD = 192
MESH = pl.DeviceIdType.MESH
NSEM = 128


def mm(a, b):
    return lax.dot_general(a, b, (((1,), (0,)), ((), ())), preferred_element_type=jnp.float32)


def mm_tn(a, b):
    return lax.dot_general(a, b, (((0,), (0,)), ((), ())), preferred_element_type=jnp.float32)


def mm_nt(a, b):
    return lax.dot_general(a, b, (((1,), (1,)), ((), ())), preferred_element_type=jnp.float32)


def keep_192(t):
    lane = lax.broadcasted_iota(jnp.int32, t.shape, 1)
    return jnp.where(lane < SHARD, t, 0.0)


def block_of(t, j):
    base = (j // 2) * 384
    if j % 2 == 0:
        return keep_192(t[:, base : base + 256])
    return keep_192(pltpu.roll(t[:, base + 128 : base + 384], 192, 1))


def pair_of(a, b):
    shifted = pltpu.roll(b, 64, 1)
    return jnp.concatenate([a[:, :128], shifted[:, :128] + a[:, 128:], shifted[:, 128:]], axis=1)


def gelu_with_slope(preact):
    normal_cdf = 0.5 * (1.0 + lax.erf(preact * 0.7071067811865476))
    density = jnp.exp(-0.5 * preact * preact) * 0.3989422804014327
    return preact * normal_cdf, normal_cdf + preact * density


def block_kernel(
    x_ref, small_ref, cos_ref, sin_lo_ref, sin_hi_ref, bup_ref,
    ct_hbm, wqkv_hbm, wup_hbm, wdown_hbm, wout_hbm,
    block_ref, igrad_ref, gqkv_ref, gout_ref, gup_ref, gdown_ref, vec_ref,
    ct, w_qkv_in, w_down, w_out, w_pack, w_qkv, w_up,
    x_all, g_all, small_all, normed, attn_in, mlp_in,
    acc_a, acc_b, acc_c, acc_d, act_b, preact_b,
    q_b, k_b, v_b, cg_b, ctx_f, ctx_b, s_buf, dp_buf, p_b, ds_b, dq_f, dk_f, dv_f, rows_b,
    down_own, up_full, qkv_full, out_full,
    part_send, part_recv, tq_send, tq_recv, tu_send, chunk, z_in, z_sum, z_other,
    rs_out, rs_out_in, rs_in, rs_in_in,
    vec_send, vec_recv, vec_core, vec_z,
    send_sem, recv_sem, local_sem,
):
    f32, bf16 = jnp.float32, jnp.bfloat16
    me = lax.axis_index("grp")
    rep = lax.axis_index("rep")
    z, core = rep // 2, rep % 2
    mx, my = me % 2, me // 2
    inner = (z == 1) | (z == 2)
    outer = (z == 0) | (z == 3)
    peers = {1: my * 2 + (1 - mx), 2: (1 - my) * 2 + mx, 3: (1 - my) * 2 + (1 - mx)}
    twin = (me, z * 2 + (1 - core))
    z_pair = (me, (z + 1 - 2 * (z % 2)) * 2 + core)
    z_mid = (me, (3 - z) * 2 + core)

    def group(d):
        return (peers[d], rep)

    def z_peer(d):
        return (me, ((z + d) % 4) * 2 + core)

    names = {}

    def remote(name, src, dst, device):
        i = names.setdefault(name, len(names))
        assert i < NSEM
        return pltpu.make_async_remote_copy(
            src_ref=src, dst_ref=dst, send_sem=send_sem.at[i], recv_sem=recv_sem.at[i],
            device_id=device, device_id_type=MESH,
        )

    pending = []

    def send(name, src, dst, device):
        copy = remote(name, src, dst, device)
        copy.start()
        pending.append(copy)
        return copy

    def at(start, size, multiple=None):
        return pl.ds(pl.multiple_of(start, multiple or size), size)

    barrier = pltpu.get_barrier_semaphore()
    everyone = [group(d) for d in (1, 2, 3)] + [twin] + [z_peer(d) for d in (1, 2, 3)]
    for device in everyone:
        pl.semaphore_signal(barrier, inc=1, device_id=device, device_id_type=MESH)

    locals_ = [
        pltpu.make_async_copy(ct_hbm, ct, local_sem.at[0]),
        pltpu.make_async_copy(wqkv_hbm, w_qkv_in, local_sem.at[1]),
        pltpu.make_async_copy(wdown_hbm, w_down, local_sem.at[2]),
        pltpu.make_async_copy(wout_hbm, w_out, local_sem.at[3]),
        pltpu.make_async_copy(
            wup_hbm.at[:, at(me * D, D, 128)], w_up.at[at(me * SHARD, SHARD)], local_sem.at[4]
        ),
    ]
    for copy in locals_:
        copy.start()
    pl.semaphore_wait(barrier, len(everyone))

    mine = at(me * 128, 128)
    half = at(me * SHARD + core * ROWS, ROWS)
    small_in, x_in, g_in, up_in, qkv_in = {}, {}, {}, {}, {}
    for d in (3, 1, 2):
        small_in[d] = send(("small", d), small_ref, small_all.at[me], group(d))
    for d in (3, 1, 2):
        x_in[d] = send(("x", d), x_ref, x_all.at[mine], group(d))
    for d in (3, 1, 2):
        up_in[d] = send(
            ("up", d),
            wup_hbm.at[at(core * ROWS, ROWS), at(peers[d] * D, D, 128)],
            w_up.at[half],
            group(d),
        )
    x_all[mine, :] = x_ref[...]
    small_all[me] = small_ref[...]
    locals_[0].wait()
    g_all[mine, :] = ct[...].astype(bf16)
    for d in (3, 1, 2):
        g_in[d] = send(("g", d), g_all.at[mine], g_all.at[mine], group(d))
    locals_[1].wait()

    @pl.loop(0, SHARD // 32)
    def _(i):
        rows = at(i * 32, 32)
        wide = w_qkv_in[rows, :].astype(f32)
        for j in range(4):
            a, b, c = (block_of(wide[:, t * D : (t + 1) * D], j) for t in range(3))
            w_pack[j, rows, :] = jnp.concatenate([pair_of(a, b), c], axis=1).astype(bf16)

    for d in (3, 1, 2):
        qkv_in[d] = send(
            ("qkv", d), w_pack.at[peers[d], at(core * ROWS, ROWS)], w_qkv.at[half], group(d)
        )
    w_qkv[at(me * SHARD, SHARD), :] = w_pack[me]

    for d in (1, 2, 3):
        small_in[d].wait_recv()
    vectors = sum(small_all[i].astype(f32) for i in range(4))
    gain_attn, shift_attn = vectors[5:6], vectors[6:7]
    gain_mlp, shift_mlp = vectors[7:8], vectors[8:9]
    bias_qkv = jnp.zeros((1, 640), f32)
    for j in range(4):
        a, b, c = (block_of(vectors[t : t + 1], j) for t in range(3))
        bias_qkv = jnp.where(me == j, jnp.concatenate([pair_of(a, b), c], axis=1), bias_qkv)
    bias_up = bup_ref[...].astype(f32)

    def norm_rows(start):
        @pl.loop(0, 128 // 16)
        def _(i):
            rows = pl.ds(pl.multiple_of(start + i * 16, 16), 16)
            t = x_all[rows, :].astype(f32)
            centered = t - jnp.mean(t, axis=1, keepdims=True)
            inverse = lax.rsqrt(jnp.mean(centered * centered, axis=1, keepdims=True) + eps)
            n = centered * inverse
            normed[rows, :] = n
            attn_in[rows, :] = (n * gain_attn + shift_attn).astype(bf16)
            mlp_in[rows, :] = (n * gain_mlp + shift_mlp).astype(bf16)

    norm_rows(me * 128)
    for d in (1, 2, 3):
        x_in[d].wait_recv()
        norm_rows(peers[d] * 128)

    def share_weight(arrived, name, buffer):
        twins = []
        for d in (1, 2, 3):
            arrived[d].wait_recv()
            rows = at(peers[d] * SHARD + core * ROWS, ROWS)
            twins.append(send((name, d), buffer.at[rows], buffer.at[rows], twin))
        return twins

    up_twins = share_weight(up_in, "up2", w_up)
    locals_[4].wait()
    for copy in up_twins:
        copy.wait_recv()

    acc_a[...] = mm(mlp_in[...], w_up[...])

    @pl.loop(0, 512 // 16)
    def _(i):
        rows = at(i * 16, 16)
        activation, slope = gelu_with_slope(acc_a[rows, :] + bias_up)
        act_b[rows, :] = activation.astype(bf16)
        acc_a[rows, :] = slope

    locals_[2].wait()
    locals_[3].wait()
    acc_b[...] = mm(act_b[...], w_down[...])

    for d in (1, 2, 3):
        g_in[d].wait_recv()
    g = g_all[...]
    other_cols = at((1 - core) * 384, 384)
    own_cols = at(core * 384, 384)

    part_send[0:384, :] = mm_tn(act_b[:, other_cols], g).astype(bf16)
    down_part = send("part_down", part_send.at[0:384], part_recv.at[0:384], twin)
    down_own[...] = mm_tn(act_b[:, own_cols], g)
    acc_c[...] = mm_nt(g, w_down[...])

    def slope_rows(i, total):
        rows = at(i * 16, 16)
        pg = acc_c[rows, :] * acc_a[rows, :]
        preact_b[rows, :] = pg.astype(bf16)
        return total + pg[:8] + pg[8:]

    up_bias_part = lax.fori_loop(0, 512 // 16, slope_rows, jnp.zeros((8, D), f32))
    up_bias_part = jnp.sum(up_bias_part, axis=0, keepdims=True)

    up_full[...] = mm_tn(mlp_in[...], preact_b[...])
    for j in range(4):
        part_send[384 + j * ROWS : 384 + (j + 1) * ROWS, :] = up_full[
            at(j * SHARD + (1 - core) * ROWS, ROWS), :
        ].astype(bf16)
    up_part = send("part_up", part_send.at[384:768], part_recv.at[384:768], twin)

    def total_ref(k, which):
        if k < 4:
            return gdown_ref.at[at(which * 384 + k * ROWS, ROWS)]
        if k < 8:
            return gup_ref.at[at(which * ROWS, ROWS), (k - 4) * D : (k - 3) * D]
        if k == 8:
            return gout_ref.at[at(which * ROWS, ROWS)]
        return gqkv_ref.at[at(which * ROWS, ROWS), (k - 9) * D : (k - 8) * D]

    def z_first(k):
        @pl.when(outer)
        def _():
            remote(("z1", k), chunk.at[k], z_in.at[k], z_pair).start()

    def z_second(k):
        @pl.when(inner)
        def _():
            remote(("z1", k), chunk.at[k], z_in.at[k], z_pair).wait_recv()
            z_sum[k] = (chunk[k].astype(f32) + z_in[k].astype(f32)).astype(bf16)
            remote(("z2", k), z_sum.at[k], z_other.at[k], z_mid).start()

    def z_third(k):
        own = total_ref(k, core)

        @pl.when(inner)
        def _():
            remote(("z2", k), z_sum.at[k], z_other.at[k], z_mid).wait_recv()
            own[...] = (z_sum[k].astype(f32) + z_other[k].astype(f32)).astype(bf16)
            remote(("z3", k), own, own, z_pair).start()

        @pl.when(outer)
        def _():
            remote(("z3", k), own, own, z_pair).wait_recv()

        remote(("last", k), own, own, twin).start()

    def z_finish(k):
        own = total_ref(k, core)
        last = remote(("last", k), own, own, twin)
        last.wait_send()
        remote(("last", k), total_ref(k, 1 - core), total_ref(k, 1 - core), twin).wait_recv()

        @pl.when(inner)
        def _():
            remote(("z2", k), z_sum.at[k], z_other.at[k], z_mid).wait_send()
            remote(("z3", k), own, own, z_pair).wait_send()

        @pl.when(outer)
        def _():
            remote(("z1", k), chunk.at[k], z_in.at[k], z_pair).wait_send()

    down_part.wait_recv()
    for k in range(4):
        rows = pl.ds(k * ROWS, ROWS)
        chunk[k] = (down_own[rows, :] + part_recv[rows, :].astype(f32)).astype(bf16)
        z_first(k)

    acc_c[...] = mm_nt(preact_b[...], w_up[...])
    cg_b[...] = jnp.zeros_like(cg_b)
    cg_b[:, :SHARD] = mm_nt(g, w_out[...]).astype(bf16)

    up_part.wait_recv()
    for j in range(4):
        tu_send[j] = (
            up_full[at(j * SHARD + core * ROWS, ROWS), :]
            + part_recv[384 + j * ROWS : 384 + (j + 1) * ROWS, :].astype(f32)
        ).astype(bf16)
    chunk[4 + me] = tu_send[me]
    tu_in = {d: send(("tu", d), tu_send.at[peers[d]], chunk.at[4 + me], group(d)) for d in (3, 1, 2)}

    qkv_twins = share_weight(qkv_in, "qkv2", w_qkv)
    z_second(0)
    for copy in qkv_twins:
        copy.wait_recv()
    qkv_full[...] = mm(attn_in[...], w_qkv[...])
    z_second(1)

    def turn(t, cos, lo, hi):
        return t * cos + pltpu.roll(t, 376, 1) * lo + pltpu.roll(t, 8, 1) * hi

    def tables(rows):
        return tuple(
            jnp.concatenate([ref[rows, :]] * 3, axis=1) for ref in (cos_ref, sin_lo_ref, sin_hi_ref)
        )

    @pl.loop(0, 512 // 16)
    def _(i):
        rows = at(i * 16, 16)
        t = qkv_full[rows, :] + bias_qkv
        cos, lo, hi = tables(rows)
        qk = turn(t[:, :384], cos, lo, hi)
        q_b[rows, :] = (keep_192(qk[:, :256]) * 0.125).astype(bf16)
        k_b[rows, :] = keep_192(pltpu.roll(qk[:, 128:384], 192, 1)).astype(bf16)
        v_b[rows, :] = keep_192(t[:, 384:640]).astype(bf16)

    ctx_f[...] = jnp.zeros_like(ctx_f)
    dq_f[...] = jnp.zeros_like(dq_f)
    dk_f[...] = jnp.zeros_like(dk_f)
    dv_f[...] = jnp.zeros_like(dv_f)
    lane256 = lax.broadcasted_iota(jnp.int32, (1, 256), 1)
    for h in range(3):
        mask = ((lane256 >= h * 64) & (lane256 < (h + 1) * 64)).astype(bf16)
        for block in range(2):
            keys = (block + 1) * 256
            rows_q = slice(block * 256, (block + 1) * 256)
            q_h = q_b[rows_q, :] * mask
            cg_h = cg_b[rows_q, :] * mask
            s_buf[:, :keys] = mm_nt(q_h, k_b[:keys, :])
            dp_buf[:, :keys] = mm_nt(cg_h, v_b[:keys, :])

            @pl.loop(0, 256 // 16)
            def _(i, keys=keys, block=block):
                rows = at(i * 16, 16)
                s = s_buf[rows, :keys]
                key_at = lax.broadcasted_iota(jnp.int32, (16, keys), 1)
                query_at = lax.broadcasted_iota(jnp.int32, (16, keys), 0) + (block * 256 + i * 16)
                s = jnp.where(key_at <= query_at, s, -jnp.inf)
                e = jnp.exp(s - jnp.max(s, axis=1, keepdims=True))
                p = e * (1.0 / jnp.sum(e, axis=1, keepdims=True))
                dp = dp_buf[rows, :keys]
                row_dot = jnp.sum(p * dp, axis=1, keepdims=True)
                p_b[rows, :keys] = p.astype(bf16)
                ds_b[rows, :keys] = (p * (dp - row_dot)).astype(bf16)

            ctx_f[rows_q, :] += mm(p_b[:, :keys], v_b[:keys, :] * mask)
            dq_f[rows_q, :] += mm(ds_b[:, :keys], k_b[:keys, :] * mask)
            dk_f[:keys, :] += mm_tn(ds_b[:, :keys], q_h)
            dv_f[:keys, :] += mm_tn(p_b[:, :keys], cg_h)
        if h < 2:
            z_second(2 + h)
        if h > 0:
            z_third(h - 1)

    ctx_b[...] = ctx_f[...].astype(bf16)

    acc_b[...] += mm(ctx_b[:, :SHARD], w_out[...])
    rs_out[...] = acc_b[...].astype(bf16)
    out_in = {
        d: send(("rs_out", d), rs_out.at[at(peers[d] * 128, 128)], rs_out_in.at[d - 1], group(d))
        for d in (3, 1, 2)
    }
    out_full[...] = mm_tn(ctx_b[:, :SHARD], g)
    part_send[768 : 768 + ROWS, :] = out_full[at((1 - core) * ROWS, ROWS), :].astype(bf16)
    out_part = send("part_out", part_send.at[768:864], part_recv.at[768:864], twin)

    def unturn_rows(i, totals):
        rows = at(i * 16, 16)
        cos, lo, hi = tables(rows)
        qk = pair_of(dq_f[rows, :] * 0.125, dk_f[rows, :])
        qk = turn(qk, cos, -lo, -hi)
        full = jnp.concatenate([qk, dv_f[rows, :]], axis=1)
        rows_b[rows, :] = full.astype(bf16)
        return totals + full[:8] + full[8:]

    qkv_bias_part = lax.fori_loop(0, 512 // 16, unturn_rows, jnp.zeros((8, 640), f32))
    qkv_bias_part = jnp.sum(qkv_bias_part, axis=0, keepdims=True)

    qkv_full2 = mm_tn(attn_in[...], rows_b[...])
    acc_d[:, :640] = qkv_full2
    for j in range(4):
        tq_send[4 + j] = acc_d[at(j * SHARD + (1 - core) * ROWS, ROWS), :640].astype(bf16)
    qkv_part = send("part_qkv", tq_send.at[4:8], tq_recv.at[4:8], twin)
    out_part.wait_recv()
    chunk[8] = (out_full[at(core * ROWS, ROWS), :] + part_recv[768:864, :].astype(f32)).astype(bf16)
    qkv_part.wait_recv()
    for j in range(4):
        tq_send[j] = (
            acc_d[at(j * SHARD + core * ROWS, ROWS), :640] + tq_recv[4 + j].astype(f32)
        ).astype(bf16)
    tq_recv[me] = tq_send[me]
    tq_in = {d: send(("tq", d), tq_send.at[peers[d]], tq_recv.at[me], group(d)) for d in (3, 1, 2)}
    for d in (1, 2, 3):
        tu_in[d].wait_recv()
    for k in range(4, 9):
        z_first(k)
    z_third(2)

    acc_b_in = mm_nt(rows_b[...], w_qkv[...])
    acc_d[0:512, :] = acc_b_in

    def norm_grad_rows(i, totals):
        rows = at(i * 16, 16)
        ag, mg, n = acc_d[rows, :], acc_c[rows, :], normed[rows, :]
        both = ag * gain_attn + mg * gain_mlp
        acc_c[rows, :] = both
        rs_in[rows, :] = both.astype(bf16)
        new = (ag * n, ag, mg * n, mg)
        return tuple(t + v[:8] + v[8:] for t, v in zip(totals, new))

    sums = lax.fori_loop(0, 512 // 16, norm_grad_rows, (jnp.zeros((8, D), f32),) * 4)
    in_in = {
        d: send(("rs_in", d), rs_in.at[at(peers[d] * 128, 128)], rs_in_in.at[d - 1], group(d))
        for d in (3, 1, 2)
    }
    z_third(3)
    z_second(4)

    def rows_sum(t):
        return jnp.sum(t, axis=0, keepdims=True)

    wide = jnp.concatenate(
        [rows_sum(ct[...])] + [rows_sum(t) for t in sums] + [jnp.zeros((3, D), f32)], axis=0
    )
    types = [
        keep_192(qkv_bias_part[:, :256]),
        keep_192(pltpu.roll(qkv_bias_part[:, 128:384], 192, 1)),
        keep_192(qkv_bias_part[:, 384:640]),
    ]
    for j in range(4):
        vec_send[j] = block_of(wide, j)
        for t in range(3):
            b = 3 * j + t
            vec_send[j, 5 + t : 6 + t, :] = jnp.where(me == b % 4, types[b // 4], 0.0)
    vec_in = {d: send(("vec", d), vec_send.at[peers[d]], vec_recv.at[d - 1], group(d)) for d in (3, 1, 2)}
    z_second(5)
    for d in (1, 2, 3):
        vec_in[d].wait_recv()
    vec_core[core, 0:8, :] = vec_send[me] + (vec_recv[0] + vec_recv[1] + vec_recv[2])
    vec_core[core, 8:16, :] = jnp.concatenate(
        [up_bias_part[:, t * 256 : (t + 1) * 256] for t in range(3)] + [jnp.zeros((5, 256), f32)], axis=0
    )
    vec_twin = send("vec_twin", vec_core.at[core], vec_core.at[core], twin)
    vec_twin.wait_recv()
    vec_z[z] = vec_core[0] + vec_core[1]
    vec_zs = [send(("vec_z", d), vec_z.at[z], vec_z.at[z], z_peer(d)) for d in (1, 2, 3)]

    for d in (1, 2, 3):
        out_in[d].wait_recv()
    bias = vectors[3:4] + vectors[4:5]

    @pl.loop(0, 128 // 16)
    def _(i):
        rows = at(i * 16, 16)
        total = acc_b[pl.ds(pl.multiple_of(me * 128 + i * 16, 16), 16), :]
        for d in range(3):
            total = total + rs_out_in[d, rows, :].astype(f32)
        block_ref[rows, :] = x_ref[rows, :].astype(f32) + bias + total

    z_second(6)
    z_third(4)

    for d in (1, 2, 3):
        tq_in[d].wait_recv()

    @pl.loop(0, ROWS // 16)
    def _(i):
        rows = at(i * 16, 16)
        parts = [tq_recv[j, rows, :].astype(f32) for j in range(4)]
        for t in range(3):
            if t == 0:
                blocks = [keep_192(v[:, :256]) for v in parts]
            elif t == 1:
                blocks = [keep_192(pltpu.roll(v[:, 128:384], 192, 1)) for v in parts]
            else:
                blocks = [keep_192(v[:, 384:640]) for v in parts]
            chunk[9 + t, rows, :] = jnp.concatenate(
                [pair_of(blocks[0], blocks[1]), pair_of(blocks[2], blocks[3])], axis=1
            ).astype(bf16)

    for k in range(9, 12):
        z_first(k)
    z_second(7)
    z_third(5)

    for d in (1, 2, 3):
        in_in[d].wait_recv()

    @pl.loop(0, 128 // 16)
    def _(i):
        rows = at(i * 16, 16)
        my_rows = pl.ds(pl.multiple_of(me * 128 + i * 16, 16), 16)
        ng = acc_c[my_rows, :]
        for d in range(3):
            ng = ng + rs_in_in[d, rows, :].astype(f32)
        t = x_ref[rows, :].astype(f32)
        centered = t - jnp.mean(t, axis=1, keepdims=True)
        inverse = lax.rsqrt(jnp.mean(centered * centered, axis=1, keepdims=True) + eps)
        n = normed[my_rows, :]
        igrad_ref[rows, :] = ct[rows, :] + inverse * (
            ng - jnp.mean(ng, axis=1, keepdims=True) - n * jnp.mean(ng * n, axis=1, keepdims=True)
        )

    for k in range(8, 12):
        z_second(k)
        z_third(k - 2)
    for k in range(10, 12):
        z_third(k)
    for d, copy in zip((1, 2, 3), vec_zs):
        remote(("vec_z", d), vec_z.at[z], vec_z.at[(z + 4 - d) % 4], z_peer(d)).wait_recv()
    vec_ref[...] = (vec_z[0] + vec_z[1]) + (vec_z[2] + vec_z[3])
    for k in range(12):
        z_finish(k)
    for copy in pending:
        copy.wait_send()


def rope_tables(length):
    half_rot = ROT // 2
    lane = np.arange(128) % HD
    frequency = 10000.0 ** (-(lane % half_rot).astype(np.float64) * (2.0 / ROT))
    angles = np.arange(length, dtype=np.float64)[:, None] * frequency[None, :]
    turned = lane < ROT
    cos = np.where(turned, np.cos(angles), 1.0)
    lo = np.where(lane < half_rot, -np.sin(angles), 0.0)
    hi = np.where(turned & (lane >= half_rot), np.sin(angles), 0.0)
    return tuple(t.astype(np.float32) for t in (cos, lo, hi))


def local_fused(
    inputs, qkv_weight, qkv_bias, out_weight, out_bias, up_weight, up_bias, down_weight, down_bias,
    attn_gain, attn_shift, mlp_gain, mlp_shift, cotangent,
):
    f32, bf16 = jnp.float32, jnp.bfloat16
    me = lax.axis_index("grp")
    length = 512
    wide = lax.dynamic_update_slice_in_dim(jnp.zeros((3 * D,), bf16), qkv_bias, me * 576, 0)
    rest = jnp.stack([out_bias, down_bias, attn_gain, attn_shift, mlp_gain, mlp_shift])
    rest = lax.dynamic_update_slice(jnp.zeros((6, D), bf16), rest, (0, me * SHARD))
    small = jnp.concatenate([wide.reshape(3, D), rest, jnp.zeros((7, D), bf16)], axis=0)

    def vmem(shape, dtype):
        return pltpu.VMEM(shape, dtype)

    inside = pl.BlockSpec(memory_space=pltpu.VMEM)
    anywhere = pl.BlockSpec(memory_space=pl.ANY)
    big = (length, D)
    outs = pl.pallas_call(
        block_kernel,
        out_shape=(
            jax.ShapeDtypeStruct((128, D), f32),
            jax.ShapeDtypeStruct((128, D), f32),
            jax.ShapeDtypeStruct((SHARD, 3 * D), bf16),
            jax.ShapeDtypeStruct((SHARD, D), bf16),
            jax.ShapeDtypeStruct((SHARD, 4 * D), bf16),
            jax.ShapeDtypeStruct((D, D), bf16),
            jax.ShapeDtypeStruct((16, 256), f32),
        ),
        in_specs=[inside] * 6 + [anywhere] * 5,
        out_specs=(inside,) * 7,
        scratch_shapes=[
            vmem((128, D), f32), vmem((SHARD, 3 * D), bf16), vmem((D, D), bf16), vmem((SHARD, D), bf16),
            vmem((4, SHARD, 640), bf16), vmem((D, 640), bf16), vmem((D, D), bf16),
            vmem(big, bf16), vmem(big, bf16), vmem((4, 16, D), bf16), vmem(big, f32), vmem(big, bf16),
            vmem(big, bf16),
            vmem(big, f32), vmem(big, f32), vmem(big, f32), vmem((D, D), f32), vmem(big, bf16), vmem(big, bf16),
            vmem((length, 256), bf16), vmem((length, 256), bf16), vmem((length, 256), bf16),
            vmem((length, 256), bf16), vmem((length, 256), f32), vmem((length, 256), bf16),
            vmem((256, length), f32), vmem((256, length), f32), vmem((256, length), bf16),
            vmem((256, length), bf16), vmem((length, 256), f32), vmem((length, 256), f32),
            vmem((length, 256), f32), vmem((length, 640), bf16),
            vmem((384, D), f32), vmem((D, D), f32), vmem((length, 640), f32), vmem((SHARD, D), f32),
            vmem((864, D), bf16), vmem((864, D), bf16), vmem((8, ROWS, 640), bf16), vmem((8, ROWS, 640), bf16),
            vmem((4, ROWS, D), bf16), vmem((12, ROWS, D), bf16), vmem((12, ROWS, D), bf16),
            vmem((12, ROWS, D), bf16), vmem((12, ROWS, D), bf16),
            vmem(big, bf16), vmem((3, 128, D), bf16), vmem(big, bf16), vmem((3, 128, D), bf16),
            vmem((4, 8, 256), f32), vmem((3, 8, 256), f32), vmem((2, 16, 256), f32), vmem((4, 16, 256), f32),
            pltpu.SemaphoreType.DMA((NSEM,)), pltpu.SemaphoreType.DMA((NSEM,)), pltpu.SemaphoreType.DMA((5,)),
        ],
        compiler_params=pltpu.CompilerParams(
            collective_id=0, has_side_effects=True, vmem_limit_bytes=56 * 1024 * 1024
        ),
    )(
        inputs[0], small, *(jnp.asarray(t) for t in rope_tables(length)), up_bias.reshape(1, D),
        cotangent[0], qkv_weight, up_weight, down_weight, out_weight,
    )
    block_out, input_grad, gqkv, gout, gup, gdown, vec = outs
    return (
        block_out[None],
        input_grad[None],
        gqkv.astype(f32),
        vec[5:8, :SHARD].reshape(-1),
        gout.astype(f32),
        vec[0, :SHARD],
        gup.astype(f32),
        vec[8:11].reshape(-1),
        gdown.astype(f32),
        vec[0, :SHARD],
        vec[1, :SHARD],
        vec[2, :SHARD],
        vec[3, :SHARD],
        vec[4, :SHARD],
    )


def solution(mesh):
    fused = (mesh.shape["grp"], mesh.shape["rep"]) == (4, 8)
    local = local_fused if fused else local_by_tokens
    placed = (
        P("rep", "grp", None),
        P("grp", None),
        P("grp"),
        P("grp", None),
        P("grp"),
        P("grp", None),
        P("grp"),
        P("grp", None),
        P("grp"),
        P("grp"),
        P("grp"),
        P("grp"),
        P("grp"),
        P("rep", "grp", None),
    )
    return jax.shard_map(
        local,
        mesh=mesh,
        in_specs=placed,
        out_specs=(
            P("rep", "grp", None),
            P("rep", "grp", None),
            P("grp", None),
            P("grp"),
            P("grp", None),
            P("grp"),
            P("grp", None),
            P("grp"),
            P("grp", None),
            P("grp"),
            P("grp"),
            P("grp"),
            P("grp"),
            P("grp"),
        ),
        check_vma=False,
    )
```

```python
import jax
import jax.numpy as jnp
import numpy as np
from jax import lax
from jax.experimental import pallas as pl
from jax.experimental.pallas import tpu as pltpu
from jax.sharding import PartitionSpec as P

D = 768
HEADS = 12
HD = 64
ROT = 16


eps = 1e-05


def layer_norm(values):
    centered = values - jnp.mean(values, axis=-1, keepdims=True)
    variance = jnp.mean(centered * centered, axis=-1, keepdims=True)
    inverse = lax.rsqrt(variance + eps)
    return (centered * inverse, inverse)


def gelu_parts(preact):
    normal_cdf = 0.5 * (1.0 + jax.scipy.special.erf(preact * 0.7071067811865476))
    density = jnp.exp(-0.5 * preact * preact) * 0.3989422804014327
    return (preact * normal_cdf, normal_cdf + preact * density)


def angle_tables(positions):
    half_rot = ROT // 2
    frequency = 10000.0 ** (-jnp.arange(half_rot, dtype=jnp.float32) * (2.0 / ROT))
    angles = positions.astype(jnp.float32)[:, None] * frequency[None, :]
    return (jnp.cos(angles)[:, None, :], jnp.sin(angles)[:, None, :])


def rotate(tensor, cos_table, sin_table):
    half_rot = ROT // 2
    lower_part = tensor[..., :half_rot]
    upper_part = tensor[..., half_rot:ROT]
    return jnp.concatenate(
        [
            lower_part * cos_table - upper_part * sin_table,
            upper_part * cos_table + lower_part * sin_table,
            tensor[..., ROT:],
        ],
        axis=-1,
    )


def unrotate(tensor, cos_table, sin_table):
    half_rot = ROT // 2
    lower_part = tensor[..., :half_rot]
    upper_part = tensor[..., half_rot:ROT]
    return jnp.concatenate(
        [
            lower_part * cos_table + upper_part * sin_table,
            upper_part * cos_table - lower_part * sin_table,
            tensor[..., ROT:],
        ],
        axis=-1,
    )


def local_by_tokens(
    inputs,
    qkv_weight,
    qkv_bias,
    out_weight,
    out_bias,
    up_weight,
    up_bias,
    down_weight,
    down_bias,
    attn_gain,
    attn_shift,
    mlp_gain,
    mlp_shift,
    cotangent,
):
    tokens = inputs.shape[1]
    (
        full_qkv,
        full_qkv_bias,
        full_out,
        full_out_bias,
        full_up,
        full_up_bias,
        full_down,
        full_down_bias,
        gain_attn,
        shift_attn,
        gain_mlp,
        shift_mlp,
    ) = (
        lax.all_gather(qkv_weight, "grp", axis=0, tiled=True),
        lax.all_gather(qkv_bias, "grp", axis=0, tiled=True),
        lax.all_gather(out_weight, "grp", axis=0, tiled=True),
        lax.all_gather(out_bias, "grp", axis=0, tiled=True),
        lax.all_gather(up_weight, "grp", axis=0, tiled=True),
        lax.all_gather(up_bias, "grp", axis=0, tiled=True),
        lax.all_gather(down_weight, "grp", axis=0, tiled=True),
        lax.all_gather(down_bias, "grp", axis=0, tiled=True),
        lax.all_gather(attn_gain, "grp", axis=0, tiled=True),
        lax.all_gather(attn_shift, "grp", axis=0, tiled=True),
        lax.all_gather(mlp_gain, "grp", axis=0, tiled=True),
        lax.all_gather(mlp_shift, "grp", axis=0, tiled=True),
    )
    first_row = lax.axis_index("grp") * tokens
    positions = first_row + jnp.arange(tokens, dtype=jnp.int32)
    cos_table, sin_table = angle_tables(positions)
    score_scale = HD ** (-0.5)
    hidden_in = inputs[0].astype(jnp.float32)
    normed, inverse = layer_norm(hidden_in)
    attn_in = (normed * gain_attn.astype(jnp.float32) + shift_attn.astype(jnp.float32)).astype(
        jnp.bfloat16
    )
    mlp_in = (normed * gain_mlp.astype(jnp.float32) + shift_mlp.astype(jnp.float32)).astype(
        jnp.bfloat16
    )
    qkv = jnp.dot(attn_in, full_qkv, preferred_element_type=jnp.float32) + full_qkv_bias.astype(
        jnp.float32
    )
    query_b = rotate(qkv[:, :D].reshape(tokens, HEADS, HD), cos_table, sin_table).astype(
        jnp.bfloat16
    )
    keys_local = (
        rotate(qkv[:, D : 2 * D].reshape(tokens, HEADS, HD), cos_table, sin_table)
        .astype(jnp.bfloat16)
        .reshape(tokens, D)
    )
    values_local = qkv[:, 2 * D :].astype(jnp.bfloat16)
    keys_all, values_all = (
        lax.all_gather(keys_local, "grp", axis=0, tiled=True),
        lax.all_gather(values_local, "grp", axis=0, tiled=True),
    )
    length = keys_all.shape[0]
    visible = jnp.arange(length, dtype=jnp.int32)[None, :] <= positions[:, None]
    query_heads = jnp.transpose(query_b, (1, 0, 2))
    key_heads = jnp.transpose(keys_all.reshape(length, HEADS, HD), (1, 0, 2))
    value_heads = jnp.transpose(values_all.reshape(length, HEADS, HD), (1, 0, 2))

    def forward_head(operands):
        query_one, key_one, value_one = operands
        scores = jnp.dot(query_one, key_one.T, preferred_element_type=jnp.float32) * score_scale
        scores = jnp.where(visible, scores, -jnp.inf)
        row_max = jnp.max(scores, axis=-1, keepdims=True)
        log_total = row_max + jnp.log(jnp.sum(jnp.exp(scores - row_max), axis=-1, keepdims=True))
        probs_b = jnp.exp(scores - log_total).astype(jnp.bfloat16)
        context_one = jnp.dot(probs_b, value_one, preferred_element_type=jnp.float32).astype(
            jnp.bfloat16
        )
        return (context_one, log_total)

    context_heads, log_totals = lax.map(forward_head, (query_heads, key_heads, value_heads))
    context = jnp.transpose(context_heads, (1, 0, 2)).reshape(tokens, D)
    attn_out = jnp.dot(
        context, full_out, preferred_element_type=jnp.float32
    ) + full_out_bias.astype(jnp.float32)
    preact = jnp.dot(mlp_in, full_up, preferred_element_type=jnp.float32) + full_up_bias.astype(
        jnp.float32
    )
    activation, slope = gelu_parts(preact)
    act_b = activation.astype(jnp.bfloat16)
    mlp_out = jnp.dot(act_b, full_down, preferred_element_type=jnp.float32) + full_down_bias.astype(
        jnp.float32
    )
    block_out = hidden_in + attn_out + mlp_out
    back_qkv, back_out, back_up, back_down, back_gain_attn, back_gain_mlp = (
        lax.all_gather(qkv_weight, "grp", axis=0, tiled=True),
        lax.all_gather(out_weight, "grp", axis=0, tiled=True),
        lax.all_gather(up_weight, "grp", axis=0, tiled=True),
        lax.all_gather(down_weight, "grp", axis=0, tiled=True),
        lax.all_gather(attn_gain, "grp", axis=0, tiled=True),
        lax.all_gather(mlp_gain, "grp", axis=0, tiled=True),
    )
    grad_out = cotangent[0]
    grad_b = grad_out.astype(jnp.bfloat16)
    down_grad = jnp.dot(act_b.T, grad_b, preferred_element_type=jnp.float32)
    out_grad = jnp.dot(context.T, grad_b, preferred_element_type=jnp.float32)
    bias_sum = jnp.sum(grad_out, axis=0)
    preact_grad = jnp.dot(grad_b, back_down.T, preferred_element_type=jnp.float32) * slope
    up_bias_grad = jnp.sum(preact_grad, axis=0)
    preact_b = preact_grad.astype(jnp.bfloat16)
    up_grad = jnp.dot(mlp_in.T, preact_b, preferred_element_type=jnp.float32)
    mlp_in_grad = jnp.dot(preact_b, back_up.T, preferred_element_type=jnp.float32)
    context_grad = jnp.dot(grad_b, back_out.T, preferred_element_type=jnp.float32).astype(
        jnp.bfloat16
    )
    context_grad_heads = jnp.transpose(context_grad.reshape(tokens, HEADS, HD), (1, 0, 2))

    def backward_head(operands):
        query_one, key_one, value_one, grad_one, log_total = operands
        scores = jnp.dot(query_one, key_one.T, preferred_element_type=jnp.float32) * score_scale
        scores = jnp.where(visible, scores, -jnp.inf)
        attn_probs = jnp.exp(scores - log_total)
        probs_b = attn_probs.astype(jnp.bfloat16)
        prob_grad = jnp.dot(grad_one, value_one.T, preferred_element_type=jnp.float32)
        row_dot = jnp.sum(attn_probs * prob_grad, axis=-1, keepdims=True)
        score_grad = (attn_probs * (prob_grad - row_dot) * score_scale).astype(jnp.bfloat16)
        query_grad = jnp.dot(score_grad, key_one, preferred_element_type=jnp.float32)
        key_grad = jnp.dot(score_grad.T, query_one, preferred_element_type=jnp.float32)
        value_grad = jnp.dot(probs_b.T, grad_one, preferred_element_type=jnp.float32)
        return (query_grad, key_grad, value_grad)

    query_grads, key_grads, value_grads = lax.map(
        backward_head, (query_heads, key_heads, value_heads, context_grad_heads, log_totals)
    )
    key_full = jnp.transpose(key_grads, (1, 0, 2)).reshape(length, D)
    value_full = jnp.transpose(value_grads, (1, 0, 2)).reshape(length, D)
    key_mine, value_mine = (
        lax.psum_scatter(key_full, "grp", scatter_dimension=0, tiled=True),
        lax.psum_scatter(value_full, "grp", scatter_dimension=0, tiled=True),
    )
    query_rows = unrotate(jnp.transpose(query_grads, (1, 0, 2)), cos_table, sin_table).reshape(
        tokens, D
    )
    key_rows = unrotate(key_mine.reshape(tokens, HEADS, HD), cos_table, sin_table).reshape(
        tokens, D
    )
    qkv_rows = jnp.concatenate([query_rows, key_rows, value_mine], axis=1)
    qkv_bias_grad = jnp.sum(qkv_rows, axis=0)
    qkv_rows_b = qkv_rows.astype(jnp.bfloat16)
    qkv_grad = jnp.dot(attn_in.T, qkv_rows_b, preferred_element_type=jnp.float32)
    attn_in_grad = jnp.dot(qkv_rows_b, back_qkv.T, preferred_element_type=jnp.float32)
    attn_gain_grad = jnp.sum(attn_in_grad * normed, axis=0)
    attn_shift_grad = jnp.sum(attn_in_grad, axis=0)
    mlp_gain_grad = jnp.sum(mlp_in_grad * normed, axis=0)
    mlp_shift_grad = jnp.sum(mlp_in_grad, axis=0)
    normed_grad = attn_in_grad * back_gain_attn.astype(
        jnp.float32
    ) + mlp_in_grad * back_gain_mlp.astype(jnp.float32)
    input_grad = grad_out + inverse * (
        normed_grad
        - jnp.mean(normed_grad, axis=-1, keepdims=True)
        - normed * jnp.mean(normed_grad * normed, axis=-1, keepdims=True)
    )
    group_parts = (
        lax.psum_scatter(qkv_grad, "grp", scatter_dimension=0, tiled=True),
        lax.psum_scatter(qkv_bias_grad, "grp", scatter_dimension=0, tiled=True),
        lax.psum_scatter(out_grad, "grp", scatter_dimension=0, tiled=True),
        lax.psum_scatter(bias_sum, "grp", scatter_dimension=0, tiled=True),
        lax.psum_scatter(up_grad, "grp", scatter_dimension=0, tiled=True),
        lax.psum_scatter(up_bias_grad, "grp", scatter_dimension=0, tiled=True),
        lax.psum_scatter(down_grad, "grp", scatter_dimension=0, tiled=True),
        lax.psum_scatter(attn_gain_grad, "grp", scatter_dimension=0, tiled=True),
        lax.psum_scatter(attn_shift_grad, "grp", scatter_dimension=0, tiled=True),
        lax.psum_scatter(mlp_gain_grad, "grp", scatter_dimension=0, tiled=True),
        lax.psum_scatter(mlp_shift_grad, "grp", scatter_dimension=0, tiled=True),
    )
    (
        qkv_part,
        qkv_bias_part,
        out_part,
        bias_part,
        up_part,
        up_bias_part,
        down_part,
        gain_attn_part,
        shift_attn_part,
        gain_mlp_part,
        shift_mlp_part,
    ) = group_parts
    (
        qkv_total,
        qkv_bias_total,
        out_total,
        bias_total,
        up_total,
        up_bias_total,
        down_total,
        gain_attn_total,
        shift_attn_total,
        gain_mlp_total,
        shift_mlp_total,
    ) = lax.psum(
        (
            qkv_part,
            qkv_bias_part,
            out_part,
            bias_part,
            up_part,
            up_bias_part,
            down_part,
            gain_attn_part,
            shift_attn_part,
            gain_mlp_part,
            shift_mlp_part,
        ),
        "rep",
    )
    return (
        block_out[None],
        input_grad[None],
        qkv_total,
        qkv_bias_total,
        out_total,
        bias_total,
        up_total,
        up_bias_total,
        down_total,
        bias_total,
        gain_attn_total,
        shift_attn_total,
        gain_mlp_total,
        shift_mlp_total,
    )


ROWS = 96
SHARD = 192
MESH = pl.DeviceIdType.MESH
NSEM = 128
UP, RL, UL, UM, RR, UR, RA, UA, US, UU, UN, UB, UC = 2, 16, 4, 1, 16, 4, 16, 4, 1, 4, 1, 4, 2


def mm(a, b):
    return lax.dot_general(a, b, (((1,), (0,)), ((), ())), preferred_element_type=jnp.float32)


def mm_tn(a, b):
    return lax.dot_general(a, b, (((0,), (0,)), ((), ())), preferred_element_type=jnp.float32)


def mm_nt(a, b):
    return lax.dot_general(a, b, (((1,), (1,)), ((), ())), preferred_element_type=jnp.float32)


def keep_192(t):
    lane = lax.broadcasted_iota(jnp.int32, t.shape, 1)
    return jnp.where(lane < SHARD, t, 0.0)


def block_of(t, j):
    base = (j // 2) * 384
    if j % 2 == 0:
        return keep_192(t[:, base : base + 256])
    return keep_192(pltpu.roll(t[:, base + 128 : base + 384], 192, 1))


def pair_of(a, b):
    shifted = pltpu.roll(b, 64, 1)
    return jnp.concatenate([a[:, :128], shifted[:, :128] + a[:, 128:], shifted[:, 128:]], axis=1)


def gelu_with_slope(preact):
    normal_cdf = 0.5 * (1.0 + lax.erf(preact * 0.7071067811865476))
    density = jnp.exp(-0.5 * preact * preact) * 0.3989422804014327
    return preact * normal_cdf, normal_cdf + preact * density


def block_kernel(
    x_ref, small_ref, cos_ref, sin_lo_ref, sin_hi_ref,
    ct_hbm, wqkv_hbm, wup_hbm, wdown_hbm, wout_hbm,
    block_ref, igrad_ref, qkv_hbm, out_hbm, up_hbm, down_hbm, vec_ref,
    gqkv_ref, gout_ref, gup_ref, gdown_ref,
    ct, w_qkv_in, w_down, w_out, w_pack, w_qkv, w_up,
    x_all, g_all, small_all, up_way, qkv_way, normed, attn_in, mlp_in,
    acc_a, acc_b, acc_c, acc_d, act_b, preact_b,
    q_b, k_b, v_b, cg_b, ctx_f, ctx_b, s_buf, dp_buf, p_b, ds_b, dq_f, dk_f, dv_f, rows_b,
    down_own, up_full, qkv_full, out_full,
    part_send, part_recv, tq_send, tq_recv, tu_send, chunk, z_in, z_sum, z_other,
    rs_out, rs_out_in, rs_in, rs_in_in,
    vec_send, vec_recv, vec_core, vec_z,
    send_sem, recv_sem, local_sem,
):
    f32, bf16 = jnp.float32, jnp.bfloat16
    me = lax.axis_index("grp")
    rep = lax.axis_index("rep")
    z, core = rep // 2, rep % 2
    mx, my = me % 2, me // 2
    inner = (z == 1) | (z == 2)
    outer = (z == 0) | (z == 3)
    peers = {1: my * 2 + (1 - mx), 2: (1 - my) * 2 + mx, 3: (1 - my) * 2 + (1 - mx)}
    twin = (me, z * 2 + (1 - core))
    z_pair = (me, (z + 1 - 2 * (z % 2)) * 2 + core)
    z_mid = (me, (3 - z) * 2 + core)

    def group(d):
        return (peers[d], rep)

    names = {}

    def over(count, step, unroll):
        def run(body):
            @pl.loop(0, count // step, unroll=unroll)
            def _(i):
                body(pl.multiple_of(i * step, step))

        return run

    def remote(name, src, dst, device):
        i = names.setdefault(name, len(names))
        assert i < NSEM
        return pltpu.make_async_remote_copy(
            src_ref=src, dst_ref=dst, send_sem=send_sem.at[i], recv_sem=recv_sem.at[i],
            device_id=device, device_id_type=MESH,
        )

    pending = []

    def send(name, src, dst, device):
        copy = remote(name, src, dst, device)
        copy.start()
        pending.append(copy)
        return copy

    def at(start, size, multiple=None):
        return pl.ds(pl.multiple_of(start, multiple or size), size)

    barrier = pltpu.get_barrier_semaphore()
    everyone = [group(d) for d in (1, 2, 3)] + [twin, z_pair]
    for device in everyone:
        pl.semaphore_signal(barrier, inc=1, device_id=device, device_id_type=MESH)

    @pl.when(inner)
    def _():
        pl.semaphore_signal(barrier, inc=1, device_id=z_mid, device_id_type=MESH)

    locals_ = [
        pltpu.make_async_copy(ct_hbm, ct, local_sem.at[0]),
        pltpu.make_async_copy(wqkv_hbm, w_qkv_in, local_sem.at[1]),
        pltpu.make_async_copy(wdown_hbm, w_down, local_sem.at[2]),
        pltpu.make_async_copy(wout_hbm, w_out, local_sem.at[3]),
        pltpu.make_async_copy(
            wup_hbm.at[:, at(me * D, D, 128)], w_up.at[at(me * SHARD, SHARD)], local_sem.at[4]
        ),
    ]
    for copy in locals_:
        copy.start()

    small_all[me] = jnp.zeros((16, 256), f32)
    small_all[me, 0:13, 0:SHARD] = small_ref[...].astype(f32)
    mine = at(me * 128, 128)
    x_all[mine, :] = x_ref[...]
    bias_up = jnp.concatenate(
        [pair_of(small_all[me, r : r + 1], small_all[me, r + 1 : r + 2]) for r in (9, 11)], axis=1
    )
    pl.semaphore_wait(barrier, len(everyone) + inner.astype(jnp.int32))

    half = at(me * SHARD + core * ROWS, ROWS)
    small_in = {d: send(("small", d), small_all.at[me], small_all.at[me], group(d)) for d in (3, 1, 2)}

    def spread_rows(name, buffer):
        copies = {}
        for h in (0, 1):
            for d in (1, 2):
                part = h if d == 1 else 1 - h
                rows = at(me * 128 + part * 64, 64)
                copies[d, part] = send((name, d, part), buffer.at[rows], buffer.at[rows], group(d))
        return copies

    def forward_rows(name, buffer, copies):
        onward = []
        for d in (1, 2):
            part = d - 1
            copies[d, part].wait_recv()
            rows = at(peers[d] * 128 + part * 64, 64)
            onward.append(send((name, "on", part), buffer.at[rows], buffer.at[rows], group(3 - d)))
        return onward

    def spread_columns(name, source, way, buffer):
        copies = {}
        for d in (1, 2):
            part = d - 1
            copies["way", part] = send(
                (name, "way", part), source(3, core * ROWS + part * 48, 48), way.at[part], group(d)
            )
        for d in (1, 2):
            copies[d] = send((name, d), source(d, core * ROWS, ROWS), buffer.at[half], group(d))
        return copies

    def forward_columns(name, way, buffer, copies):
        onward = []
        for d in (1, 2):
            part = d - 1
            copies["way", part].wait_recv()
            rows = at(peers[d] * SHARD + core * ROWS + part * 48, 48)
            onward.append(send((name, "on", part), way.at[part], buffer.at[rows], group(3 - d)))
        return onward

    def share_weight(name, buffer, copies, onward):
        twins = []
        for d in (1, 2, 3):
            if d == 3:
                for copy in onward:
                    copy.wait_recv()
            else:
                copies[d].wait_recv()
            rows = at(peers[d] * SHARD + core * ROWS, ROWS)
            twins.append(send((name, "twin", d), buffer.at[rows], buffer.at[rows], twin))
        return twins

    def up_source(d, start, size):
        return wup_hbm.at[at(start, size, 16), at(peers[d] * D, D, 128)]

    def qkv_source(d, start, size):
        return w_pack.at[peers[d], at(start, size, 16)]

    x_in = spread_rows("x", x_all)
    up_in = spread_columns("up", up_source, up_way, w_up)
    locals_[0].wait()
    g_all[mine, :] = ct[...].astype(bf16)

    for d in (1, 2, 3):
        small_in[d].wait_recv()

    def vector(r):
        rows = [small_all[i, r : r + 1] for i in range(4)]
        return jnp.concatenate([pair_of(rows[0], rows[1]), pair_of(rows[2], rows[3])], axis=1)

    gain_attn, shift_attn, gain_mlp, shift_mlp = vector(5), vector(6), vector(7), vector(8)
    bias = vector(3) + vector(4)
    bias_qkv = jnp.zeros((1, 640), f32)
    for j in range(4):
        a, b, c = (
            small_all[(4 * t + j) // 3, (4 * t + j) % 3 : (4 * t + j) % 3 + 1] for t in range(3)
        )
        bias_qkv = jnp.where(me == j, jnp.concatenate([pair_of(a, b), c], axis=1), bias_qkv)

    def norm_rows(start):
        @over(128, RL, UL)
        def _(i):
            rows = pl.ds(pl.multiple_of(start + i, RL), RL)
            t = x_all[rows, :].astype(f32)
            centered = t - jnp.mean(t, axis=1, keepdims=True)
            inverse = lax.rsqrt(jnp.mean(centered * centered, axis=1, keepdims=True) + eps)
            n = centered * inverse
            normed[rows, :] = n
            attn_in[rows, :] = (n * gain_attn + shift_attn).astype(bf16)
            mlp_in[rows, :] = (n * gain_mlp + shift_mlp).astype(bf16)

    norm_rows(me * 128)
    x_on = forward_rows("x", x_all, x_in)
    g_in = spread_rows("g", g_all)
    for d in (1, 2):
        x_in[d, 2 - d].wait_recv()
        norm_rows(peers[d] * 128)
    up_on = forward_columns("up", up_way, w_up, up_in)
    locals_[1].wait()

    @over(SHARD, 32, UP)
    def _(start):
        rows = pl.ds(start, 32)
        wide = w_qkv_in[rows, :].astype(f32)
        for j in range(4):
            a, b, c = (block_of(wide[:, t * D : (t + 1) * D], j) for t in range(3))
            w_pack[j, rows, :] = jnp.concatenate([pair_of(a, b), c], axis=1).astype(bf16)

    w_qkv[at(me * SHARD, SHARD), :] = w_pack[me]
    for copy in x_on:
        copy.wait_recv()
    norm_rows(peers[3] * 128)

    up_twins = share_weight("up", w_up, up_in, up_on)
    g_on = forward_rows("g", g_all, g_in)
    qkv_in = spread_columns("qkv", qkv_source, qkv_way, w_qkv)
    locals_[4].wait()
    for copy in up_twins:
        copy.wait_recv()

    acc_a[...] = mm(mlp_in[...], w_up[...])

    @over(512, 16, UM)
    def _(start):
        rows = pl.ds(start, 16)
        activation, slope = gelu_with_slope(acc_a[rows, :] + bias_up)
        act_b[rows, :] = activation.astype(bf16)
        acc_a[rows, :] = slope

    locals_[2].wait()
    locals_[3].wait()
    acc_b[...] = mm(act_b[...], w_down[...])

    for d in (1, 2):
        g_in[d, 2 - d].wait_recv()
    for copy in g_on:
        copy.wait_recv()
    g = g_all[...]
    other_cols = at((1 - core) * 384, 384)
    own_cols = at(core * 384, 384)

    part_send[0:384, :] = mm_tn(act_b[:, other_cols], g).astype(bf16)
    down_part = send("part_down", part_send.at[0:384], part_recv.at[0:384], twin)
    down_own[...] = mm_tn(act_b[:, own_cols], g)
    acc_c[...] = mm_nt(g, w_down[...])

    def slope_rows(i, total):
        rows = at(i * 16, 16)
        pg = acc_c[rows, :] * acc_a[rows, :]
        preact_b[rows, :] = pg.astype(bf16)
        return total + pg[:8] + pg[8:]

    up_bias_part = lax.fori_loop(0, 512 // 16, slope_rows, jnp.zeros((8, D), f32), unroll=US)
    up_bias_part = jnp.sum(up_bias_part, axis=0, keepdims=True)

    up_full[...] = mm_tn(mlp_in[...], preact_b[...])
    for j in range(4):
        part_send[384 + j * ROWS : 384 + (j + 1) * ROWS, :] = up_full[
            at(j * SHARD + (1 - core) * ROWS, ROWS), :
        ].astype(bf16)
    up_part = send("part_up", part_send.at[384:768], part_recv.at[384:768], twin)

    def total_of(refs, k, which):
        gqkv, gout, gup, gdown = refs
        if k < 4:
            return gdown.at[at(which * 384 + k * ROWS, ROWS)]
        if k < 8:
            return gup.at[at(which * ROWS, ROWS), (k - 4) * D : (k - 3) * D]
        if k == 8:
            return gout.at[at(which * ROWS, ROWS)]
        return gqkv.at[at(which * ROWS, ROWS), (k - 9) * D : (k - 8) * D]

    def total_ref(k, which):
        return total_of((gqkv_ref, gout_ref, gup_ref, gdown_ref), k, which)

    def store_total(k, which, i):
        return pltpu.make_async_copy(
            total_ref(k, which), total_of((qkv_hbm, out_hbm, up_hbm, down_hbm), k, which), local_sem.at[5 + 2 * k + i]
        )

    def z_first(k):
        @pl.when(outer)
        def _():
            remote(("z1", k), chunk.at[k], z_in.at[k], z_pair).start()

    def z_second(k):
        @pl.when(inner)
        def _():
            remote(("z1", k), chunk.at[k], z_in.at[k], z_pair).wait_recv()
            z_sum[k] = (chunk[k].astype(f32) + z_in[k].astype(f32)).astype(bf16)
            remote(("z2", k), z_sum.at[k], z_other.at[k], z_mid).start()

    def z_third(k):
        own = total_ref(k, core)

        @pl.when(inner)
        def _():
            remote(("z2", k), z_sum.at[k], z_other.at[k], z_mid).wait_recv()
            own[...] = (z_sum[k].astype(f32) + z_other[k].astype(f32)).astype(bf16)
            remote(("z3", k), own, own, z_pair).start()

        @pl.when(outer)
        def _():
            remote(("z3", k), own, own, z_pair).wait_recv()

        remote(("last", k), own, own, twin).start()
        store_total(k, core, 0).start()

    def z_fourth(k):
        remote(("last", k), total_ref(k, 1 - core), total_ref(k, 1 - core), twin).wait_recv()
        store_total(k, 1 - core, 1).start()

    def z_finish(k):
        own = total_ref(k, core)
        last = remote(("last", k), own, own, twin)
        last.wait_send()
        store_total(k, core, 0).wait()
        store_total(k, 1 - core, 1).wait()

        @pl.when(inner)
        def _():
            remote(("z2", k), z_sum.at[k], z_other.at[k], z_mid).wait_send()
            remote(("z3", k), own, own, z_pair).wait_send()

        @pl.when(outer)
        def _():
            remote(("z1", k), chunk.at[k], z_in.at[k], z_pair).wait_send()

    down_part.wait_recv()
    for k in range(4):
        rows = pl.ds(k * ROWS, ROWS)
        chunk[k] = (down_own[rows, :] + part_recv[rows, :].astype(f32)).astype(bf16)
        z_first(k)

    acc_c[...] = mm_nt(preact_b[...], w_up[...])
    cg_b[...] = jnp.zeros_like(cg_b)
    cg_b[:, :SHARD] = mm_nt(g, w_out[...]).astype(bf16)

    up_part.wait_recv()
    for j in range(4):
        tu_send[j] = (
            up_full[at(j * SHARD + core * ROWS, ROWS), :]
            + part_recv[384 + j * ROWS : 384 + (j + 1) * ROWS, :].astype(f32)
        ).astype(bf16)
    chunk[4 + me] = tu_send[me]
    tu_in = {d: send(("tu", d), tu_send.at[peers[d]], chunk.at[4 + me], group(d)) for d in (3, 1, 2)}

    qkv_on = forward_columns("qkv", qkv_way, w_qkv, qkv_in)
    qkv_twins = share_weight("qkv", w_qkv, qkv_in, qkv_on)
    for copy in qkv_twins:
        copy.wait_recv()
    qkv_full[...] = mm(attn_in[...], w_qkv[...])
    z_second(0)

    def turn(t, cos, lo, hi):
        return t * cos + pltpu.roll(t, 376, 1) * lo + pltpu.roll(t, 8, 1) * hi

    def tables(rows):
        return tuple(
            jnp.concatenate([ref[rows, :]] * 3, axis=1) for ref in (cos_ref, sin_lo_ref, sin_hi_ref)
        )

    @over(512, RR, UR)
    def _(start):
        rows = pl.ds(start, RR)
        t = qkv_full[rows, :] + bias_qkv
        cos, lo, hi = tables(rows)
        qk = turn(t[:, :384], cos, lo, hi)
        q_b[rows, :] = (keep_192(qk[:, :256]) * 0.125).astype(bf16)
        k_b[rows, :] = keep_192(pltpu.roll(qk[:, 128:384], 192, 1)).astype(bf16)
        v_b[rows, :] = keep_192(t[:, 384:640]).astype(bf16)

    ctx_f[...] = jnp.zeros_like(ctx_f)
    dq_f[...] = jnp.zeros_like(dq_f)
    dk_f[...] = jnp.zeros_like(dk_f)
    dv_f[...] = jnp.zeros_like(dv_f)
    lane256 = lax.broadcasted_iota(jnp.int32, (1, 256), 1)
    for h in range(3):
        mask = ((lane256 >= h * 64) & (lane256 < (h + 1) * 64)).astype(bf16)
        for block in range(2):
            keys = (block + 1) * 256
            rows_q = slice(block * 256, (block + 1) * 256)
            q_h = q_b[rows_q, :] * mask
            cg_h = cg_b[rows_q, :] * mask
            s_buf[:, :keys] = mm_nt(q_h, k_b[:keys, :])
            dp_buf[:, :keys] = mm_nt(cg_h, v_b[:keys, :])

            @over(256, RA, UA)
            def _(start, keys=keys, block=block):
                rows = pl.ds(start, RA)
                s = s_buf[rows, :keys]
                key_at = lax.broadcasted_iota(jnp.int32, (RA, keys), 1)
                query_at = lax.broadcasted_iota(jnp.int32, (RA, keys), 0) + (block * 256 + start)
                s = jnp.where(key_at <= query_at, s, -jnp.inf)
                e = jnp.exp(s - jnp.max(s, axis=1, keepdims=True))
                dp = dp_buf[rows, :keys]
                share = 1.0 / jnp.sum(e, axis=1, keepdims=True)
                row_dot = jnp.sum(e * dp, axis=1, keepdims=True) * share
                p = e * share
                p_b[rows, :keys] = p.astype(bf16)
                ds_b[rows, :keys] = (p * (dp - row_dot)).astype(bf16)

            ctx_f[rows_q, :] += mm(p_b[:, :keys], v_b[:keys, :] * mask)
            dq_f[rows_q, :] += mm(ds_b[:, :keys], k_b[:keys, :] * mask)
            dk_f[:keys, :] += mm_tn(ds_b[:, :keys], q_h)
            dv_f[:keys, :] += mm_tn(p_b[:, :keys], cg_h)
            if (h, block) == (0, 1):
                z_second(1)
                z_third(0)
            elif (h, block) == (1, 0):
                for d in (1, 2, 3):
                    tu_in[d].wait_recv()
                for k in range(4, 8):
                    z_first(k)
                z_second(2)
            elif (h, block) == (1, 1):
                z_third(1)
            elif (h, block) == (2, 0):
                z_second(3)

    ctx_b[...] = ctx_f[...].astype(bf16)

    acc_b[...] += mm(ctx_b[:, :SHARD], w_out[...])
    rs_out[...] = acc_b[...].astype(bf16)
    out_in = {
        d: send(("rs_out", d), rs_out.at[at(peers[d] * 128, 128)], rs_out_in.at[d - 1], group(d))
        for d in (3, 1, 2)
    }

    z_third(2)
    out_full[...] = mm_tn(ctx_b[:, :SHARD], g)
    part_send[768 : 768 + ROWS, :] = out_full[at((1 - core) * ROWS, ROWS), :].astype(bf16)
    out_part = send("part_out", part_send.at[768:864], part_recv.at[768:864], twin)

    z_second(4)

    def unturn_rows(i, totals):
        rows = at(i * 16, 16)
        cos, lo, hi = tables(rows)
        qk = pair_of(dq_f[rows, :] * 0.125, dk_f[rows, :])
        qk = turn(qk, cos, -lo, -hi)
        full = jnp.concatenate([qk, dv_f[rows, :]], axis=1)
        rows_b[rows, :] = full.astype(bf16)
        return totals + full[:8] + full[8:]

    qkv_bias_part = lax.fori_loop(0, 512 // 16, unturn_rows, jnp.zeros((8, 640), f32), unroll=UU)
    qkv_bias_part = jnp.sum(qkv_bias_part, axis=0, keepdims=True)

    acc_d[:, :640] = mm_tn(attn_in[...], rows_b[...])
    for j in range(4):
        tq_send[4 + j] = acc_d[at(j * SHARD + (1 - core) * ROWS, ROWS), :640].astype(bf16)
    qkv_part = send("part_qkv", tq_send.at[4:8], tq_recv.at[4:8], twin)
    out_part.wait_recv()
    chunk[8] = (out_full[at(core * ROWS, ROWS), :] + part_recv[768:864, :].astype(f32)).astype(bf16)
    z_first(8)
    qkv_part.wait_recv()
    for j in range(4):
        tq_send[j] = (
            acc_d[at(j * SHARD + core * ROWS, ROWS), :640] + tq_recv[4 + j].astype(f32)
        ).astype(bf16)
    tq_recv[me] = tq_send[me]
    tq_in = {d: send(("tq", d), tq_send.at[peers[d]], tq_recv.at[me], group(d)) for d in (3, 1, 2)}

    z_third(3)
    z_second(5)
    acc_b_in = mm_nt(rows_b[...], w_qkv[...])
    acc_d[0:512, :] = acc_b_in

    def norm_grad_rows(i, totals):
        rows = at(i * 16, 16)
        ag, mg, n = acc_d[rows, :], acc_c[rows, :], normed[rows, :]
        both = ag * gain_attn + mg * gain_mlp
        acc_c[rows, :] = both
        rs_in[rows, :] = both.astype(bf16)
        new = (ag * n, ag, mg * n, mg)
        return tuple(t + v[:8] + v[8:] for t, v in zip(totals, new))

    sums = lax.fori_loop(0, 512 // 16, norm_grad_rows, (jnp.zeros((8, D), f32),) * 4, unroll=UN)
    z_third(4)
    z_second(6)

    def rows_sum(t):
        return jnp.sum(t, axis=0, keepdims=True)

    wide = jnp.concatenate(
        [rows_sum(ct[...])] + [rows_sum(t) for t in sums] + [jnp.zeros((3, D), f32)], axis=0
    )
    types = [
        keep_192(qkv_bias_part[:, :256]),
        keep_192(pltpu.roll(qkv_bias_part[:, 128:384], 192, 1)),
        keep_192(qkv_bias_part[:, 384:640]),
    ]
    for j in range(4):
        vec_send[j] = block_of(wide, j)
        for t in range(3):
            b = 3 * j + t
            vec_send[j, 5 + t : 6 + t, :] = jnp.where(me == b % 4, types[b // 4], 0.0)
    vec_in = {d: send(("vec", d), vec_send.at[peers[d]], vec_recv.at[d - 1], group(d)) for d in (3, 1, 2)}
    z_third(5)
    z_second(7)

    for d in (1, 2, 3):
        tq_in[d].wait_recv()

    @over(ROWS, 16, UC)
    def _(start):
        rows = pl.ds(start, 16)
        parts = [tq_recv[j, rows, :].astype(f32) for j in range(4)]
        for t in range(3):
            if t == 0:
                blocks = [keep_192(v[:, :256]) for v in parts]
            elif t == 1:
                blocks = [keep_192(pltpu.roll(v[:, 128:384], 192, 1)) for v in parts]
            else:
                blocks = [keep_192(v[:, 384:640]) for v in parts]
            chunk[9 + t, rows, :] = jnp.concatenate(
                [pair_of(blocks[0], blocks[1]), pair_of(blocks[2], blocks[3])], axis=1
            ).astype(bf16)

    for k in range(9, 12):
        z_first(k)
    in_in = {
        d: send(("rs_in", d), rs_in.at[at(peers[d] * 128, 128)], rs_in_in.at[d - 1], group(d))
        for d in (3, 1, 2)
    }
    z_third(6)
    z_second(8)
    z_third(7)
    for n in range(5):
        z_fourth(n)


    for d in (1, 2, 3):
        out_in[d].wait_recv()

    @over(128, 16, UB)
    def _(start):
        rows = pl.ds(start, 16)
        total = acc_b[pl.ds(pl.multiple_of(me * 128 + start, 16), 16), :]
        for d in range(3):
            total = total + rs_out_in[d, rows, :].astype(f32)
        block_ref[rows, :] = x_ref[rows, :].astype(f32) + bias + total


    z_second(9)
    z_third(8)
    for n in range(5, 8):
        z_fourth(n)
    z_second(10)

    for d in (1, 2, 3):
        in_in[d].wait_recv()

    @over(128, 16, UB)
    def _(start):
        rows = pl.ds(start, 16)
        my_rows = pl.ds(pl.multiple_of(me * 128 + start, 16), 16)
        ng = acc_c[my_rows, :]
        for d in range(3):
            ng = ng + rs_in_in[d, rows, :].astype(f32)
        t = x_ref[rows, :].astype(f32)
        centered = t - jnp.mean(t, axis=1, keepdims=True)
        inverse = lax.rsqrt(jnp.mean(centered * centered, axis=1, keepdims=True) + eps)
        n = normed[my_rows, :]
        igrad_ref[rows, :] = ct[rows, :] + inverse * (
            ng - jnp.mean(ng, axis=1, keepdims=True) - n * jnp.mean(ng * n, axis=1, keepdims=True)
        )

    z_third(9)
    z_second(11)
    for d in (1, 2, 3):
        vec_in[d].wait_recv()
    vec_core[core, 0:8, :] = vec_send[me] + (vec_recv[0] + vec_recv[1] + vec_recv[2])
    vec_core[core, 8:16, :] = jnp.concatenate(
        [up_bias_part[:, t * 256 : (t + 1) * 256] for t in range(3)] + [jnp.zeros((5, 256), f32)], axis=0
    )
    vec_twin = send("vec_twin", vec_core.at[core], vec_core.at[core], twin)
    vec_twin.wait_recv()
    vec_z[0] = vec_core[0] + vec_core[1]
    vec_first = remote("vec_z1", vec_z.at[0], vec_z.at[1], z_pair)
    vec_second = remote("vec_z2", vec_z.at[2], vec_z.at[3], z_mid)
    vec_third = remote("vec_z3", vec_ref, vec_ref, z_pair)

    @pl.when(outer)
    def _():
        vec_first.start()


    @pl.when(inner)
    def _():
        vec_first.wait_recv()
        vec_z[2] = vec_z[0] + vec_z[1]
        vec_second.start()

    z_third(10)
    for n in range(8, 10):
        z_fourth(n)


    @pl.when(inner)
    def _():
        vec_second.wait_recv()
        vec_ref[...] = vec_z[2] + vec_z[3]
        vec_third.start()

    z_third(11)
    z_fourth(10)
    z_fourth(11)

    @pl.when(inner)
    def _():
        vec_second.wait_send()
        vec_third.wait_send()

    @pl.when(outer)
    def _():
        vec_first.wait_send()
        vec_third.wait_recv()

    for k in range(12):
        z_finish(k)
    for copy in pending:
        copy.wait_send()


def widen_kernel(
    block_in, igrad_in, qkv_in, out_in, up_in, down_in, vec_in,
    block_ref, igrad_ref, qkv_ref, out_ref, up_ref, down_ref, *vec_refs,
):
    for source, target in ((qkv_in, qkv_ref), (out_in, out_ref), (up_in, up_ref), (down_in, down_ref)):
        target[...] = source[...].astype(jnp.float32)

    @pl.when(pl.program_id(0) == 0)
    def _():
        block_ref[...] = block_in[...]
        igrad_ref[...] = igrad_in[...]
        for r in range(5):
            vec_refs[r][...] = vec_in[r : r + 1, :SHARD]
        rows = [vec_in[r : r + 1, :] for r in (5, 6, 7)]
        vec_refs[5][...] = jnp.concatenate([pair_of(rows[0], rows[1]), rows[2]], axis=1)[:, : 3 * SHARD]
        vec_refs[6][...] = jnp.concatenate([vec_in[r : r + 1, :] for r in (8, 9, 10)], axis=1)


def rope_tables(length):
    half_rot = ROT // 2
    lane = np.arange(128) % HD
    frequency = 10000.0 ** (-(lane % half_rot).astype(np.float64) * (2.0 / ROT))
    angles = np.arange(length, dtype=np.float64)[:, None] * frequency[None, :]
    turned = lane < ROT
    cos = np.where(turned, np.cos(angles), 1.0)
    lo = np.where(lane < half_rot, -np.sin(angles), 0.0)
    hi = np.where(turned & (lane >= half_rot), np.sin(angles), 0.0)
    return tuple(t.astype(np.float32) for t in (cos, lo, hi))


def local_fused(
    inputs, qkv_weight, qkv_bias, out_weight, out_bias, up_weight, up_bias, down_weight, down_bias,
    attn_gain, attn_shift, mlp_gain, mlp_shift, cotangent,
):
    f32, bf16 = jnp.float32, jnp.bfloat16
    length = 512
    small = jnp.concatenate(
        [qkv_bias, out_bias, down_bias, attn_gain, attn_shift, mlp_gain, mlp_shift, up_bias]
    ).reshape(13, SHARD)

    def vmem(shape, dtype):
        return pltpu.VMEM(shape, dtype)

    inside = pl.BlockSpec(memory_space=pltpu.VMEM)
    anywhere = pl.BlockSpec(memory_space=pl.ANY)
    big = (length, D)
    outs = pl.pallas_call(
        block_kernel,
        out_shape=(
            jax.ShapeDtypeStruct((128, D), f32),
            jax.ShapeDtypeStruct((128, D), f32),
            jax.ShapeDtypeStruct((SHARD, 3 * D), bf16),
            jax.ShapeDtypeStruct((SHARD, D), bf16),
            jax.ShapeDtypeStruct((SHARD, 4 * D), bf16),
            jax.ShapeDtypeStruct((D, D), bf16),
            jax.ShapeDtypeStruct((16, 256), f32),
        ),
        in_specs=[inside] * 5 + [anywhere] * 5,
        out_specs=(inside,) * 2 + (anywhere,) * 4 + (inside,),
        scratch_shapes=[
            vmem((SHARD, 3 * D), bf16), vmem((SHARD, D), bf16), vmem((SHARD, 4 * D), bf16), vmem((D, D), bf16),
            vmem((128, D), f32), vmem((SHARD, 3 * D), bf16), vmem((D, D), bf16), vmem((SHARD, D), bf16),
            vmem((4, SHARD, 640), bf16), vmem((D, 640), bf16), vmem((D, D), bf16),
            vmem(big, bf16), vmem(big, bf16), vmem((4, 16, 256), f32), vmem((2, 48, D), bf16),
            vmem((2, 48, 640), bf16), vmem(big, f32), vmem(big, bf16),
            vmem(big, bf16),
            vmem(big, f32), vmem(big, f32), vmem(big, f32), vmem((D, D), f32), vmem(big, bf16), vmem(big, bf16),
            vmem((length, 256), bf16), vmem((length, 256), bf16), vmem((length, 256), bf16),
            vmem((length, 256), bf16), vmem((length, 256), f32), vmem((length, 256), bf16),
            vmem((256, length), f32), vmem((256, length), f32), vmem((256, length), bf16),
            vmem((256, length), bf16), vmem((length, 256), f32), vmem((length, 256), f32),
            vmem((length, 256), f32), vmem((length, 640), bf16),
            vmem((384, D), f32), vmem((D, D), f32), vmem((length, 640), f32), vmem((SHARD, D), f32),
            vmem((864, D), bf16), vmem((864, D), bf16), vmem((8, ROWS, 640), bf16), vmem((8, ROWS, 640), bf16),
            vmem((4, ROWS, D), bf16), vmem((12, ROWS, D), bf16), vmem((12, ROWS, D), bf16),
            vmem((12, ROWS, D), bf16), vmem((12, ROWS, D), bf16),
            vmem(big, bf16), vmem((3, 128, D), bf16), vmem(big, bf16), vmem((3, 128, D), bf16),
            vmem((4, 8, 256), f32), vmem((3, 8, 256), f32), vmem((2, 16, 256), f32), vmem((4, 16, 256), f32),
            pltpu.SemaphoreType.DMA((NSEM,)), pltpu.SemaphoreType.DMA((NSEM,)), pltpu.SemaphoreType.DMA((29,)),
        ],
        compiler_params=pltpu.CompilerParams(
            collective_id=0, has_side_effects=True, vmem_limit_bytes=56 * 1024 * 1024
        ),
    )(
        inputs[0], small, *(jnp.asarray(t) for t in rope_tables(length)),
        cotangent[0], qkv_weight, up_weight, down_weight, out_weight,
    )
    def part(shape, whole=False):
        return pl.BlockSpec(shape, (lambda i: (0, 0)) if whole else (lambda i: (i, 0)))

    steps = 6
    specs = [part((128, D), True)] * 2 + [
        part((SHARD // steps, 3 * D)), part((SHARD // steps, D)), part((SHARD // steps, 4 * D)), part((D // steps, D))
    ]
    widths = [SHARD] * 5 + [3 * SHARD, 4 * SHARD]
    (block_out, input_grad, gqkv, gout, gup, gdown, bias_sum, gain_attn, shift_attn, gain_mlp, shift_mlp, bqkv, bup) = (
        pl.pallas_call(
            widen_kernel,
            grid=(steps,),
            out_shape=tuple(jax.ShapeDtypeStruct(t.shape, f32) for t in outs[:6])
            + tuple(jax.ShapeDtypeStruct((1, n), f32) for n in widths),
            in_specs=specs + [part((16, 256), True)],
            out_specs=tuple(specs) + tuple(part((1, n), True) for n in widths),
        )(*outs)
    )
    bias_sum = bias_sum[0]
    return (
        block_out[None], input_grad[None], gqkv, bqkv[0], gout, bias_sum, gup, bup[0], gdown, bias_sum,
        gain_attn[0], shift_attn[0], gain_mlp[0], shift_mlp[0],
    )


def solution(mesh):
    fused = (mesh.shape["grp"], mesh.shape["rep"]) == (4, 8)
    local = local_fused if fused else local_by_tokens
    placed = (
        P("rep", "grp", None),
        P("grp", None),
        P("grp"),
        P("grp", None),
        P("grp"),
        P("grp", None),
        P("grp"),
        P("grp", None),
        P("grp"),
        P("grp"),
        P("grp"),
        P("grp"),
        P("grp"),
        P("rep", "grp", None),
    )
    return jax.shard_map(
        local,
        mesh=mesh,
        in_specs=placed,
        out_specs=(
            P("rep", "grp", None),
            P("rep", "grp", None),
            P("grp", None),
            P("grp"),
            P("grp", None),
            P("grp"),
            P("grp", None),
            P("grp"),
            P("grp", None),
            P("grp"),
            P("grp"),
            P("grp"),
            P("grp"),
            P("grp"),
        ),
        check_vma=False,
    )
```

```python
import jax
import jax.numpy as jnp
import numpy as np
from jax import lax
from jax.experimental import pallas as pl
from jax.experimental.pallas import tpu as pltpu
from jax.sharding import PartitionSpec as P

D = 768
HEADS = 12
HD = 64
ROT = 16


eps = 1e-05


def layer_norm(values):
    centered = values - jnp.mean(values, axis=-1, keepdims=True)
    variance = jnp.mean(centered * centered, axis=-1, keepdims=True)
    inverse = lax.rsqrt(variance + eps)
    return (centered * inverse, inverse)


def gelu_parts(preact):
    normal_cdf = 0.5 * (1.0 + jax.scipy.special.erf(preact * 0.7071067811865476))
    density = jnp.exp(-0.5 * preact * preact) * 0.3989422804014327
    return (preact * normal_cdf, normal_cdf + preact * density)


def angle_tables(positions):
    half_rot = ROT // 2
    frequency = 10000.0 ** (-jnp.arange(half_rot, dtype=jnp.float32) * (2.0 / ROT))
    angles = positions.astype(jnp.float32)[:, None] * frequency[None, :]
    return (jnp.cos(angles)[:, None, :], jnp.sin(angles)[:, None, :])


def rotate(tensor, cos_table, sin_table):
    half_rot = ROT // 2
    lower_part = tensor[..., :half_rot]
    upper_part = tensor[..., half_rot:ROT]
    return jnp.concatenate(
        [
            lower_part * cos_table - upper_part * sin_table,
            upper_part * cos_table + lower_part * sin_table,
            tensor[..., ROT:],
        ],
        axis=-1,
    )


def unrotate(tensor, cos_table, sin_table):
    half_rot = ROT // 2
    lower_part = tensor[..., :half_rot]
    upper_part = tensor[..., half_rot:ROT]
    return jnp.concatenate(
        [
            lower_part * cos_table + upper_part * sin_table,
            upper_part * cos_table - lower_part * sin_table,
            tensor[..., ROT:],
        ],
        axis=-1,
    )


def local_by_tokens(
    inputs,
    qkv_weight,
    qkv_bias,
    out_weight,
    out_bias,
    up_weight,
    up_bias,
    down_weight,
    down_bias,
    attn_gain,
    attn_shift,
    mlp_gain,
    mlp_shift,
    cotangent,
):
    tokens = inputs.shape[1]
    (
        full_qkv,
        full_qkv_bias,
        full_out,
        full_out_bias,
        full_up,
        full_up_bias,
        full_down,
        full_down_bias,
        gain_attn,
        shift_attn,
        gain_mlp,
        shift_mlp,
    ) = (
        lax.all_gather(qkv_weight, "grp", axis=0, tiled=True),
        lax.all_gather(qkv_bias, "grp", axis=0, tiled=True),
        lax.all_gather(out_weight, "grp", axis=0, tiled=True),
        lax.all_gather(out_bias, "grp", axis=0, tiled=True),
        lax.all_gather(up_weight, "grp", axis=0, tiled=True),
        lax.all_gather(up_bias, "grp", axis=0, tiled=True),
        lax.all_gather(down_weight, "grp", axis=0, tiled=True),
        lax.all_gather(down_bias, "grp", axis=0, tiled=True),
        lax.all_gather(attn_gain, "grp", axis=0, tiled=True),
        lax.all_gather(attn_shift, "grp", axis=0, tiled=True),
        lax.all_gather(mlp_gain, "grp", axis=0, tiled=True),
        lax.all_gather(mlp_shift, "grp", axis=0, tiled=True),
    )
    first_row = lax.axis_index("grp") * tokens
    positions = first_row + jnp.arange(tokens, dtype=jnp.int32)
    cos_table, sin_table = angle_tables(positions)
    score_scale = HD ** (-0.5)
    hidden_in = inputs[0].astype(jnp.float32)
    normed, inverse = layer_norm(hidden_in)
    attn_in = (normed * gain_attn.astype(jnp.float32) + shift_attn.astype(jnp.float32)).astype(
        jnp.bfloat16
    )
    mlp_in = (normed * gain_mlp.astype(jnp.float32) + shift_mlp.astype(jnp.float32)).astype(
        jnp.bfloat16
    )
    qkv = jnp.dot(attn_in, full_qkv, preferred_element_type=jnp.float32) + full_qkv_bias.astype(
        jnp.float32
    )
    query_b = rotate(qkv[:, :D].reshape(tokens, HEADS, HD), cos_table, sin_table).astype(
        jnp.bfloat16
    )
    keys_local = (
        rotate(qkv[:, D : 2 * D].reshape(tokens, HEADS, HD), cos_table, sin_table)
        .astype(jnp.bfloat16)
        .reshape(tokens, D)
    )
    values_local = qkv[:, 2 * D :].astype(jnp.bfloat16)
    keys_all, values_all = (
        lax.all_gather(keys_local, "grp", axis=0, tiled=True),
        lax.all_gather(values_local, "grp", axis=0, tiled=True),
    )
    length = keys_all.shape[0]
    visible = jnp.arange(length, dtype=jnp.int32)[None, :] <= positions[:, None]
    query_heads = jnp.transpose(query_b, (1, 0, 2))
    key_heads = jnp.transpose(keys_all.reshape(length, HEADS, HD), (1, 0, 2))
    value_heads = jnp.transpose(values_all.reshape(length, HEADS, HD), (1, 0, 2))

    def forward_head(operands):
        query_one, key_one, value_one = operands
        scores = jnp.dot(query_one, key_one.T, preferred_element_type=jnp.float32) * score_scale
        scores = jnp.where(visible, scores, -jnp.inf)
        row_max = jnp.max(scores, axis=-1, keepdims=True)
        log_total = row_max + jnp.log(jnp.sum(jnp.exp(scores - row_max), axis=-1, keepdims=True))
        probs_b = jnp.exp(scores - log_total).astype(jnp.bfloat16)
        context_one = jnp.dot(probs_b, value_one, preferred_element_type=jnp.float32).astype(
            jnp.bfloat16
        )
        return (context_one, log_total)

    context_heads, log_totals = lax.map(forward_head, (query_heads, key_heads, value_heads))
    context = jnp.transpose(context_heads, (1, 0, 2)).reshape(tokens, D)
    attn_out = jnp.dot(
        context, full_out, preferred_element_type=jnp.float32
    ) + full_out_bias.astype(jnp.float32)
    preact = jnp.dot(mlp_in, full_up, preferred_element_type=jnp.float32) + full_up_bias.astype(
        jnp.float32
    )
    activation, slope = gelu_parts(preact)
    act_b = activation.astype(jnp.bfloat16)
    mlp_out = jnp.dot(act_b, full_down, preferred_element_type=jnp.float32) + full_down_bias.astype(
        jnp.float32
    )
    block_out = hidden_in + attn_out + mlp_out
    back_qkv, back_out, back_up, back_down, back_gain_attn, back_gain_mlp = (
        lax.all_gather(qkv_weight, "grp", axis=0, tiled=True),
        lax.all_gather(out_weight, "grp", axis=0, tiled=True),
        lax.all_gather(up_weight, "grp", axis=0, tiled=True),
        lax.all_gather(down_weight, "grp", axis=0, tiled=True),
        lax.all_gather(attn_gain, "grp", axis=0, tiled=True),
        lax.all_gather(mlp_gain, "grp", axis=0, tiled=True),
    )
    grad_out = cotangent[0]
    grad_b = grad_out.astype(jnp.bfloat16)
    down_grad = jnp.dot(act_b.T, grad_b, preferred_element_type=jnp.float32)
    out_grad = jnp.dot(context.T, grad_b, preferred_element_type=jnp.float32)
    bias_sum = jnp.sum(grad_out, axis=0)
    preact_grad = jnp.dot(grad_b, back_down.T, preferred_element_type=jnp.float32) * slope
    up_bias_grad = jnp.sum(preact_grad, axis=0)
    preact_b = preact_grad.astype(jnp.bfloat16)
    up_grad = jnp.dot(mlp_in.T, preact_b, preferred_element_type=jnp.float32)
    mlp_in_grad = jnp.dot(preact_b, back_up.T, preferred_element_type=jnp.float32)
    context_grad = jnp.dot(grad_b, back_out.T, preferred_element_type=jnp.float32).astype(
        jnp.bfloat16
    )
    context_grad_heads = jnp.transpose(context_grad.reshape(tokens, HEADS, HD), (1, 0, 2))

    def backward_head(operands):
        query_one, key_one, value_one, grad_one, log_total = operands
        scores = jnp.dot(query_one, key_one.T, preferred_element_type=jnp.float32) * score_scale
        scores = jnp.where(visible, scores, -jnp.inf)
        attn_probs = jnp.exp(scores - log_total)
        probs_b = attn_probs.astype(jnp.bfloat16)
        prob_grad = jnp.dot(grad_one, value_one.T, preferred_element_type=jnp.float32)
        row_dot = jnp.sum(attn_probs * prob_grad, axis=-1, keepdims=True)
        score_grad = (attn_probs * (prob_grad - row_dot) * score_scale).astype(jnp.bfloat16)
        query_grad = jnp.dot(score_grad, key_one, preferred_element_type=jnp.float32)
        key_grad = jnp.dot(score_grad.T, query_one, preferred_element_type=jnp.float32)
        value_grad = jnp.dot(probs_b.T, grad_one, preferred_element_type=jnp.float32)
        return (query_grad, key_grad, value_grad)

    query_grads, key_grads, value_grads = lax.map(
        backward_head, (query_heads, key_heads, value_heads, context_grad_heads, log_totals)
    )
    key_full = jnp.transpose(key_grads, (1, 0, 2)).reshape(length, D)
    value_full = jnp.transpose(value_grads, (1, 0, 2)).reshape(length, D)
    key_mine, value_mine = (
        lax.psum_scatter(key_full, "grp", scatter_dimension=0, tiled=True),
        lax.psum_scatter(value_full, "grp", scatter_dimension=0, tiled=True),
    )
    query_rows = unrotate(jnp.transpose(query_grads, (1, 0, 2)), cos_table, sin_table).reshape(
        tokens, D
    )
    key_rows = unrotate(key_mine.reshape(tokens, HEADS, HD), cos_table, sin_table).reshape(
        tokens, D
    )
    qkv_rows = jnp.concatenate([query_rows, key_rows, value_mine], axis=1)
    qkv_bias_grad = jnp.sum(qkv_rows, axis=0)
    qkv_rows_b = qkv_rows.astype(jnp.bfloat16)
    qkv_grad = jnp.dot(attn_in.T, qkv_rows_b, preferred_element_type=jnp.float32)
    attn_in_grad = jnp.dot(qkv_rows_b, back_qkv.T, preferred_element_type=jnp.float32)
    attn_gain_grad = jnp.sum(attn_in_grad * normed, axis=0)
    attn_shift_grad = jnp.sum(attn_in_grad, axis=0)
    mlp_gain_grad = jnp.sum(mlp_in_grad * normed, axis=0)
    mlp_shift_grad = jnp.sum(mlp_in_grad, axis=0)
    normed_grad = attn_in_grad * back_gain_attn.astype(
        jnp.float32
    ) + mlp_in_grad * back_gain_mlp.astype(jnp.float32)
    input_grad = grad_out + inverse * (
        normed_grad
        - jnp.mean(normed_grad, axis=-1, keepdims=True)
        - normed * jnp.mean(normed_grad * normed, axis=-1, keepdims=True)
    )
    group_parts = (
        lax.psum_scatter(qkv_grad, "grp", scatter_dimension=0, tiled=True),
        lax.psum_scatter(qkv_bias_grad, "grp", scatter_dimension=0, tiled=True),
        lax.psum_scatter(out_grad, "grp", scatter_dimension=0, tiled=True),
        lax.psum_scatter(bias_sum, "grp", scatter_dimension=0, tiled=True),
        lax.psum_scatter(up_grad, "grp", scatter_dimension=0, tiled=True),
        lax.psum_scatter(up_bias_grad, "grp", scatter_dimension=0, tiled=True),
        lax.psum_scatter(down_grad, "grp", scatter_dimension=0, tiled=True),
        lax.psum_scatter(attn_gain_grad, "grp", scatter_dimension=0, tiled=True),
        lax.psum_scatter(attn_shift_grad, "grp", scatter_dimension=0, tiled=True),
        lax.psum_scatter(mlp_gain_grad, "grp", scatter_dimension=0, tiled=True),
        lax.psum_scatter(mlp_shift_grad, "grp", scatter_dimension=0, tiled=True),
    )
    (
        qkv_part,
        qkv_bias_part,
        out_part,
        bias_part,
        up_part,
        up_bias_part,
        down_part,
        gain_attn_part,
        shift_attn_part,
        gain_mlp_part,
        shift_mlp_part,
    ) = group_parts
    (
        qkv_total,
        qkv_bias_total,
        out_total,
        bias_total,
        up_total,
        up_bias_total,
        down_total,
        gain_attn_total,
        shift_attn_total,
        gain_mlp_total,
        shift_mlp_total,
    ) = lax.psum(
        (
            qkv_part,
            qkv_bias_part,
            out_part,
            bias_part,
            up_part,
            up_bias_part,
            down_part,
            gain_attn_part,
            shift_attn_part,
            gain_mlp_part,
            shift_mlp_part,
        ),
        "rep",
    )
    return (
        block_out[None],
        input_grad[None],
        qkv_total,
        qkv_bias_total,
        out_total,
        bias_total,
        up_total,
        up_bias_total,
        down_total,
        bias_total,
        gain_attn_total,
        shift_attn_total,
        gain_mlp_total,
        shift_mlp_total,
    )


ROWS = 96
SHARD = 192
MESH = pl.DeviceIdType.MESH
NSEM = 128
UP, RL, UL, UM, RR, UR, RA, UA, US, UU, UN, UB, UC = 2, 16, 4, 1, 16, 4, 16, 4, 1, 4, 1, 4, 2


def mm(a, b):
    return lax.dot_general(a, b, (((1,), (0,)), ((), ())), preferred_element_type=jnp.float32)


def mm_tn(a, b):
    return lax.dot_general(a, b, (((0,), (0,)), ((), ())), preferred_element_type=jnp.float32)


def mm_nt(a, b):
    return lax.dot_general(a, b, (((1,), (1,)), ((), ())), preferred_element_type=jnp.float32)


def keep_192(t):
    lane = lax.broadcasted_iota(jnp.int32, t.shape, 1)
    return jnp.where(lane < SHARD, t, 0.0)


def block_of(t, j):
    base = (j // 2) * 384
    if j % 2 == 0:
        return keep_192(t[:, base : base + 256])
    return keep_192(pltpu.roll(t[:, base + 128 : base + 384], 192, 1))


def pair_of(a, b):
    shifted = pltpu.roll(b, 64, 1)
    return jnp.concatenate([a[:, :128], shifted[:, :128] + a[:, 128:], shifted[:, 128:]], axis=1)


def gelu_with_slope(preact):
    normal_cdf = 0.5 * (1.0 + lax.erf(preact * 0.7071067811865476))
    density = jnp.exp(-0.5 * preact * preact) * 0.3989422804014327
    return preact * normal_cdf, normal_cdf + preact * density


def block_kernel(
    x_ref, bqkv_ref, bout_ref, bdown_ref, ga_ref, sa_ref, gm_ref, sm_ref, bup_ref, cos_ref, sin_lo_ref, sin_hi_ref,
    ct_hbm, wqkv_hbm, wup_hbm, wdown_hbm, wout_hbm,
    block_hbm, igrad_hbm, qkv_hbm, out_hbm, up_hbm, down_hbm, vec_ref, block_ref, igrad_ref,
    gqkv_ref, gout_ref, gup_ref, gdown_ref,
    ct, w_qkv_in, w_down, w_out, w_pack, w_qkv, w_up,
    x_all, g_all, small_all, row640, up_way, qkv_way, normed, attn_in, mlp_in,
    acc_a, acc_b, acc_c, act_b, preact_b,
    q_b, k_b, v_b, cg_b, ctx_f, ctx_b, s_buf, dp_buf, p_b, ds_b, dq_f, dk_f, dv_f, rows_b,
    down_own, up_full, qkv_full, out_full,
    part_send, part_recv, tq_send, tq_recv, tu_send, chunk, z_in, z_sum, z_other,
    rs_out, rs_out_in, rs_in, rs_in_in,
    vec_send, vec_recv, vec_core, vec_z,
    send_sem, recv_sem, local_sem,
):
    f32, bf16 = jnp.float32, jnp.bfloat16
    me = lax.axis_index("grp")
    rep = lax.axis_index("rep")
    z, core = rep // 2, rep % 2
    mx, my = me % 2, me // 2
    inner = (z == 1) | (z == 2)
    outer = (z == 0) | (z == 3)
    peers = {1: my * 2 + (1 - mx), 2: (1 - my) * 2 + mx, 3: (1 - my) * 2 + (1 - mx)}
    twin = (me, z * 2 + (1 - core))
    z_pair = (me, (z + 1 - 2 * (z % 2)) * 2 + core)
    z_mid = (me, (3 - z) * 2 + core)

    def group(d):
        return (peers[d], rep)

    names = {}

    def over(count, step, unroll):
        def run(body):
            @pl.loop(0, count // step, unroll=unroll)
            def _(i):
                body(pl.multiple_of(i * step, step))

        return run

    def remote(name, src, dst, device):
        i = names.setdefault(name, len(names))
        assert i < NSEM
        return pltpu.make_async_remote_copy(
            src_ref=src, dst_ref=dst, send_sem=send_sem.at[i], recv_sem=recv_sem.at[i],
            device_id=device, device_id_type=MESH,
        )

    pending = []

    def send(name, src, dst, device):
        copy = remote(name, src, dst, device)
        copy.start()
        pending.append(copy)
        return copy

    def at(start, size, multiple=None):
        return pl.ds(pl.multiple_of(start, multiple or size), size)

    barrier = pltpu.get_barrier_semaphore()
    everyone = [group(d) for d in (1, 2, 3)] + [twin, z_pair]
    for device in everyone:
        pl.semaphore_signal(barrier, inc=1, device_id=device, device_id_type=MESH)

    @pl.when(inner)
    def _():
        pl.semaphore_signal(barrier, inc=1, device_id=z_mid, device_id_type=MESH)

    locals_ = [
        pltpu.make_async_copy(ct_hbm, ct, local_sem.at[0]),
        pltpu.make_async_copy(wqkv_hbm, w_qkv_in, local_sem.at[1]),
        pltpu.make_async_copy(wdown_hbm, w_down, local_sem.at[2]),
        pltpu.make_async_copy(wout_hbm, w_out, local_sem.at[3]),
        pltpu.make_async_copy(
            wup_hbm.at[:, at(me * D, D, 128)], w_up.at[at(me * SHARD, SHARD)], local_sem.at[4]
        ),
    ]
    for copy in locals_:
        copy.start()

    small_all[me] = jnp.zeros((16, 256), f32)
    row640[...] = jnp.zeros((1, 640), f32)
    row640[:, : 3 * SHARD] = bqkv_ref[...].astype(f32).reshape(1, 3 * SHARD)
    for r in range(3):
        small_all[me, r : r + 1, :] = block_of(row640[...], r)
    for r, ref in enumerate((bout_ref, bdown_ref, ga_ref, sa_ref, gm_ref, sm_ref)):
        small_all[me, 3 + r : 4 + r, 0:SHARD] = ref[...].astype(f32).reshape(1, SHARD)
    mine = at(me * 128, 128)
    x_all[mine, :] = x_ref[...]
    bias_up = bup_ref[...].astype(f32).reshape(1, D)
    pl.semaphore_wait(barrier, len(everyone) + inner.astype(jnp.int32))

    half = at(me * SHARD + core * ROWS, ROWS)
    small_in = {d: send(("small", d), small_all.at[me], small_all.at[me], group(d)) for d in (3, 1, 2)}

    def spread_rows(name, buffer):
        copies = {}
        for h in (0, 1):
            for d in (1, 2):
                part = h if d == 1 else 1 - h
                rows = at(me * 128 + part * 64, 64)
                copies[d, part] = send((name, d, part), buffer.at[rows], buffer.at[rows], group(d))
        return copies

    def forward_rows(name, buffer, copies):
        onward = []
        for d in (1, 2):
            part = d - 1
            copies[d, part].wait_recv()
            rows = at(peers[d] * 128 + part * 64, 64)
            onward.append(send((name, "on", part), buffer.at[rows], buffer.at[rows], group(3 - d)))
        return onward

    def spread_columns(name, source, way, buffer):
        copies = {}
        for d in (1, 2):
            part = d - 1
            copies["way", part] = send(
                (name, "way", part), source(3, core * ROWS + part * 48, 48), way.at[part], group(d)
            )
        for d in (1, 2):
            copies[d] = send((name, d), source(d, core * ROWS, ROWS), buffer.at[half], group(d))
        return copies

    def forward_columns(name, way, buffer, copies):
        onward = []
        for d in (1, 2):
            part = d - 1
            copies["way", part].wait_recv()
            rows = at(peers[d] * SHARD + core * ROWS + part * 48, 48)
            onward.append(send((name, "on", part), way.at[part], buffer.at[rows], group(3 - d)))
        return onward

    def share_weight(name, buffer, copies, onward):
        twins = []
        for d in (1, 2, 3):
            if d == 3:
                for copy in onward:
                    copy.wait_recv()
            else:
                copies[d].wait_recv()
            rows = at(peers[d] * SHARD + core * ROWS, ROWS)
            twins.append(send((name, "twin", d), buffer.at[rows], buffer.at[rows], twin))
        return twins

    def up_source(d, start, size):
        return wup_hbm.at[at(start, size, 16), at(peers[d] * D, D, 128)]

    def qkv_source(d, start, size):
        return w_pack.at[peers[d], at(start, size, 16)]

    x_in = spread_rows("x", x_all)
    up_in = spread_columns("up", up_source, up_way, w_up)
    locals_[0].wait()
    g_all[mine, :] = ct[...].astype(bf16)

    for d in (1, 2, 3):
        small_in[d].wait_recv()

    def vector(r):
        rows = [small_all[i, r : r + 1] for i in range(4)]
        return jnp.concatenate([pair_of(rows[0], rows[1]), pair_of(rows[2], rows[3])], axis=1)

    gain_attn, shift_attn, gain_mlp, shift_mlp = vector(5), vector(6), vector(7), vector(8)
    bias = vector(3) + vector(4)
    bias_qkv = jnp.zeros((1, 640), f32)
    for j in range(4):
        a, b, c = (
            small_all[(4 * t + j) // 3, (4 * t + j) % 3 : (4 * t + j) % 3 + 1] for t in range(3)
        )
        bias_qkv = jnp.where(me == j, jnp.concatenate([pair_of(a, b), c], axis=1), bias_qkv)

    def norm_rows(start):
        @over(128, RL, UL)
        def _(i):
            rows = pl.ds(pl.multiple_of(start + i, RL), RL)
            t = x_all[rows, :].astype(f32)
            centered = t - jnp.mean(t, axis=1, keepdims=True)
            inverse = lax.rsqrt(jnp.mean(centered * centered, axis=1, keepdims=True) + eps)
            n = centered * inverse
            normed[rows, :] = n
            attn_in[rows, :] = (n * gain_attn + shift_attn).astype(bf16)
            mlp_in[rows, :] = (n * gain_mlp + shift_mlp).astype(bf16)

    norm_rows(me * 128)
    x_on = forward_rows("x", x_all, x_in)
    g_in = spread_rows("g", g_all)
    for d in (1, 2):
        x_in[d, 2 - d].wait_recv()
        norm_rows(peers[d] * 128)
    up_on = forward_columns("up", up_way, w_up, up_in)
    locals_[1].wait()

    @over(SHARD, 32, UP)
    def _(start):
        rows = pl.ds(start, 32)
        wide = w_qkv_in[rows, :].astype(f32)
        for j in range(4):
            a, b, c = (block_of(wide[:, t * D : (t + 1) * D], j) for t in range(3))
            w_pack[j, rows, :] = jnp.concatenate([pair_of(a, b), c], axis=1).astype(bf16)

    w_qkv[at(me * SHARD, SHARD), :] = w_pack[me]
    for copy in x_on:
        copy.wait_recv()
    norm_rows(peers[3] * 128)

    up_twins = share_weight("up", w_up, up_in, up_on)
    g_on = forward_rows("g", g_all, g_in)
    qkv_in = spread_columns("qkv", qkv_source, qkv_way, w_qkv)
    locals_[4].wait()
    for copy in up_twins:
        copy.wait_recv()

    acc_a[...] = mm(mlp_in[...], w_up[...])

    @over(512, 16, UM)
    def _(start):
        rows = pl.ds(start, 16)
        activation, slope = gelu_with_slope(acc_a[rows, :] + bias_up)
        act_b[rows, :] = activation.astype(bf16)
        acc_a[rows, :] = slope

    locals_[2].wait()
    locals_[3].wait()
    acc_b[...] = mm(act_b[...], w_down[...])

    for d in (1, 2):
        g_in[d, 2 - d].wait_recv()
    for copy in g_on:
        copy.wait_recv()
    g = g_all[...]
    other_cols = at((1 - core) * 384, 384)
    own_cols = at(core * 384, 384)

    part_send[0:384, :] = mm_tn(act_b[:, other_cols], g).astype(bf16)
    down_part = send("part_down", part_send.at[0:384], part_recv.at[0:384], twin)
    down_own[...] = mm_tn(act_b[:, own_cols], g)
    acc_c[...] = mm_nt(g, w_down[...])

    def slope_rows(i, total):
        rows = at(i * 16, 16)
        pg = acc_c[rows, :] * acc_a[rows, :]
        preact_b[rows, :] = pg.astype(bf16)
        return total + pg[:8] + pg[8:]

    up_bias_part = lax.fori_loop(0, 512 // 16, slope_rows, jnp.zeros((8, D), f32), unroll=US)
    up_bias_part = jnp.sum(up_bias_part, axis=0, keepdims=True)

    up_full[...] = mm_tn(mlp_in[...], preact_b[...])
    for j in range(4):
        part_send[384 + j * ROWS : 384 + (j + 1) * ROWS, :] = up_full[
            at(j * SHARD + (1 - core) * ROWS, ROWS), :
        ].astype(bf16)
    up_part = send("part_up", part_send.at[384:768], part_recv.at[384:768], twin)

    def total_of(refs, k, which):
        gqkv, gout, gup, gdown = refs
        if k < 4:
            return gdown.at[at(which * 384 + k * ROWS, ROWS)]
        if k < 8:
            return gup.at[at(which * ROWS, ROWS), (k - 4) * D : (k - 3) * D]
        if k == 8:
            return gout.at[at(which * ROWS, ROWS)]
        return gqkv.at[at(which * ROWS, ROWS), (k - 9) * D : (k - 8) * D]

    def total_ref(k, which):
        return total_of((gqkv_ref, gout_ref, gup_ref, gdown_ref), k, which)

    def store_total(k, which, i):
        return pltpu.make_async_copy(
            total_ref(k, which),
            total_of((qkv_hbm, out_hbm, up_hbm, down_hbm), k, which),
            local_sem.at[5 + 2 * k + i],
        )

    def z_first(k):
        @pl.when(outer)
        def _():
            remote(("z1", k), chunk.at[k], z_in.at[k], z_pair).start()

    def z_second(k):
        @pl.when(inner)
        def _():
            remote(("z1", k), chunk.at[k], z_in.at[k], z_pair).wait_recv()
            z_sum[k] = (chunk[k].astype(f32) + z_in[k].astype(f32)).astype(bf16)
            remote(("z2", k), z_sum.at[k], z_other.at[k], z_mid).start()

    def hand_over(k):
        own = total_ref(k, core)
        remote(("last", k), own, own, twin).start()
        store_total(k, core, 0).start()

    def z_third(k):
        @pl.when(inner)
        def _():
            own = total_ref(k, core)
            remote(("z2", k), z_sum.at[k], z_other.at[k], z_mid).wait_recv()
            own[...] = (z_sum[k].astype(f32) + z_other[k].astype(f32)).astype(bf16)
            remote(("z3", k), own, own, z_pair).start()
            hand_over(k)

    def z_late(k):
        @pl.when(outer)
        def _():
            own = total_ref(k, core)
            remote(("z3", k), own, own, z_pair).wait_recv()
            hand_over(k)

    def z_fourth(k):
        remote(("last", k), total_ref(k, 1 - core), total_ref(k, 1 - core), twin).wait_recv()
        store_total(k, 1 - core, 1).start()

    def z_finish(k):
        own = total_ref(k, core)
        last = remote(("last", k), own, own, twin)
        last.wait_send()
        store_total(k, core, 0).wait()
        store_total(k, 1 - core, 1).wait()

        @pl.when(inner)
        def _():
            remote(("z2", k), z_sum.at[k], z_other.at[k], z_mid).wait_send()
            remote(("z3", k), own, own, z_pair).wait_send()

        @pl.when(outer)
        def _():
            remote(("z1", k), chunk.at[k], z_in.at[k], z_pair).wait_send()

    down_part.wait_recv()
    for k in range(4):
        rows = pl.ds(k * ROWS, ROWS)
        chunk[k] = (down_own[rows, :] + part_recv[rows, :].astype(f32)).astype(bf16)
        z_first(k)

    acc_c[...] = mm_nt(preact_b[...], w_up[...])
    cg_b[...] = jnp.zeros_like(cg_b)
    cg_b[:, :SHARD] = mm_nt(g, w_out[...]).astype(bf16)

    up_part.wait_recv()
    for j in range(4):
        tu_send[j] = (
            up_full[at(j * SHARD + core * ROWS, ROWS), :]
            + part_recv[384 + j * ROWS : 384 + (j + 1) * ROWS, :].astype(f32)
        ).astype(bf16)
    chunk[4 + me] = tu_send[me]
    tu_in = {d: send(("tu", d), tu_send.at[peers[d]], chunk.at[4 + me], group(d)) for d in (3, 1, 2)}

    qkv_on = forward_columns("qkv", qkv_way, w_qkv, qkv_in)
    qkv_twins = share_weight("qkv", w_qkv, qkv_in, qkv_on)
    for copy in qkv_twins:
        copy.wait_recv()
    qkv_full[...] = mm(attn_in[...], w_qkv[...])
    z_second(0)

    def turn(t, cos, lo, hi):
        return t * cos + pltpu.roll(t, 376, 1) * lo + pltpu.roll(t, 8, 1) * hi

    def tables(rows):
        return tuple(
            jnp.concatenate([ref[rows, :]] * 3, axis=1) for ref in (cos_ref, sin_lo_ref, sin_hi_ref)
        )

    @over(512, RR, UR)
    def _(start):
        rows = pl.ds(start, RR)
        t = qkv_full[rows, :] + bias_qkv
        cos, lo, hi = tables(rows)
        qk = turn(t[:, :384], cos, lo, hi)
        q_b[rows, :] = (keep_192(qk[:, :256]) * 0.125).astype(bf16)
        k_b[rows, :] = keep_192(pltpu.roll(qk[:, 128:384], 192, 1)).astype(bf16)
        v_b[rows, :] = keep_192(t[:, 384:640]).astype(bf16)

    z_second(1)
    ctx_f[...] = jnp.zeros_like(ctx_f)
    dq_f[...] = jnp.zeros_like(dq_f)
    dk_f[...] = jnp.zeros_like(dk_f)
    dv_f[...] = jnp.zeros_like(dv_f)
    lane256 = lax.broadcasted_iota(jnp.int32, (1, 256), 1)
    for h in range(3):
        mask = ((lane256 >= h * 64) & (lane256 < (h + 1) * 64)).astype(bf16)
        for block in range(2):
            keys = (block + 1) * 256
            rows_q = slice(block * 256, (block + 1) * 256)
            q_h = q_b[rows_q, :] * mask
            cg_h = cg_b[rows_q, :] * mask
            s_buf[:, :keys] = mm_nt(q_h, k_b[:keys, :])
            dp_buf[:, :keys] = mm_nt(cg_h, v_b[:keys, :])

            @over(256, RA, UA)
            def _(start, keys=keys, block=block):
                rows = pl.ds(start, RA)
                s = s_buf[rows, :keys]
                key_at = lax.broadcasted_iota(jnp.int32, (RA, keys), 1)
                query_at = lax.broadcasted_iota(jnp.int32, (RA, keys), 0) + (block * 256 + start)
                s = jnp.where(key_at <= query_at, s, -jnp.inf)
                e = jnp.exp(s - jnp.max(s, axis=1, keepdims=True))
                dp = dp_buf[rows, :keys]
                share = 1.0 / jnp.sum(e, axis=1, keepdims=True)
                row_dot = jnp.sum(e * dp, axis=1, keepdims=True) * share
                p = e * share
                p_b[rows, :keys] = p.astype(bf16)
                ds_b[rows, :keys] = (p * (dp - row_dot)).astype(bf16)

            ctx_f[rows_q, :] += mm(p_b[:, :keys], v_b[:keys, :] * mask)
            dq_f[rows_q, :] += mm(ds_b[:, :keys], k_b[:keys, :] * mask)
            dk_f[:keys, :] += mm_tn(ds_b[:, :keys], q_h)
            dv_f[:keys, :] += mm_tn(p_b[:, :keys], cg_h)
            if (h, block) == (0, 1):
                z_second(2)
                z_third(0)
            elif (h, block) == (1, 0):
                for d in (1, 2, 3):
                    tu_in[d].wait_recv()
                for k in range(4, 8):
                    z_first(k)
                z_third(1)
            elif (h, block) == (1, 1):
                z_second(3)
            elif (h, block) == (2, 0):
                z_third(2)

    z_second(4)
    ctx_b[...] = ctx_f[...].astype(bf16)
    out_full[...] = mm_tn(ctx_b[:, :SHARD], g)
    part_send[768 : 768 + ROWS, :] = out_full[at((1 - core) * ROWS, ROWS), :].astype(bf16)
    out_part = send("part_out", part_send.at[768:864], part_recv.at[768:864], twin)

    z_third(3)

    def unturn_rows(i, totals):
        rows = at(i * 16, 16)
        cos, lo, hi = tables(rows)
        qk = pair_of(dq_f[rows, :] * 0.125, dk_f[rows, :])
        qk = turn(qk, cos, -lo, -hi)
        full = jnp.concatenate([qk, dv_f[rows, :]], axis=1)
        rows_b[rows, :] = full.astype(bf16)
        return totals + full[:8] + full[8:]

    qkv_bias_part = lax.fori_loop(0, 512 // 16, unturn_rows, jnp.zeros((8, 640), f32), unroll=UU)
    qkv_bias_part = jnp.sum(qkv_bias_part, axis=0, keepdims=True)

    up_full[:, :640] = mm_tn(attn_in[...], rows_b[...])
    for j in range(4):
        tq_send[4 + j] = up_full[at(j * SHARD + (1 - core) * ROWS, ROWS), :640].astype(bf16)
    qkv_part = send("part_qkv", tq_send.at[4:8], tq_recv.at[4:8], twin)
    out_part.wait_recv()
    chunk[8] = (out_full[at(core * ROWS, ROWS), :] + part_recv[768:864, :].astype(f32)).astype(bf16)
    z_first(8)
    qkv_part.wait_recv()
    for j in range(4):
        tq_send[j] = (
            up_full[at(j * SHARD + core * ROWS, ROWS), :640] + tq_recv[4 + j].astype(f32)
        ).astype(bf16)
    tq_recv[me] = tq_send[me]
    tq_in = {d: send(("tq", d), tq_send.at[peers[d]], tq_recv.at[me], group(d)) for d in (3, 1, 2)}

    z_second(5)
    z_third(4)
    acc_b_in = mm_nt(rows_b[...], w_qkv[...])
    up_full[0:512, :] = acc_b_in

    def norm_grad_rows(i, totals):
        rows = at(i * 16, 16)
        ag, mg, n = up_full[rows, :], acc_c[rows, :], normed[rows, :]
        both = ag * gain_attn + mg * gain_mlp
        acc_c[rows, :] = both
        rs_in[rows, :] = both.astype(bf16)
        new = (ag * n, ag, mg * n, mg)
        return tuple(t + v[:8] + v[8:] for t, v in zip(totals, new))

    sums = lax.fori_loop(0, 512 // 16, norm_grad_rows, (jnp.zeros((8, D), f32),) * 4, unroll=UN)
    z_second(6)
    z_third(5)

    def rows_sum(t):
        return jnp.sum(t, axis=0, keepdims=True)

    wide = jnp.concatenate(
        [rows_sum(ct[...])] + [rows_sum(t) for t in sums] + [jnp.zeros((3, D), f32)], axis=0
    )
    types = [
        keep_192(qkv_bias_part[:, :256]),
        keep_192(pltpu.roll(qkv_bias_part[:, 128:384], 192, 1)),
        keep_192(qkv_bias_part[:, 384:640]),
    ]
    for j in range(4):
        vec_send[j] = block_of(wide, j)
        for t in range(3):
            b = 3 * j + t
            vec_send[j, 5 + t : 6 + t, :] = jnp.where(me == b % 4, types[b // 4], 0.0)
    vec_in = {d: send(("vec", d), vec_send.at[peers[d]], vec_recv.at[d - 1], group(d)) for d in (3, 1, 2)}
    acc_b[...] += mm(ctx_b[:, :SHARD], w_out[...])
    rs_out[...] = acc_b[...].astype(bf16)
    z_second(7)
    z_third(6)

    for d in (1, 2, 3):
        tq_in[d].wait_recv()

    @over(ROWS, 16, UC)
    def _(start):
        rows = pl.ds(start, 16)
        parts = [tq_recv[j, rows, :].astype(f32) for j in range(4)]
        for t in range(3):
            if t == 0:
                blocks = [keep_192(v[:, :256]) for v in parts]
            elif t == 1:
                blocks = [keep_192(pltpu.roll(v[:, 128:384], 192, 1)) for v in parts]
            else:
                blocks = [keep_192(v[:, 384:640]) for v in parts]
            chunk[9 + t, rows, :] = jnp.concatenate(
                [pair_of(blocks[0], blocks[1]), pair_of(blocks[2], blocks[3])], axis=1
            ).astype(bf16)

    for k in range(9, 12):
        z_first(k)
    out_in = {
        d: send(("rs_out", d), rs_out.at[at(peers[d] * 128, 128)], rs_out_in.at[d - 1], group(d))
        for d in (3, 1, 2)
    }
    in_in = {
        d: send(("rs_in", d), rs_in.at[at(peers[d] * 128, 128)], rs_in_in.at[d - 1], group(d))
        for d in (3, 1, 2)
    }
    z_second(8)
    z_third(7)
    for n in range(5):
        z_late(n)


    for d in (1, 2, 3):
        vec_in[d].wait_recv()
    vec_core[core, 0:8, :] = vec_send[me] + (vec_recv[0] + vec_recv[1] + vec_recv[2])
    vec_core[core, 8:16, :] = jnp.concatenate(
        [up_bias_part[:, t * 256 : (t + 1) * 256] for t in range(3)] + [jnp.zeros((5, 256), f32)], axis=0
    )
    vec_twin = send("vec_twin", vec_core.at[core], vec_core.at[core], twin)
    z_second(9)
    z_third(8)
    vec_twin.wait_recv()
    vec_z[0] = vec_core[0] + vec_core[1]
    vec_first = remote("vec_z1", vec_z.at[0], vec_z.at[1], z_pair)
    vec_second = remote("vec_z2", vec_z.at[2], vec_z.at[3], z_mid)
    vec_third = remote("vec_z3", vec_ref, vec_ref, z_pair)

    @pl.when(outer)
    def _():
        vec_first.start()

    z_second(10)
    for n in range(5):
        z_fourth(n)
    z_third(9)

    @pl.when(inner)
    def _():
        vec_first.wait_recv()
        vec_z[2] = vec_z[0] + vec_z[1]
        vec_second.start()

    z_second(11)
    for n in range(5, 8):
        z_late(n)
    z_third(10)

    @pl.when(inner)
    def _():
        vec_second.wait_recv()
        vec_ref[...] = vec_z[2] + vec_z[3]
        vec_third.start()

    for d in (1, 2, 3):
        out_in[d].wait_recv()

    @over(128, 16, UB)
    def _(start):
        rows = pl.ds(start, 16)
        total = acc_b[pl.ds(pl.multiple_of(me * 128 + start, 16), 16), :]
        for d in range(3):
            total = total + rs_out_in[d, rows, :].astype(f32)
        block_ref[rows, :] = x_ref[rows, :].astype(f32) + bias + total


    block_store = pltpu.make_async_copy(block_ref, block_hbm, local_sem.at[29])
    block_store.start()
    for d in (1, 2, 3):
        in_in[d].wait_recv()

    @over(128, 16, UB)
    def _(start):
        rows = pl.ds(start, 16)
        my_rows = pl.ds(pl.multiple_of(me * 128 + start, 16), 16)
        ng = acc_c[my_rows, :]
        for d in range(3):
            ng = ng + rs_in_in[d, rows, :].astype(f32)
        t = x_ref[rows, :].astype(f32)
        centered = t - jnp.mean(t, axis=1, keepdims=True)
        inverse = lax.rsqrt(jnp.mean(centered * centered, axis=1, keepdims=True) + eps)
        n = normed[my_rows, :]
        igrad_ref[rows, :] = ct[rows, :] + inverse * (
            ng - jnp.mean(ng, axis=1, keepdims=True) - n * jnp.mean(ng * n, axis=1, keepdims=True)
        )

    igrad_store = pltpu.make_async_copy(igrad_ref, igrad_hbm, local_sem.at[30])
    igrad_store.start()
    z_third(11)
    z_late(8)
    for n in range(5, 9):
        z_fourth(n)
    for n in range(9, 12):
        z_late(n)
    for n in range(9, 12):
        z_fourth(n)

    @pl.when(inner)
    def _():
        vec_second.wait_send()
        vec_third.wait_send()

    @pl.when(outer)
    def _():
        vec_first.wait_send()
        vec_third.wait_recv()

    block_store.wait()
    igrad_store.wait()
    for k in range(12):
        z_finish(k)
    for copy in pending:
        copy.wait_send()


def finish_kernel(*refs):
    vec_in, vec_refs, held, wide, in_sems, out_sems = (
        refs[6], refs[13:21], refs[21:27], refs[27:31], refs[31], refs[32],
    )
    pieces = []
    for n, parts in ((3, 1), (5, 4), (4, 4), (2, 4), (0, 1), (1, 1)):
        size = refs[n].shape[0] // parts
        for p in range(parts):
            rows = pl.ds(p * size, size)
            staged = wide[n - 2] if n >= 2 else held[n]
            pieces.append((
                n, rows,
                pltpu.make_async_copy(refs[n].at[rows], held[n].at[rows], in_sems.at[len(pieces)]),
                pltpu.make_async_copy(staged.at[rows], refs[7 + n].at[rows], out_sems.at[len(pieces)]),
            ))
    for piece in pieces:
        piece[2].start()
    for r, target in enumerate(vec_refs[:6]):
        target[...] = vec_in[max(r - 1, 0), :][:SHARD]
    rows = [vec_in[r : r + 1, :] for r in (5, 6, 7)]
    full = jnp.concatenate([pair_of(rows[0], rows[1]), rows[2]], axis=1)
    vec_refs[6][...] = full[:, : 3 * SHARD].reshape(3 * SHARD)
    vec_refs[7][...] = jnp.concatenate([vec_in[r : r + 1, :] for r in (8, 9, 10)], axis=1).reshape(4 * SHARD)
    for n, rows, arrives, leaves in pieces:
        arrives.wait()
        if n >= 2:
            wide[n - 2][rows, :] = held[n][rows, :].astype(jnp.float32)
        leaves.start()
    for piece in pieces:
        piece[3].wait()


def rope_tables(length):
    half_rot = ROT // 2
    lane = np.arange(128) % HD
    frequency = 10000.0 ** (-(lane % half_rot).astype(np.float64) * (2.0 / ROT))
    angles = np.arange(length, dtype=np.float64)[:, None] * frequency[None, :]
    turned = lane < ROT
    cos = np.where(turned, np.cos(angles), 1.0)
    lo = np.where(lane < half_rot, -np.sin(angles), 0.0)
    hi = np.where(turned & (lane >= half_rot), np.sin(angles), 0.0)
    return tuple(t.astype(np.float32) for t in (cos, lo, hi))


def local_fused(
    inputs, qkv_weight, qkv_bias, out_weight, out_bias, up_weight, up_bias, down_weight, down_bias,
    attn_gain, attn_shift, mlp_gain, mlp_shift, cotangent,
):
    f32, bf16 = jnp.float32, jnp.bfloat16
    length = 512
    def vmem(shape, dtype):
        return pltpu.VMEM(shape, dtype)

    inside = pl.BlockSpec(memory_space=pltpu.VMEM)
    anywhere = pl.BlockSpec(memory_space=pl.ANY)
    big = (length, D)
    outs = pl.pallas_call(
        block_kernel,
        out_shape=(
            jax.ShapeDtypeStruct((128, D), f32),
            jax.ShapeDtypeStruct((128, D), f32),
            jax.ShapeDtypeStruct((SHARD, 3 * D), bf16),
            jax.ShapeDtypeStruct((SHARD, D), bf16),
            jax.ShapeDtypeStruct((SHARD, 4 * D), bf16),
            jax.ShapeDtypeStruct((D, D), bf16),
            jax.ShapeDtypeStruct((16, 256), f32),
        ),
        in_specs=[inside] * 12 + [anywhere] * 5,
        out_specs=(anywhere,) * 6 + (inside,),
        scratch_shapes=[
            vmem((128, D), f32), vmem((128, D), f32),
            vmem((SHARD, 3 * D), bf16), vmem((SHARD, D), bf16), vmem((SHARD, 4 * D), bf16), vmem((D, D), bf16),
            vmem((128, D), f32), vmem((SHARD, 3 * D), bf16), vmem((D, D), bf16), vmem((SHARD, D), bf16),
            vmem((4, SHARD, 640), bf16), vmem((D, 640), bf16), vmem((D, D), bf16),
            vmem(big, bf16), vmem(big, bf16), vmem((4, 16, 256), f32), vmem((1, 640), f32), vmem((2, 48, D), bf16),
            vmem((2, 48, 640), bf16), vmem(big, f32), vmem(big, bf16),
            vmem(big, bf16),
            vmem(big, f32), vmem(big, f32), vmem(big, f32), vmem(big, bf16), vmem(big, bf16),
            vmem((length, 256), bf16), vmem((length, 256), bf16), vmem((length, 256), bf16),
            vmem((length, 256), bf16), vmem((length, 256), f32), vmem((length, 256), bf16),
            vmem((256, length), f32), vmem((256, length), f32), vmem((256, length), bf16),
            vmem((256, length), bf16), vmem((length, 256), f32), vmem((length, 256), f32),
            vmem((length, 256), f32), vmem((length, 640), bf16),
            vmem((384, D), f32), vmem((D, D), f32), vmem((length, 640), f32), vmem((SHARD, D), f32),
            vmem((864, D), bf16), vmem((864, D), bf16), vmem((8, ROWS, 640), bf16), vmem((8, ROWS, 640), bf16),
            vmem((4, ROWS, D), bf16), vmem((12, ROWS, D), bf16), vmem((12, ROWS, D), bf16),
            vmem((12, ROWS, D), bf16), vmem((12, ROWS, D), bf16),
            vmem(big, bf16), vmem((3, 128, D), bf16), vmem(big, bf16), vmem((3, 128, D), bf16),
            vmem((4, 8, 256), f32), vmem((3, 8, 256), f32), vmem((2, 16, 256), f32), vmem((4, 16, 256), f32),
            pltpu.SemaphoreType.DMA((NSEM,)), pltpu.SemaphoreType.DMA((NSEM,)), pltpu.SemaphoreType.DMA((31,)),
        ],
        compiler_params=pltpu.CompilerParams(
            collective_id=0, has_side_effects=True, vmem_limit_bytes=56 * 1024 * 1024
        ),
    )(
        inputs[0], qkv_bias, out_bias, down_bias, attn_gain, attn_shift, mlp_gain, mlp_shift, up_bias,
        *(jnp.asarray(t) for t in rope_tables(length)),
        cotangent[0], qkv_weight, up_weight, down_weight, out_weight,
    )
    widths = [SHARD] * 6 + [3 * SHARD, 4 * SHARD]
    (
        block_out, input_grad, gqkv, gout, gup, gdown,
        out_bias_sum, down_bias_sum, gain_attn, shift_attn, gain_mlp, shift_mlp, bqkv, bup,
    ) = pl.pallas_call(
        finish_kernel,
        out_shape=tuple(jax.ShapeDtypeStruct(t.shape, f32) for t in outs[:6])
        + tuple(jax.ShapeDtypeStruct((n,), f32) for n in widths),
        in_specs=[anywhere] * 6 + [inside],
        out_specs=(anywhere,) * 6 + (inside,) * 8,
        scratch_shapes=[vmem(t.shape, t.dtype) for t in outs[:6]]
        + [vmem(t.shape, f32) for t in outs[2:6]]
        + [pltpu.SemaphoreType.DMA((15,)), pltpu.SemaphoreType.DMA((15,))],
        compiler_params=pltpu.CompilerParams(vmem_limit_bytes=56 * 1024 * 1024),
    )(*outs)
    return (
        block_out[None], input_grad[None], gqkv, bqkv, gout, out_bias_sum, gup, bup, gdown, down_bias_sum,
        gain_attn, shift_attn, gain_mlp, shift_mlp,
    )


def solution(mesh):
    fused = (mesh.shape["grp"], mesh.shape["rep"]) == (4, 8)
    local = local_fused if fused else local_by_tokens
    placed = (
        P("rep", "grp", None),
        P("grp", None),
        P("grp"),
        P("grp", None),
        P("grp"),
        P("grp", None),
        P("grp"),
        P("grp", None),
        P("grp"),
        P("grp"),
        P("grp"),
        P("grp"),
        P("grp"),
        P("rep", "grp", None),
    )
    return jax.shard_map(
        local,
        mesh=mesh,
        in_specs=placed,
        out_specs=(
            P("rep", "grp", None),
            P("rep", "grp", None),
            P("grp", None),
            P("grp"),
            P("grp", None),
            P("grp"),
            P("grp", None),
            P("grp"),
            P("grp", None),
            P("grp"),
            P("grp"),
            P("grp"),
            P("grp"),
            P("grp"),
        ),
        check_vma=False,
    )
```

```python
import jax
import jax.numpy as jnp
import numpy as np
from jax import lax
from jax.experimental import pallas as pl
from jax.experimental.pallas import tpu as pltpu
from jax.sharding import PartitionSpec as P

D = 768
HEADS = 12
HD = 64
ROT = 16


eps = 1e-05


def layer_norm(values):
    centered = values - jnp.mean(values, axis=-1, keepdims=True)
    variance = jnp.mean(centered * centered, axis=-1, keepdims=True)
    inverse = lax.rsqrt(variance + eps)
    return (centered * inverse, inverse)


def gelu_parts(preact):
    normal_cdf = 0.5 * (1.0 + jax.scipy.special.erf(preact * 0.7071067811865476))
    density = jnp.exp(-0.5 * preact * preact) * 0.3989422804014327
    return (preact * normal_cdf, normal_cdf + preact * density)


def angle_tables(positions):
    half_rot = ROT // 2
    frequency = 10000.0 ** (-jnp.arange(half_rot, dtype=jnp.float32) * (2.0 / ROT))
    angles = positions.astype(jnp.float32)[:, None] * frequency[None, :]
    return (jnp.cos(angles)[:, None, :], jnp.sin(angles)[:, None, :])


def rotate(tensor, cos_table, sin_table):
    half_rot = ROT // 2
    lower_part = tensor[..., :half_rot]
    upper_part = tensor[..., half_rot:ROT]
    return jnp.concatenate(
        [
            lower_part * cos_table - upper_part * sin_table,
            upper_part * cos_table + lower_part * sin_table,
            tensor[..., ROT:],
        ],
        axis=-1,
    )


def unrotate(tensor, cos_table, sin_table):
    half_rot = ROT // 2
    lower_part = tensor[..., :half_rot]
    upper_part = tensor[..., half_rot:ROT]
    return jnp.concatenate(
        [
            lower_part * cos_table + upper_part * sin_table,
            upper_part * cos_table - lower_part * sin_table,
            tensor[..., ROT:],
        ],
        axis=-1,
    )


def local_by_tokens(
    inputs,
    qkv_weight,
    qkv_bias,
    out_weight,
    out_bias,
    up_weight,
    up_bias,
    down_weight,
    down_bias,
    attn_gain,
    attn_shift,
    mlp_gain,
    mlp_shift,
    cotangent,
):
    tokens = inputs.shape[1]
    (
        full_qkv,
        full_qkv_bias,
        full_out,
        full_out_bias,
        full_up,
        full_up_bias,
        full_down,
        full_down_bias,
        gain_attn,
        shift_attn,
        gain_mlp,
        shift_mlp,
    ) = (
        lax.all_gather(qkv_weight, "grp", axis=0, tiled=True),
        lax.all_gather(qkv_bias, "grp", axis=0, tiled=True),
        lax.all_gather(out_weight, "grp", axis=0, tiled=True),
        lax.all_gather(out_bias, "grp", axis=0, tiled=True),
        lax.all_gather(up_weight, "grp", axis=0, tiled=True),
        lax.all_gather(up_bias, "grp", axis=0, tiled=True),
        lax.all_gather(down_weight, "grp", axis=0, tiled=True),
        lax.all_gather(down_bias, "grp", axis=0, tiled=True),
        lax.all_gather(attn_gain, "grp", axis=0, tiled=True),
        lax.all_gather(attn_shift, "grp", axis=0, tiled=True),
        lax.all_gather(mlp_gain, "grp", axis=0, tiled=True),
        lax.all_gather(mlp_shift, "grp", axis=0, tiled=True),
    )
    first_row = lax.axis_index("grp") * tokens
    positions = first_row + jnp.arange(tokens, dtype=jnp.int32)
    cos_table, sin_table = angle_tables(positions)
    score_scale = HD ** (-0.5)
    hidden_in = inputs[0].astype(jnp.float32)
    normed, inverse = layer_norm(hidden_in)
    attn_in = (normed * gain_attn.astype(jnp.float32) + shift_attn.astype(jnp.float32)).astype(
        jnp.bfloat16
    )
    mlp_in = (normed * gain_mlp.astype(jnp.float32) + shift_mlp.astype(jnp.float32)).astype(
        jnp.bfloat16
    )
    qkv = jnp.dot(attn_in, full_qkv, preferred_element_type=jnp.float32) + full_qkv_bias.astype(
        jnp.float32
    )
    query_b = rotate(qkv[:, :D].reshape(tokens, HEADS, HD), cos_table, sin_table).astype(
        jnp.bfloat16
    )
    keys_local = (
        rotate(qkv[:, D : 2 * D].reshape(tokens, HEADS, HD), cos_table, sin_table)
        .astype(jnp.bfloat16)
        .reshape(tokens, D)
    )
    values_local = qkv[:, 2 * D :].astype(jnp.bfloat16)
    keys_all, values_all = (
        lax.all_gather(keys_local, "grp", axis=0, tiled=True),
        lax.all_gather(values_local, "grp", axis=0, tiled=True),
    )
    length = keys_all.shape[0]
    visible = jnp.arange(length, dtype=jnp.int32)[None, :] <= positions[:, None]
    query_heads = jnp.transpose(query_b, (1, 0, 2))
    key_heads = jnp.transpose(keys_all.reshape(length, HEADS, HD), (1, 0, 2))
    value_heads = jnp.transpose(values_all.reshape(length, HEADS, HD), (1, 0, 2))

    def forward_head(operands):
        query_one, key_one, value_one = operands
        scores = jnp.dot(query_one, key_one.T, preferred_element_type=jnp.float32) * score_scale
        scores = jnp.where(visible, scores, -jnp.inf)
        row_max = jnp.max(scores, axis=-1, keepdims=True)
        log_total = row_max + jnp.log(jnp.sum(jnp.exp(scores - row_max), axis=-1, keepdims=True))
        probs_b = jnp.exp(scores - log_total).astype(jnp.bfloat16)
        context_one = jnp.dot(probs_b, value_one, preferred_element_type=jnp.float32).astype(
            jnp.bfloat16
        )
        return (context_one, log_total)

    context_heads, log_totals = lax.map(forward_head, (query_heads, key_heads, value_heads))
    context = jnp.transpose(context_heads, (1, 0, 2)).reshape(tokens, D)
    attn_out = jnp.dot(
        context, full_out, preferred_element_type=jnp.float32
    ) + full_out_bias.astype(jnp.float32)
    preact = jnp.dot(mlp_in, full_up, preferred_element_type=jnp.float32) + full_up_bias.astype(
        jnp.float32
    )
    activation, slope = gelu_parts(preact)
    act_b = activation.astype(jnp.bfloat16)
    mlp_out = jnp.dot(act_b, full_down, preferred_element_type=jnp.float32) + full_down_bias.astype(
        jnp.float32
    )
    block_out = hidden_in + attn_out + mlp_out
    back_qkv, back_out, back_up, back_down, back_gain_attn, back_gain_mlp = (
        lax.all_gather(qkv_weight, "grp", axis=0, tiled=True),
        lax.all_gather(out_weight, "grp", axis=0, tiled=True),
        lax.all_gather(up_weight, "grp", axis=0, tiled=True),
        lax.all_gather(down_weight, "grp", axis=0, tiled=True),
        lax.all_gather(attn_gain, "grp", axis=0, tiled=True),
        lax.all_gather(mlp_gain, "grp", axis=0, tiled=True),
    )
    grad_out = cotangent[0]
    grad_b = grad_out.astype(jnp.bfloat16)
    down_grad = jnp.dot(act_b.T, grad_b, preferred_element_type=jnp.float32)
    out_grad = jnp.dot(context.T, grad_b, preferred_element_type=jnp.float32)
    bias_sum = jnp.sum(grad_out, axis=0)
    preact_grad = jnp.dot(grad_b, back_down.T, preferred_element_type=jnp.float32) * slope
    up_bias_grad = jnp.sum(preact_grad, axis=0)
    preact_b = preact_grad.astype(jnp.bfloat16)
    up_grad = jnp.dot(mlp_in.T, preact_b, preferred_element_type=jnp.float32)
    mlp_in_grad = jnp.dot(preact_b, back_up.T, preferred_element_type=jnp.float32)
    context_grad = jnp.dot(grad_b, back_out.T, preferred_element_type=jnp.float32).astype(
        jnp.bfloat16
    )
    context_grad_heads = jnp.transpose(context_grad.reshape(tokens, HEADS, HD), (1, 0, 2))

    def backward_head(operands):
        query_one, key_one, value_one, grad_one, log_total = operands
        scores = jnp.dot(query_one, key_one.T, preferred_element_type=jnp.float32) * score_scale
        scores = jnp.where(visible, scores, -jnp.inf)
        attn_probs = jnp.exp(scores - log_total)
        probs_b = attn_probs.astype(jnp.bfloat16)
        prob_grad = jnp.dot(grad_one, value_one.T, preferred_element_type=jnp.float32)
        row_dot = jnp.sum(attn_probs * prob_grad, axis=-1, keepdims=True)
        score_grad = (attn_probs * (prob_grad - row_dot) * score_scale).astype(jnp.bfloat16)
        query_grad = jnp.dot(score_grad, key_one, preferred_element_type=jnp.float32)
        key_grad = jnp.dot(score_grad.T, query_one, preferred_element_type=jnp.float32)
        value_grad = jnp.dot(probs_b.T, grad_one, preferred_element_type=jnp.float32)
        return (query_grad, key_grad, value_grad)

    query_grads, key_grads, value_grads = lax.map(
        backward_head, (query_heads, key_heads, value_heads, context_grad_heads, log_totals)
    )
    key_full = jnp.transpose(key_grads, (1, 0, 2)).reshape(length, D)
    value_full = jnp.transpose(value_grads, (1, 0, 2)).reshape(length, D)
    key_mine, value_mine = (
        lax.psum_scatter(key_full, "grp", scatter_dimension=0, tiled=True),
        lax.psum_scatter(value_full, "grp", scatter_dimension=0, tiled=True),
    )
    query_rows = unrotate(jnp.transpose(query_grads, (1, 0, 2)), cos_table, sin_table).reshape(
        tokens, D
    )
    key_rows = unrotate(key_mine.reshape(tokens, HEADS, HD), cos_table, sin_table).reshape(
        tokens, D
    )
    qkv_rows = jnp.concatenate([query_rows, key_rows, value_mine], axis=1)
    qkv_bias_grad = jnp.sum(qkv_rows, axis=0)
    qkv_rows_b = qkv_rows.astype(jnp.bfloat16)
    qkv_grad = jnp.dot(attn_in.T, qkv_rows_b, preferred_element_type=jnp.float32)
    attn_in_grad = jnp.dot(qkv_rows_b, back_qkv.T, preferred_element_type=jnp.float32)
    attn_gain_grad = jnp.sum(attn_in_grad * normed, axis=0)
    attn_shift_grad = jnp.sum(attn_in_grad, axis=0)
    mlp_gain_grad = jnp.sum(mlp_in_grad * normed, axis=0)
    mlp_shift_grad = jnp.sum(mlp_in_grad, axis=0)
    normed_grad = attn_in_grad * back_gain_attn.astype(
        jnp.float32
    ) + mlp_in_grad * back_gain_mlp.astype(jnp.float32)
    input_grad = grad_out + inverse * (
        normed_grad
        - jnp.mean(normed_grad, axis=-1, keepdims=True)
        - normed * jnp.mean(normed_grad * normed, axis=-1, keepdims=True)
    )
    group_parts = (
        lax.psum_scatter(qkv_grad, "grp", scatter_dimension=0, tiled=True),
        lax.psum_scatter(qkv_bias_grad, "grp", scatter_dimension=0, tiled=True),
        lax.psum_scatter(out_grad, "grp", scatter_dimension=0, tiled=True),
        lax.psum_scatter(bias_sum, "grp", scatter_dimension=0, tiled=True),
        lax.psum_scatter(up_grad, "grp", scatter_dimension=0, tiled=True),
        lax.psum_scatter(up_bias_grad, "grp", scatter_dimension=0, tiled=True),
        lax.psum_scatter(down_grad, "grp", scatter_dimension=0, tiled=True),
        lax.psum_scatter(attn_gain_grad, "grp", scatter_dimension=0, tiled=True),
        lax.psum_scatter(attn_shift_grad, "grp", scatter_dimension=0, tiled=True),
        lax.psum_scatter(mlp_gain_grad, "grp", scatter_dimension=0, tiled=True),
        lax.psum_scatter(mlp_shift_grad, "grp", scatter_dimension=0, tiled=True),
    )
    (
        qkv_part,
        qkv_bias_part,
        out_part,
        bias_part,
        up_part,
        up_bias_part,
        down_part,
        gain_attn_part,
        shift_attn_part,
        gain_mlp_part,
        shift_mlp_part,
    ) = group_parts
    (
        qkv_total,
        qkv_bias_total,
        out_total,
        bias_total,
        up_total,
        up_bias_total,
        down_total,
        gain_attn_total,
        shift_attn_total,
        gain_mlp_total,
        shift_mlp_total,
    ) = lax.psum(
        (
            qkv_part,
            qkv_bias_part,
            out_part,
            bias_part,
            up_part,
            up_bias_part,
            down_part,
            gain_attn_part,
            shift_attn_part,
            gain_mlp_part,
            shift_mlp_part,
        ),
        "rep",
    )
    return (
        block_out[None],
        input_grad[None],
        qkv_total,
        qkv_bias_total,
        out_total,
        bias_total,
        up_total,
        up_bias_total,
        down_total,
        bias_total,
        gain_attn_total,
        shift_attn_total,
        gain_mlp_total,
        shift_mlp_total,
    )


ROWS = 96
SHARD = 192
MESH = pl.DeviceIdType.MESH
NSEM = 128
UP, RL, UL, UM, RR, UR, RA, UA, US, UU, UN, UB, UC = 2, 16, 4, 1, 16, 4, 16, 4, 1, 4, 1, 4, 2


def mm(a, b):
    return lax.dot_general(a, b, (((1,), (0,)), ((), ())), preferred_element_type=jnp.float32)


def mm_tn(a, b):
    return lax.dot_general(a, b, (((0,), (0,)), ((), ())), preferred_element_type=jnp.float32)


def mm_nt(a, b):
    return lax.dot_general(a, b, (((1,), (1,)), ((), ())), preferred_element_type=jnp.float32)


def keep_192(t):
    lane = lax.broadcasted_iota(jnp.int32, t.shape, 1)
    return jnp.where(lane < SHARD, t, 0.0)


def block_of(t, j):
    base = (j // 2) * 384
    if j % 2 == 0:
        return keep_192(t[:, base : base + 256])
    return keep_192(pltpu.roll(t[:, base + 128 : base + 384], 192, 1))


def pair_of(a, b):
    shifted = pltpu.roll(b, 64, 1)
    return jnp.concatenate([a[:, :128], shifted[:, :128] + a[:, 128:], shifted[:, 128:]], axis=1)


def gelu_with_slope(preact):
    normal_cdf = 0.5 * (1.0 + lax.erf(preact * 0.7071067811865476))
    density = jnp.exp(-0.5 * preact * preact) * 0.3989422804014327
    return preact * normal_cdf, normal_cdf + preact * density


def block_kernel(
    x_ref, bqkv_ref, bout_ref, bdown_ref, ga_ref, sa_ref, gm_ref, sm_ref, bup_ref, cos_ref, sin_lo_ref, sin_hi_ref,
    ct_hbm, wqkv_hbm, wup_hbm, wdown_hbm, wout_hbm,
    block_hbm, igrad_hbm, qkv_hbm, out_hbm, up_hbm, down_hbm, vec_ref, block_ref, igrad_ref,
    gqkv_ref, gout_ref, gup_ref, gdown_ref,
    ct, w_qkv_in, w_down, w_out, w_pack, w_qkv, w_up,
    x_all, g_all, small_all, row640, up_way, qkv_way, normed, attn_in, mlp_in,
    acc_a, acc_b, acc_c, act_b, preact_b,
    q_b, k_b, v_b, cg_b, ctx_f, ctx_b, s_buf, dp_buf, p_b, ds_b, dq_f, dk_f, dv_f, rows_b,
    down_own, up_full, qkv_full, out_full,
    part_send, part_recv, tq_send, tq_recv, tu_send, chunk, z_in, z_sum, z_other,
    rs_out, rs_out_in, rs_in, rs_in_in,
    vec_send, vec_recv, vec_core, vec_z,
    send_sem, recv_sem, local_sem,
):
    f32, bf16 = jnp.float32, jnp.bfloat16
    me = lax.axis_index("grp")
    rep = lax.axis_index("rep")
    z, core = rep // 2, rep % 2
    mx, my = me % 2, me // 2
    inner = (z == 1) | (z == 2)
    outer = (z == 0) | (z == 3)
    peers = {1: my * 2 + (1 - mx), 2: (1 - my) * 2 + mx, 3: (1 - my) * 2 + (1 - mx)}
    twin = (me, z * 2 + (1 - core))
    z_pair = (me, (z + 1 - 2 * (z % 2)) * 2 + core)
    z_mid = (me, (3 - z) * 2 + core)

    def group(d):
        return (peers[d], rep)

    names = {}

    def over(count, step, unroll):
        def run(body):
            @pl.loop(0, count // step, unroll=unroll)
            def _(i):
                body(pl.multiple_of(i * step, step))

        return run

    def remote(name, src, dst, device):
        i = names.setdefault(name, len(names))
        assert i < NSEM
        return pltpu.make_async_remote_copy(
            src_ref=src, dst_ref=dst, send_sem=send_sem.at[i], recv_sem=recv_sem.at[i],
            device_id=device, device_id_type=MESH,
        )

    pending = []

    def send(name, src, dst, device):
        copy = remote(name, src, dst, device)
        copy.start()
        pending.append(copy)
        return copy

    def at(start, size, multiple=None):
        return pl.ds(pl.multiple_of(start, multiple or size), size)

    barrier = pltpu.get_barrier_semaphore()
    everyone = [group(d) for d in (1, 2, 3)] + [twin, z_pair]
    for device in everyone:
        pl.semaphore_signal(barrier, inc=1, device_id=device, device_id_type=MESH)

    @pl.when(inner)
    def _():
        pl.semaphore_signal(barrier, inc=1, device_id=z_mid, device_id_type=MESH)

    locals_ = [
        pltpu.make_async_copy(ct_hbm, ct, local_sem.at[0]),
        pltpu.make_async_copy(wqkv_hbm, w_qkv_in, local_sem.at[1]),
        pltpu.make_async_copy(wdown_hbm, w_down, local_sem.at[2]),
        pltpu.make_async_copy(wout_hbm, w_out, local_sem.at[3]),
        pltpu.make_async_copy(
            wup_hbm.at[:, at(me * D, D, 128)], w_up.at[at(me * SHARD, SHARD)], local_sem.at[4]
        ),
    ]
    for copy in locals_:
        copy.start()

    small_all[me] = jnp.zeros((16, 256), f32)
    row640[...] = jnp.zeros((1, 640), f32)
    row640[:, : 3 * SHARD] = bqkv_ref[...].astype(f32).reshape(1, 3 * SHARD)
    for r in range(3):
        small_all[me, r : r + 1, :] = block_of(row640[...], r)
    for r, ref in enumerate((bout_ref, bdown_ref, ga_ref, sa_ref, gm_ref, sm_ref)):
        small_all[me, 3 + r : 4 + r, 0:SHARD] = ref[...].astype(f32).reshape(1, SHARD)
    mine = at(me * 128, 128)
    x_all[mine, :] = x_ref[...]
    bias_up = bup_ref[...].astype(f32).reshape(1, D)
    pl.semaphore_wait(barrier, len(everyone) + inner.astype(jnp.int32))

    half = at(me * SHARD + core * ROWS, ROWS)
    small_in = {d: send(("small", d), small_all.at[me], small_all.at[me], group(d)) for d in (3, 1, 2)}

    def spread_rows(name, buffer):
        copies = {}
        for h in (0, 1):
            for d in (1, 2):
                part = h if d == 1 else 1 - h
                rows = at(me * 128 + part * 64, 64)
                copies[d, part] = send((name, d, part), buffer.at[rows], buffer.at[rows], group(d))
        return copies

    def forward_rows(name, buffer, copies):
        onward = []
        for d in (1, 2):
            part = d - 1
            copies[d, part].wait_recv()
            rows = at(peers[d] * 128 + part * 64, 64)
            onward.append(send((name, "on", part), buffer.at[rows], buffer.at[rows], group(3 - d)))
        return onward

    def spread_columns(name, source, way, buffer):
        copies = {}
        for d in (1, 2):
            part = d - 1
            copies["way", part] = send(
                (name, "way", part), source(3, core * ROWS + part * 48, 48), way.at[part], group(d)
            )
        for d in (1, 2):
            copies[d] = send((name, d), source(d, core * ROWS, ROWS), buffer.at[half], group(d))
        return copies

    def forward_columns(name, way, buffer, copies):
        onward = []
        for d in (1, 2):
            part = d - 1
            copies["way", part].wait_recv()
            rows = at(peers[d] * SHARD + core * ROWS + part * 48, 48)
            onward.append(send((name, "on", part), way.at[part], buffer.at[rows], group(3 - d)))
        return onward

    def share_weight(name, buffer, copies, onward):
        twins = []
        for d in (1, 2, 3):
            if d == 3:
                for copy in onward:
                    copy.wait_recv()
            else:
                copies[d].wait_recv()
            rows = at(peers[d] * SHARD + core * ROWS, ROWS)
            twins.append(send((name, "twin", d), buffer.at[rows], buffer.at[rows], twin))
        return twins

    def up_source(d, start, size):
        return wup_hbm.at[at(start, size, 16), at(peers[d] * D, D, 128)]

    def qkv_source(d, start, size):
        return w_pack.at[peers[d], at(start, size, 16)]

    x_in = spread_rows("x", x_all)
    up_in = spread_columns("up", up_source, up_way, w_up)
    locals_[0].wait()
    g_all[mine, :] = ct[...].astype(bf16)

    for d in (1, 2, 3):
        small_in[d].wait_recv()

    def vector(r):
        rows = [small_all[i, r : r + 1] for i in range(4)]
        return jnp.concatenate([pair_of(rows[0], rows[1]), pair_of(rows[2], rows[3])], axis=1)

    gain_attn, shift_attn, gain_mlp, shift_mlp = vector(5), vector(6), vector(7), vector(8)
    bias = vector(3) + vector(4)
    bias_qkv = jnp.zeros((1, 640), f32)
    for j in range(4):
        a, b, c = (
            small_all[(4 * t + j) // 3, (4 * t + j) % 3 : (4 * t + j) % 3 + 1] for t in range(3)
        )
        bias_qkv = jnp.where(me == j, jnp.concatenate([pair_of(a, b), c], axis=1), bias_qkv)

    def norm_rows(start):
        @over(128, RL, UL)
        def _(i):
            rows = pl.ds(pl.multiple_of(start + i, RL), RL)
            t = x_all[rows, :].astype(f32)
            centered = t - jnp.mean(t, axis=1, keepdims=True)
            inverse = lax.rsqrt(jnp.mean(centered * centered, axis=1, keepdims=True) + eps)
            n = centered * inverse
            normed[rows, :] = n
            attn_in[rows, :] = (n * gain_attn + shift_attn).astype(bf16)
            mlp_in[rows, :] = (n * gain_mlp + shift_mlp).astype(bf16)

    norm_rows(me * 128)
    x_on = forward_rows("x", x_all, x_in)
    g_in = spread_rows("g", g_all)
    for d in (1, 2):
        x_in[d, 2 - d].wait_recv()
        norm_rows(peers[d] * 128)
    up_on = forward_columns("up", up_way, w_up, up_in)
    locals_[1].wait()

    @over(SHARD, 32, UP)
    def _(start):
        rows = pl.ds(start, 32)
        wide = w_qkv_in[rows, :].astype(f32)
        for j in range(4):
            a, b, c = (block_of(wide[:, t * D : (t + 1) * D], j) for t in range(3))
            w_pack[j, rows, :] = jnp.concatenate([pair_of(a, b), c], axis=1).astype(bf16)

    w_qkv[at(me * SHARD, SHARD), :] = w_pack[me]
    for copy in x_on:
        copy.wait_recv()
    norm_rows(peers[3] * 128)

    up_twins = share_weight("up", w_up, up_in, up_on)
    g_on = forward_rows("g", g_all, g_in)
    qkv_in = spread_columns("qkv", qkv_source, qkv_way, w_qkv)
    locals_[4].wait()
    for copy in up_twins:
        copy.wait_recv()

    acc_a[...] = mm(mlp_in[...], w_up[...])

    @over(512, 16, UM)
    def _(start):
        rows = pl.ds(start, 16)
        activation, slope = gelu_with_slope(acc_a[rows, :] + bias_up)
        act_b[rows, :] = activation.astype(bf16)
        acc_a[rows, :] = slope

    locals_[2].wait()
    locals_[3].wait()
    acc_b[...] = mm(act_b[...], w_down[...])

    def total_of(refs, k, which):
        gqkv, gout, gup, gdown = refs
        if k < 4:
            return gdown.at[at(which * 384 + k * ROWS, ROWS)]
        if k < 8:
            return gup.at[at(which * ROWS, ROWS), (k - 4) * D : (k - 3) * D]
        if k == 8:
            return gout.at[at(which * ROWS, ROWS)]
        return gqkv.at[at(which * ROWS, ROWS), (k - 9) * D : (k - 8) * D]

    def total_ref(k, which):
        return total_of((gqkv_ref, gout_ref, gup_ref, gdown_ref), k, which)

    def store_total(k, which, i):
        return pltpu.make_async_copy(
            total_ref(k, which),
            total_of((qkv_hbm, out_hbm, up_hbm, down_hbm), k, which),
            local_sem.at[5 + 2 * k + i],
        )

    def z_first(k):
        @pl.when(outer)
        def _():
            remote(("z1", k), chunk.at[k], z_in.at[k], z_pair).start()

    def z_second(k):
        @pl.when(inner)
        def _():
            remote(("z1", k), chunk.at[k], z_in.at[k], z_pair).wait_recv()
            z_sum[k] = (chunk[k].astype(f32) + z_in[k].astype(f32)).astype(bf16)
            remote(("z2", k), z_sum.at[k], z_other.at[k], z_mid).start()

    def hand_over(k):
        own = total_ref(k, core)
        remote(("last", k), own, own, twin).start()
        store_total(k, core, 0).start()

    def z_third(k):
        @pl.when(inner)
        def _():
            own = total_ref(k, core)
            remote(("z2", k), z_sum.at[k], z_other.at[k], z_mid).wait_recv()
            own[...] = (z_sum[k].astype(f32) + z_other[k].astype(f32)).astype(bf16)
            remote(("z3", k), own, own, z_pair).start()
            hand_over(k)

    def z_late(k):
        @pl.when(outer)
        def _():
            own = total_ref(k, core)
            remote(("z3", k), own, own, z_pair).wait_recv()
            hand_over(k)

    def z_fourth(k):
        remote(("last", k), total_ref(k, 1 - core), total_ref(k, 1 - core), twin).wait_recv()
        store_total(k, 1 - core, 1).start()

    def z_finish(k):
        own = total_ref(k, core)
        last = remote(("last", k), own, own, twin)
        last.wait_send()
        store_total(k, core, 0).wait()
        store_total(k, 1 - core, 1).wait()

        @pl.when(inner)
        def _():
            remote(("z2", k), z_sum.at[k], z_other.at[k], z_mid).wait_send()
            remote(("z3", k), own, own, z_pair).wait_send()

        @pl.when(outer)
        def _():
            remote(("z1", k), chunk.at[k], z_in.at[k], z_pair).wait_send()

    for d in (1, 2):
        g_in[d, 2 - d].wait_recv()
    for copy in g_on:
        copy.wait_recv()
    g = g_all[...]
    other_cols = at((1 - core) * 384, 384)
    own_cols = at(core * 384, 384)

    part_send[0:384, :] = mm_tn(act_b[:, other_cols], g).astype(bf16)
    down_part = send("part_down", part_send.at[0:384], part_recv.at[0:384], twin)
    down_own[...] = mm_tn(act_b[:, own_cols], g)
    acc_c[...] = mm_nt(g, w_down[...])
    down_part.wait_recv()
    for k in range(4):
        rows = pl.ds(k * ROWS, ROWS)
        chunk[k] = (down_own[rows, :] + part_recv[rows, :].astype(f32)).astype(bf16)
        z_first(k)


    def slope_rows(i, total):
        rows = at(i * 16, 16)
        pg = acc_c[rows, :] * acc_a[rows, :]
        preact_b[rows, :] = pg.astype(bf16)
        return total + pg[:8] + pg[8:]

    up_bias_part = lax.fori_loop(0, 512 // 16, slope_rows, jnp.zeros((8, D), f32), unroll=US)
    up_bias_part = jnp.sum(up_bias_part, axis=0, keepdims=True)

    up_full[...] = mm_tn(mlp_in[...], preact_b[...])
    for j in range(4):
        part_send[384 + j * ROWS : 384 + (j + 1) * ROWS, :] = up_full[
            at(j * SHARD + (1 - core) * ROWS, ROWS), :
        ].astype(bf16)
    up_part = send("part_up", part_send.at[384:768], part_recv.at[384:768], twin)

    acc_c[...] = mm_nt(preact_b[...], w_up[...])
    cg_b[...] = jnp.zeros_like(cg_b)
    cg_b[:, :SHARD] = mm_nt(g, w_out[...]).astype(bf16)

    up_part.wait_recv()
    for j in range(4):
        tu_send[j] = (
            up_full[at(j * SHARD + core * ROWS, ROWS), :]
            + part_recv[384 + j * ROWS : 384 + (j + 1) * ROWS, :].astype(f32)
        ).astype(bf16)
    chunk[4 + me] = tu_send[me]
    tu_in = {d: send(("tu", d), tu_send.at[peers[d]], chunk.at[4 + me], group(d)) for d in (3, 1, 2)}

    z_second(0)
    qkv_on = forward_columns("qkv", qkv_way, w_qkv, qkv_in)
    qkv_twins = share_weight("qkv", w_qkv, qkv_in, qkv_on)
    for copy in qkv_twins:
        copy.wait_recv()
    qkv_full[...] = mm(attn_in[...], w_qkv[...])
    z_second(1)

    def turn(t, cos, lo, hi):
        return t * cos + pltpu.roll(t, 376, 1) * lo + pltpu.roll(t, 8, 1) * hi

    def tables(rows):
        return tuple(
            jnp.concatenate([ref[rows, :]] * 3, axis=1) for ref in (cos_ref, sin_lo_ref, sin_hi_ref)
        )

    @over(512, RR, UR)
    def _(start):
        rows = pl.ds(start, RR)
        t = qkv_full[rows, :] + bias_qkv
        cos, lo, hi = tables(rows)
        qk = turn(t[:, :384], cos, lo, hi)
        q_b[rows, :] = (keep_192(qk[:, :256]) * 0.125).astype(bf16)
        k_b[rows, :] = keep_192(pltpu.roll(qk[:, 128:384], 192, 1)).astype(bf16)
        v_b[rows, :] = keep_192(t[:, 384:640]).astype(bf16)

    ctx_f[...] = jnp.zeros_like(ctx_f)
    dq_f[...] = jnp.zeros_like(dq_f)
    dk_f[...] = jnp.zeros_like(dk_f)
    dv_f[...] = jnp.zeros_like(dv_f)
    lane256 = lax.broadcasted_iota(jnp.int32, (1, 256), 1)
    for h in range(3):
        mask = ((lane256 >= h * 64) & (lane256 < (h + 1) * 64)).astype(bf16)
        for block in range(2):
            keys = (block + 1) * 256
            rows_q = slice(block * 256, (block + 1) * 256)
            q_h = q_b[rows_q, :] * mask
            cg_h = cg_b[rows_q, :] * mask
            s_buf[:, :keys] = mm_nt(q_h, k_b[:keys, :])
            dp_buf[:, :keys] = mm_nt(cg_h, v_b[:keys, :])

            @over(256, RA, UA)
            def _(start, keys=keys, block=block):
                rows = pl.ds(start, RA)
                s = s_buf[rows, :keys]
                key_at = lax.broadcasted_iota(jnp.int32, (RA, keys), 1)
                query_at = lax.broadcasted_iota(jnp.int32, (RA, keys), 0) + (block * 256 + start)
                s = jnp.where(key_at <= query_at, s, -jnp.inf)
                e = jnp.exp(s - jnp.max(s, axis=1, keepdims=True))
                dp = dp_buf[rows, :keys]
                share = 1.0 / jnp.sum(e, axis=1, keepdims=True)
                row_dot = jnp.sum(e * dp, axis=1, keepdims=True) * share
                p = e * share
                p_b[rows, :keys] = p.astype(bf16)
                ds_b[rows, :keys] = (p * (dp - row_dot)).astype(bf16)

            ctx_f[rows_q, :] += mm(p_b[:, :keys], v_b[:keys, :] * mask)
            dq_f[rows_q, :] += mm(ds_b[:, :keys], k_b[:keys, :] * mask)
            dk_f[:keys, :] += mm_tn(ds_b[:, :keys], q_h)
            dv_f[:keys, :] += mm_tn(p_b[:, :keys], cg_h)
            if (h, block) == (0, 0):
                z_second(2)
                z_third(0)
            elif (h, block) == (0, 1):
                for d in (1, 2, 3):
                    tu_in[d].wait_recv()
                for k in range(4, 8):
                    z_first(k)
                z_third(1)
            elif (h, block) == (1, 0):
                z_second(3)
            elif (h, block) == (1, 1):
                z_third(2)
            elif (h, block) == (2, 0):
                z_second(4)
            elif (h, block) == (2, 1):
                z_third(3)

    ctx_b[...] = ctx_f[...].astype(bf16)
    out_full[...] = mm_tn(ctx_b[:, :SHARD], g)
    part_send[768 : 768 + ROWS, :] = out_full[at((1 - core) * ROWS, ROWS), :].astype(bf16)
    out_part = send("part_out", part_send.at[768:864], part_recv.at[768:864], twin)


    z_second(5)

    def unturn_rows(i, totals):
        rows = at(i * 16, 16)
        cos, lo, hi = tables(rows)
        qk = pair_of(dq_f[rows, :] * 0.125, dk_f[rows, :])
        qk = turn(qk, cos, -lo, -hi)
        full = jnp.concatenate([qk, dv_f[rows, :]], axis=1)
        rows_b[rows, :] = full.astype(bf16)
        return totals + full[:8] + full[8:]

    qkv_bias_part = lax.fori_loop(0, 512 // 16, unturn_rows, jnp.zeros((8, 640), f32), unroll=UU)
    qkv_bias_part = jnp.sum(qkv_bias_part, axis=0, keepdims=True)

    up_full[:, :640] = mm_tn(attn_in[...], rows_b[...])
    for j in range(4):
        tq_send[4 + j] = up_full[at(j * SHARD + (1 - core) * ROWS, ROWS), :640].astype(bf16)
    qkv_part = send("part_qkv", tq_send.at[4:8], tq_recv.at[4:8], twin)
    z_third(4)
    out_part.wait_recv()
    chunk[8] = (out_full[at(core * ROWS, ROWS), :] + part_recv[768:864, :].astype(f32)).astype(bf16)
    z_first(8)
    qkv_part.wait_recv()
    for j in range(4):
        tq_send[j] = (
            up_full[at(j * SHARD + core * ROWS, ROWS), :640] + tq_recv[4 + j].astype(f32)
        ).astype(bf16)
    tq_recv[me] = tq_send[me]
    tq_in = {d: send(("tq", d), tq_send.at[peers[d]], tq_recv.at[me], group(d)) for d in (3, 1, 2)}

    z_second(6)
    acc_b_in = mm_nt(rows_b[...], w_qkv[...])
    up_full[0:512, :] = acc_b_in

    def norm_grad_rows(i, totals):
        rows = at(i * 16, 16)
        ag, mg, n = up_full[rows, :], acc_c[rows, :], normed[rows, :]
        both = ag * gain_attn + mg * gain_mlp
        acc_c[rows, :] = both
        rs_in[rows, :] = both.astype(bf16)
        new = (ag * n, ag, mg * n, mg)
        return tuple(t + v[:8] + v[8:] for t, v in zip(totals, new))

    sums = lax.fori_loop(0, 512 // 16, norm_grad_rows, (jnp.zeros((8, D), f32),) * 4, unroll=UN)

    z_third(5)
    z_second(7)

    def rows_sum(t):
        return jnp.sum(t, axis=0, keepdims=True)

    wide = jnp.concatenate(
        [rows_sum(ct[...])] + [rows_sum(t) for t in sums] + [jnp.zeros((3, D), f32)], axis=0
    )
    types = [
        keep_192(qkv_bias_part[:, :256]),
        keep_192(pltpu.roll(qkv_bias_part[:, 128:384], 192, 1)),
        keep_192(qkv_bias_part[:, 384:640]),
    ]
    for j in range(4):
        vec_send[j] = block_of(wide, j)
        for t in range(3):
            b = 3 * j + t
            vec_send[j, 5 + t : 6 + t, :] = jnp.where(me == b % 4, types[b // 4], 0.0)
    vec_in = {d: send(("vec", d), vec_send.at[peers[d]], vec_recv.at[d - 1], group(d)) for d in (3, 1, 2)}
    acc_b[...] += mm(ctx_b[:, :SHARD], w_out[...])
    rs_out[...] = acc_b[...].astype(bf16)
    z_third(6)

    for d in (1, 2, 3):
        tq_in[d].wait_recv()

    @over(ROWS, 16, UC)
    def _(start):
        rows = pl.ds(start, 16)
        parts = [tq_recv[j, rows, :].astype(f32) for j in range(4)]
        for t in range(3):
            if t == 0:
                blocks = [keep_192(v[:, :256]) for v in parts]
            elif t == 1:
                blocks = [keep_192(pltpu.roll(v[:, 128:384], 192, 1)) for v in parts]
            else:
                blocks = [keep_192(v[:, 384:640]) for v in parts]
            chunk[9 + t, rows, :] = jnp.concatenate(
                [pair_of(blocks[0], blocks[1]), pair_of(blocks[2], blocks[3])], axis=1
            ).astype(bf16)

    for k in range(9, 12):
        z_first(k)
    out_in = {
        d: send(("rs_out", d), rs_out.at[at(peers[d] * 128, 128)], rs_out_in.at[d - 1], group(d))
        for d in (3, 1, 2)
    }
    in_in = {
        d: send(("rs_in", d), rs_in.at[at(peers[d] * 128, 128)], rs_in_in.at[d - 1], group(d))
        for d in (3, 1, 2)
    }
    z_second(8)
    z_third(7)
    for n in range(5):
        z_late(n)


    for d in (1, 2, 3):
        vec_in[d].wait_recv()
    vec_core[core, 0:8, :] = vec_send[me] + (vec_recv[0] + vec_recv[1] + vec_recv[2])
    vec_core[core, 8:16, :] = jnp.concatenate(
        [up_bias_part[:, t * 256 : (t + 1) * 256] for t in range(3)] + [jnp.zeros((5, 256), f32)], axis=0
    )
    vec_twin = send("vec_twin", vec_core.at[core], vec_core.at[core], twin)
    z_second(9)
    z_third(8)
    vec_twin.wait_recv()
    vec_z[0] = vec_core[0] + vec_core[1]
    vec_first = remote("vec_z1", vec_z.at[0], vec_z.at[1], z_pair)
    vec_second = remote("vec_z2", vec_z.at[2], vec_z.at[3], z_mid)
    vec_third = remote("vec_z3", vec_ref, vec_ref, z_pair)

    @pl.when(outer)
    def _():
        vec_first.start()

    z_second(10)
    for n in range(5):
        z_fourth(n)
    z_third(9)

    @pl.when(inner)
    def _():
        vec_first.wait_recv()
        vec_z[2] = vec_z[0] + vec_z[1]
        vec_second.start()

    z_second(11)
    for n in range(5, 8):
        z_late(n)
    z_third(10)

    @pl.when(inner)
    def _():
        vec_second.wait_recv()
        vec_ref[...] = vec_z[2] + vec_z[3]
        vec_third.start()

    for d in (1, 2, 3):
        out_in[d].wait_recv()

    @over(128, 16, UB)
    def _(start):
        rows = pl.ds(start, 16)
        total = acc_b[pl.ds(pl.multiple_of(me * 128 + start, 16), 16), :]
        for d in range(3):
            total = total + rs_out_in[d, rows, :].astype(f32)
        block_ref[rows, :] = x_ref[rows, :].astype(f32) + bias + total


    block_store = pltpu.make_async_copy(block_ref, block_hbm, local_sem.at[29])
    block_store.start()
    for d in (1, 2, 3):
        in_in[d].wait_recv()

    @over(128, 16, UB)
    def _(start):
        rows = pl.ds(start, 16)
        my_rows = pl.ds(pl.multiple_of(me * 128 + start, 16), 16)
        ng = acc_c[my_rows, :]
        for d in range(3):
            ng = ng + rs_in_in[d, rows, :].astype(f32)
        t = x_ref[rows, :].astype(f32)
        centered = t - jnp.mean(t, axis=1, keepdims=True)
        inverse = lax.rsqrt(jnp.mean(centered * centered, axis=1, keepdims=True) + eps)
        n = normed[my_rows, :]
        igrad_ref[rows, :] = ct[rows, :] + inverse * (
            ng - jnp.mean(ng, axis=1, keepdims=True) - n * jnp.mean(ng * n, axis=1, keepdims=True)
        )

    igrad_store = pltpu.make_async_copy(igrad_ref, igrad_hbm, local_sem.at[30])
    igrad_store.start()
    z_third(11)
    z_late(8)
    for n in range(5, 9):
        z_fourth(n)
    for n in range(9, 12):
        z_late(n)
    for n in range(9, 12):
        z_fourth(n)

    @pl.when(inner)
    def _():
        vec_second.wait_send()
        vec_third.wait_send()

    @pl.when(outer)
    def _():
        vec_first.wait_send()
        vec_third.wait_recv()

    block_store.wait()
    igrad_store.wait()
    for k in range(12):
        z_finish(k)
    for copy in pending:
        copy.wait_send()


def finish_kernel(*refs):
    vec_in, vec_refs, held, wide, in_sems, out_sems = (
        refs[6], refs[13:21], refs[21:27], refs[27:31], refs[31], refs[32],
    )
    pieces = []
    for n, parts in ((3, 1), (5, 4), (4, 4), (2, 4), (0, 1), (1, 1)):
        size = refs[n].shape[0] // parts
        for p in range(parts):
            rows = pl.ds(p * size, size)
            staged = wide[n - 2] if n >= 2 else held[n]
            pieces.append((
                n, rows,
                pltpu.make_async_copy(refs[n].at[rows], held[n].at[rows], in_sems.at[len(pieces)]),
                pltpu.make_async_copy(staged.at[rows], refs[7 + n].at[rows], out_sems.at[len(pieces)]),
            ))
    for piece in pieces:
        piece[2].start()
    for r, target in enumerate(vec_refs[:6]):
        target[...] = vec_in[max(r - 1, 0), :][:SHARD]
    rows = [vec_in[r : r + 1, :] for r in (5, 6, 7)]
    full = jnp.concatenate([pair_of(rows[0], rows[1]), rows[2]], axis=1)
    vec_refs[6][...] = full[:, : 3 * SHARD].reshape(3 * SHARD)
    vec_refs[7][...] = jnp.concatenate([vec_in[r : r + 1, :] for r in (8, 9, 10)], axis=1).reshape(4 * SHARD)
    for n, rows, arrives, leaves in pieces:
        arrives.wait()
        if n >= 2:
            wide[n - 2][rows, :] = held[n][rows, :].astype(jnp.float32)
        leaves.start()
    for piece in pieces:
        piece[3].wait()


def rope_tables(length):
    half_rot = ROT // 2
    lane = np.arange(128) % HD
    frequency = 10000.0 ** (-(lane % half_rot).astype(np.float64) * (2.0 / ROT))
    angles = np.arange(length, dtype=np.float64)[:, None] * frequency[None, :]
    turned = lane < ROT
    cos = np.where(turned, np.cos(angles), 1.0)
    lo = np.where(lane < half_rot, -np.sin(angles), 0.0)
    hi = np.where(turned & (lane >= half_rot), np.sin(angles), 0.0)
    return tuple(t.astype(np.float32) for t in (cos, lo, hi))


def local_fused(
    inputs, qkv_weight, qkv_bias, out_weight, out_bias, up_weight, up_bias, down_weight, down_bias,
    attn_gain, attn_shift, mlp_gain, mlp_shift, cotangent,
):
    f32, bf16 = jnp.float32, jnp.bfloat16
    length = 512
    def vmem(shape, dtype):
        return pltpu.VMEM(shape, dtype)

    inside = pl.BlockSpec(memory_space=pltpu.VMEM)
    anywhere = pl.BlockSpec(memory_space=pl.ANY)
    big = (length, D)
    outs = pl.pallas_call(
        block_kernel,
        out_shape=(
            jax.ShapeDtypeStruct((128, D), f32),
            jax.ShapeDtypeStruct((128, D), f32),
            jax.ShapeDtypeStruct((SHARD, 3 * D), bf16),
            jax.ShapeDtypeStruct((SHARD, D), bf16),
            jax.ShapeDtypeStruct((SHARD, 4 * D), bf16),
            jax.ShapeDtypeStruct((D, D), bf16),
            jax.ShapeDtypeStruct((16, 256), f32),
        ),
        in_specs=[inside] * 12 + [anywhere] * 5,
        out_specs=(anywhere,) * 6 + (inside,),
        scratch_shapes=[
            vmem((128, D), f32), vmem((128, D), f32),
            vmem((SHARD, 3 * D), bf16), vmem((SHARD, D), bf16), vmem((SHARD, 4 * D), bf16), vmem((D, D), bf16),
            vmem((128, D), f32), vmem((SHARD, 3 * D), bf16), vmem((D, D), bf16), vmem((SHARD, D), bf16),
            vmem((4, SHARD, 640), bf16), vmem((D, 640), bf16), vmem((D, D), bf16),
            vmem(big, bf16), vmem(big, bf16), vmem((4, 16, 256), f32), vmem((1, 640), f32), vmem((2, 48, D), bf16),
            vmem((2, 48, 640), bf16), vmem(big, f32), vmem(big, bf16),
            vmem(big, bf16),
            vmem(big, f32), vmem(big, f32), vmem(big, f32), vmem(big, bf16), vmem(big, bf16),
            vmem((length, 256), bf16), vmem((length, 256), bf16), vmem((length, 256), bf16),
            vmem((length, 256), bf16), vmem((length, 256), f32), vmem((length, 256), bf16),
            vmem((256, length), f32), vmem((256, length), f32), vmem((256, length), bf16),
            vmem((256, length), bf16), vmem((length, 256), f32), vmem((length, 256), f32),
            vmem((length, 256), f32), vmem((length, 640), bf16),
            vmem((384, D), f32), vmem((D, D), f32), vmem((length, 640), f32), vmem((SHARD, D), f32),
            vmem((864, D), bf16), vmem((864, D), bf16), vmem((8, ROWS, 640), bf16), vmem((8, ROWS, 640), bf16),
            vmem((4, ROWS, D), bf16), vmem((12, ROWS, D), bf16), vmem((12, ROWS, D), bf16),
            vmem((12, ROWS, D), bf16), vmem((12, ROWS, D), bf16),
            vmem(big, bf16), vmem((3, 128, D), bf16), vmem(big, bf16), vmem((3, 128, D), bf16),
            vmem((4, 8, 256), f32), vmem((3, 8, 256), f32), vmem((2, 16, 256), f32), vmem((4, 16, 256), f32),
            pltpu.SemaphoreType.DMA((NSEM,)), pltpu.SemaphoreType.DMA((NSEM,)), pltpu.SemaphoreType.DMA((31,)),
        ],
        compiler_params=pltpu.CompilerParams(
            collective_id=0, has_side_effects=True, vmem_limit_bytes=56 * 1024 * 1024
        ),
    )(
        inputs[0], qkv_bias, out_bias, down_bias, attn_gain, attn_shift, mlp_gain, mlp_shift, up_bias,
        *(jnp.asarray(t) for t in rope_tables(length)),
        cotangent[0], qkv_weight, up_weight, down_weight, out_weight,
    )
    widths = [SHARD] * 6 + [3 * SHARD, 4 * SHARD]
    (
        block_out, input_grad, gqkv, gout, gup, gdown,
        out_bias_sum, down_bias_sum, gain_attn, shift_attn, gain_mlp, shift_mlp, bqkv, bup,
    ) = pl.pallas_call(
        finish_kernel,
        out_shape=tuple(jax.ShapeDtypeStruct(t.shape, f32) for t in outs[:6])
        + tuple(jax.ShapeDtypeStruct((n,), f32) for n in widths),
        in_specs=[anywhere] * 6 + [inside],
        out_specs=(anywhere,) * 6 + (inside,) * 8,
        scratch_shapes=[vmem(t.shape, t.dtype) for t in outs[:6]]
        + [vmem(t.shape, f32) for t in outs[2:6]]
        + [pltpu.SemaphoreType.DMA((15,)), pltpu.SemaphoreType.DMA((15,))],
        compiler_params=pltpu.CompilerParams(vmem_limit_bytes=56 * 1024 * 1024),
    )(*outs)
    return (
        block_out[None], input_grad[None], gqkv, bqkv, gout, out_bias_sum, gup, bup, gdown, down_bias_sum,
        gain_attn, shift_attn, gain_mlp, shift_mlp,
    )


def solution(mesh):
    fused = (mesh.shape["grp"], mesh.shape["rep"]) == (4, 8)
    local = local_fused if fused else local_by_tokens
    placed = (
        P("rep", "grp", None),
        P("grp", None),
        P("grp"),
        P("grp", None),
        P("grp"),
        P("grp", None),
        P("grp"),
        P("grp", None),
        P("grp"),
        P("grp"),
        P("grp"),
        P("grp"),
        P("grp"),
        P("rep", "grp", None),
    )
    return jax.shard_map(
        local,
        mesh=mesh,
        in_specs=placed,
        out_specs=(
            P("rep", "grp", None),
            P("rep", "grp", None),
            P("grp", None),
            P("grp"),
            P("grp", None),
            P("grp"),
            P("grp", None),
            P("grp"),
            P("grp", None),
            P("grp"),
            P("grp"),
            P("grp"),
            P("grp"),
            P("grp"),
        ),
        check_vma=False,
    )
```

```python
import jax
import jax.numpy as jnp
import numpy as np
from jax import lax
from jax.experimental import pallas as pl
from jax.experimental.pallas import tpu as pltpu
from jax.sharding import PartitionSpec as P

D = 768
HEADS = 12
HD = 64
ROT = 16


eps = 1e-05


def layer_norm(values):
    centered = values - jnp.mean(values, axis=-1, keepdims=True)
    variance = jnp.mean(centered * centered, axis=-1, keepdims=True)
    inverse = lax.rsqrt(variance + eps)
    return (centered * inverse, inverse)


def gelu_parts(preact):
    normal_cdf = 0.5 * (1.0 + jax.scipy.special.erf(preact * 0.7071067811865476))
    density = jnp.exp(-0.5 * preact * preact) * 0.3989422804014327
    return (preact * normal_cdf, normal_cdf + preact * density)


def angle_tables(positions):
    half_rot = ROT // 2
    frequency = 10000.0 ** (-jnp.arange(half_rot, dtype=jnp.float32) * (2.0 / ROT))
    angles = positions.astype(jnp.float32)[:, None] * frequency[None, :]
    return (jnp.cos(angles)[:, None, :], jnp.sin(angles)[:, None, :])


def rotate(tensor, cos_table, sin_table):
    half_rot = ROT // 2
    lower_part = tensor[..., :half_rot]
    upper_part = tensor[..., half_rot:ROT]
    return jnp.concatenate(
        [
            lower_part * cos_table - upper_part * sin_table,
            upper_part * cos_table + lower_part * sin_table,
            tensor[..., ROT:],
        ],
        axis=-1,
    )


def unrotate(tensor, cos_table, sin_table):
    half_rot = ROT // 2
    lower_part = tensor[..., :half_rot]
    upper_part = tensor[..., half_rot:ROT]
    return jnp.concatenate(
        [
            lower_part * cos_table + upper_part * sin_table,
            upper_part * cos_table - lower_part * sin_table,
            tensor[..., ROT:],
        ],
        axis=-1,
    )


def local_by_tokens(
    inputs,
    qkv_weight,
    qkv_bias,
    out_weight,
    out_bias,
    up_weight,
    up_bias,
    down_weight,
    down_bias,
    attn_gain,
    attn_shift,
    mlp_gain,
    mlp_shift,
    cotangent,
):
    tokens = inputs.shape[1]
    (
        full_qkv,
        full_qkv_bias,
        full_out,
        full_out_bias,
        full_up,
        full_up_bias,
        full_down,
        full_down_bias,
        gain_attn,
        shift_attn,
        gain_mlp,
        shift_mlp,
    ) = (
        lax.all_gather(qkv_weight, "grp", axis=0, tiled=True),
        lax.all_gather(qkv_bias, "grp", axis=0, tiled=True),
        lax.all_gather(out_weight, "grp", axis=0, tiled=True),
        lax.all_gather(out_bias, "grp", axis=0, tiled=True),
        lax.all_gather(up_weight, "grp", axis=0, tiled=True),
        lax.all_gather(up_bias, "grp", axis=0, tiled=True),
        lax.all_gather(down_weight, "grp", axis=0, tiled=True),
        lax.all_gather(down_bias, "grp", axis=0, tiled=True),
        lax.all_gather(attn_gain, "grp", axis=0, tiled=True),
        lax.all_gather(attn_shift, "grp", axis=0, tiled=True),
        lax.all_gather(mlp_gain, "grp", axis=0, tiled=True),
        lax.all_gather(mlp_shift, "grp", axis=0, tiled=True),
    )
    first_row = lax.axis_index("grp") * tokens
    positions = first_row + jnp.arange(tokens, dtype=jnp.int32)
    cos_table, sin_table = angle_tables(positions)
    score_scale = HD ** (-0.5)
    hidden_in = inputs[0].astype(jnp.float32)
    normed, inverse = layer_norm(hidden_in)
    attn_in = (normed * gain_attn.astype(jnp.float32) + shift_attn.astype(jnp.float32)).astype(
        jnp.bfloat16
    )
    mlp_in = (normed * gain_mlp.astype(jnp.float32) + shift_mlp.astype(jnp.float32)).astype(
        jnp.bfloat16
    )
    qkv = jnp.dot(attn_in, full_qkv, preferred_element_type=jnp.float32) + full_qkv_bias.astype(
        jnp.float32
    )
    query_b = rotate(qkv[:, :D].reshape(tokens, HEADS, HD), cos_table, sin_table).astype(
        jnp.bfloat16
    )
    keys_local = (
        rotate(qkv[:, D : 2 * D].reshape(tokens, HEADS, HD), cos_table, sin_table)
        .astype(jnp.bfloat16)
        .reshape(tokens, D)
    )
    values_local = qkv[:, 2 * D :].astype(jnp.bfloat16)
    keys_all, values_all = (
        lax.all_gather(keys_local, "grp", axis=0, tiled=True),
        lax.all_gather(values_local, "grp", axis=0, tiled=True),
    )
    length = keys_all.shape[0]
    visible = jnp.arange(length, dtype=jnp.int32)[None, :] <= positions[:, None]
    query_heads = jnp.transpose(query_b, (1, 0, 2))
    key_heads = jnp.transpose(keys_all.reshape(length, HEADS, HD), (1, 0, 2))
    value_heads = jnp.transpose(values_all.reshape(length, HEADS, HD), (1, 0, 2))

    def forward_head(operands):
        query_one, key_one, value_one = operands
        scores = jnp.dot(query_one, key_one.T, preferred_element_type=jnp.float32) * score_scale
        scores = jnp.where(visible, scores, -jnp.inf)
        row_max = jnp.max(scores, axis=-1, keepdims=True)
        log_total = row_max + jnp.log(jnp.sum(jnp.exp(scores - row_max), axis=-1, keepdims=True))
        probs_b = jnp.exp(scores - log_total).astype(jnp.bfloat16)
        context_one = jnp.dot(probs_b, value_one, preferred_element_type=jnp.float32).astype(
            jnp.bfloat16
        )
        return (context_one, log_total)

    context_heads, log_totals = lax.map(forward_head, (query_heads, key_heads, value_heads))
    context = jnp.transpose(context_heads, (1, 0, 2)).reshape(tokens, D)
    attn_out = jnp.dot(
        context, full_out, preferred_element_type=jnp.float32
    ) + full_out_bias.astype(jnp.float32)
    preact = jnp.dot(mlp_in, full_up, preferred_element_type=jnp.float32) + full_up_bias.astype(
        jnp.float32
    )
    activation, slope = gelu_parts(preact)
    act_b = activation.astype(jnp.bfloat16)
    mlp_out = jnp.dot(act_b, full_down, preferred_element_type=jnp.float32) + full_down_bias.astype(
        jnp.float32
    )
    block_out = hidden_in + attn_out + mlp_out
    back_qkv, back_out, back_up, back_down, back_gain_attn, back_gain_mlp = (
        lax.all_gather(qkv_weight, "grp", axis=0, tiled=True),
        lax.all_gather(out_weight, "grp", axis=0, tiled=True),
        lax.all_gather(up_weight, "grp", axis=0, tiled=True),
        lax.all_gather(down_weight, "grp", axis=0, tiled=True),
        lax.all_gather(attn_gain, "grp", axis=0, tiled=True),
        lax.all_gather(mlp_gain, "grp", axis=0, tiled=True),
    )
    grad_out = cotangent[0]
    grad_b = grad_out.astype(jnp.bfloat16)
    down_grad = jnp.dot(act_b.T, grad_b, preferred_element_type=jnp.float32)
    out_grad = jnp.dot(context.T, grad_b, preferred_element_type=jnp.float32)
    bias_sum = jnp.sum(grad_out, axis=0)
    preact_grad = jnp.dot(grad_b, back_down.T, preferred_element_type=jnp.float32) * slope
    up_bias_grad = jnp.sum(preact_grad, axis=0)
    preact_b = preact_grad.astype(jnp.bfloat16)
    up_grad = jnp.dot(mlp_in.T, preact_b, preferred_element_type=jnp.float32)
    mlp_in_grad = jnp.dot(preact_b, back_up.T, preferred_element_type=jnp.float32)
    context_grad = jnp.dot(grad_b, back_out.T, preferred_element_type=jnp.float32).astype(
        jnp.bfloat16
    )
    context_grad_heads = jnp.transpose(context_grad.reshape(tokens, HEADS, HD), (1, 0, 2))

    def backward_head(operands):
        query_one, key_one, value_one, grad_one, log_total = operands
        scores = jnp.dot(query_one, key_one.T, preferred_element_type=jnp.float32) * score_scale
        scores = jnp.where(visible, scores, -jnp.inf)
        attn_probs = jnp.exp(scores - log_total)
        probs_b = attn_probs.astype(jnp.bfloat16)
        prob_grad = jnp.dot(grad_one, value_one.T, preferred_element_type=jnp.float32)
        row_dot = jnp.sum(attn_probs * prob_grad, axis=-1, keepdims=True)
        score_grad = (attn_probs * (prob_grad - row_dot) * score_scale).astype(jnp.bfloat16)
        query_grad = jnp.dot(score_grad, key_one, preferred_element_type=jnp.float32)
        key_grad = jnp.dot(score_grad.T, query_one, preferred_element_type=jnp.float32)
        value_grad = jnp.dot(probs_b.T, grad_one, preferred_element_type=jnp.float32)
        return (query_grad, key_grad, value_grad)

    query_grads, key_grads, value_grads = lax.map(
        backward_head, (query_heads, key_heads, value_heads, context_grad_heads, log_totals)
    )
    key_full = jnp.transpose(key_grads, (1, 0, 2)).reshape(length, D)
    value_full = jnp.transpose(value_grads, (1, 0, 2)).reshape(length, D)
    key_mine, value_mine = (
        lax.psum_scatter(key_full, "grp", scatter_dimension=0, tiled=True),
        lax.psum_scatter(value_full, "grp", scatter_dimension=0, tiled=True),
    )
    query_rows = unrotate(jnp.transpose(query_grads, (1, 0, 2)), cos_table, sin_table).reshape(
        tokens, D
    )
    key_rows = unrotate(key_mine.reshape(tokens, HEADS, HD), cos_table, sin_table).reshape(
        tokens, D
    )
    qkv_rows = jnp.concatenate([query_rows, key_rows, value_mine], axis=1)
    qkv_bias_grad = jnp.sum(qkv_rows, axis=0)
    qkv_rows_b = qkv_rows.astype(jnp.bfloat16)
    qkv_grad = jnp.dot(attn_in.T, qkv_rows_b, preferred_element_type=jnp.float32)
    attn_in_grad = jnp.dot(qkv_rows_b, back_qkv.T, preferred_element_type=jnp.float32)
    attn_gain_grad = jnp.sum(attn_in_grad * normed, axis=0)
    attn_shift_grad = jnp.sum(attn_in_grad, axis=0)
    mlp_gain_grad = jnp.sum(mlp_in_grad * normed, axis=0)
    mlp_shift_grad = jnp.sum(mlp_in_grad, axis=0)
    normed_grad = attn_in_grad * back_gain_attn.astype(
        jnp.float32
    ) + mlp_in_grad * back_gain_mlp.astype(jnp.float32)
    input_grad = grad_out + inverse * (
        normed_grad
        - jnp.mean(normed_grad, axis=-1, keepdims=True)
        - normed * jnp.mean(normed_grad * normed, axis=-1, keepdims=True)
    )
    group_parts = (
        lax.psum_scatter(qkv_grad, "grp", scatter_dimension=0, tiled=True),
        lax.psum_scatter(qkv_bias_grad, "grp", scatter_dimension=0, tiled=True),
        lax.psum_scatter(out_grad, "grp", scatter_dimension=0, tiled=True),
        lax.psum_scatter(bias_sum, "grp", scatter_dimension=0, tiled=True),
        lax.psum_scatter(up_grad, "grp", scatter_dimension=0, tiled=True),
        lax.psum_scatter(up_bias_grad, "grp", scatter_dimension=0, tiled=True),
        lax.psum_scatter(down_grad, "grp", scatter_dimension=0, tiled=True),
        lax.psum_scatter(attn_gain_grad, "grp", scatter_dimension=0, tiled=True),
        lax.psum_scatter(attn_shift_grad, "grp", scatter_dimension=0, tiled=True),
        lax.psum_scatter(mlp_gain_grad, "grp", scatter_dimension=0, tiled=True),
        lax.psum_scatter(mlp_shift_grad, "grp", scatter_dimension=0, tiled=True),
    )
    (
        qkv_part,
        qkv_bias_part,
        out_part,
        bias_part,
        up_part,
        up_bias_part,
        down_part,
        gain_attn_part,
        shift_attn_part,
        gain_mlp_part,
        shift_mlp_part,
    ) = group_parts
    (
        qkv_total,
        qkv_bias_total,
        out_total,
        bias_total,
        up_total,
        up_bias_total,
        down_total,
        gain_attn_total,
        shift_attn_total,
        gain_mlp_total,
        shift_mlp_total,
    ) = lax.psum(
        (
            qkv_part,
            qkv_bias_part,
            out_part,
            bias_part,
            up_part,
            up_bias_part,
            down_part,
            gain_attn_part,
            shift_attn_part,
            gain_mlp_part,
            shift_mlp_part,
        ),
        "rep",
    )
    return (
        block_out[None],
        input_grad[None],
        qkv_total,
        qkv_bias_total,
        out_total,
        bias_total,
        up_total,
        up_bias_total,
        down_total,
        bias_total,
        gain_attn_total,
        shift_attn_total,
        gain_mlp_total,
        shift_mlp_total,
    )


ROWS = 96
SHARD = 192
MESH = pl.DeviceIdType.MESH
NSEM = 128
UP, RL, UL, UM, RR, UR, RA, UA, US, UU, UN, UB, UC = 2, 16, 4, 1, 16, 4, 16, 4, 1, 4, 1, 4, 2


def mm(a, b):
    return lax.dot_general(a, b, (((1,), (0,)), ((), ())), preferred_element_type=jnp.float32)


def mm_tn(a, b):
    return lax.dot_general(a, b, (((0,), (0,)), ((), ())), preferred_element_type=jnp.float32)


def mm_nt(a, b):
    return lax.dot_general(a, b, (((1,), (1,)), ((), ())), preferred_element_type=jnp.float32)


def keep_192(t):
    lane = lax.broadcasted_iota(jnp.int32, t.shape, 1)
    return jnp.where(lane < SHARD, t, 0.0)


def block_of(t, j):
    base = (j // 2) * 384
    if j % 2 == 0:
        return keep_192(t[:, base : base + 256])
    return keep_192(pltpu.roll(t[:, base + 128 : base + 384], 192, 1))


def pair_of(a, b):
    shifted = pltpu.roll(b, 64, 1)
    return jnp.concatenate([a[:, :128], shifted[:, :128] + a[:, 128:], shifted[:, 128:]], axis=1)


def gelu_with_slope(preact):
    normal_cdf = 0.5 * (1.0 + lax.erf(preact * 0.7071067811865476))
    density = jnp.exp(-0.5 * preact * preact) * 0.3989422804014327
    return preact * normal_cdf, normal_cdf + preact * density


def block_kernel(
    x_ref, bqkv_ref, bout_ref, bdown_ref, ga_ref, sa_ref, gm_ref, sm_ref, bup_ref, cos_ref, sin_lo_ref, sin_hi_ref,
    ct_hbm, wqkv_hbm, wup_hbm, wdown_hbm, wout_hbm,
    block_hbm, igrad_hbm, qkv_hbm, out_hbm, up_hbm, down_hbm, vec_ref, block_ref, igrad_ref,
    gqkv_ref, gout_ref, gup_ref, gdown_ref,
    ct, w_qkv_in, w_down, w_out, w_pack, w_qkv, w_up,
    x_all, g_all, small_all, row640, up_way, qkv_way, normed, attn_in, mlp_in,
    acc_a, acc_b, acc_c, act_b, preact_b,
    q_b, k_b, v_b, cg_b, ctx_f, ctx_b, s_buf, dp_buf, p_b, ds_b, dq_f, dk_f, dv_f, rows_b,
    down_own, up_full, qkv_full, out_full,
    part_send, part_recv, tq_send, tq_recv, tu_send, chunk, z_in, z_sum, z_other,
    rs_out, rs_out_in, rs_in, rs_in_in,
    vec_send, vec_recv, vec_core, vec_z,
    send_sem, recv_sem, local_sem,
):
    f32, bf16 = jnp.float32, jnp.bfloat16
    me = lax.axis_index("grp")
    rep = lax.axis_index("rep")
    z, core = rep // 2, rep % 2
    mx, my = me % 2, me // 2
    inner = (z == 1) | (z == 2)
    outer = (z == 0) | (z == 3)
    peers = {1: my * 2 + (1 - mx), 2: (1 - my) * 2 + mx, 3: (1 - my) * 2 + (1 - mx)}
    twin = (me, z * 2 + (1 - core))
    z_pair = (me, (z + 1 - 2 * (z % 2)) * 2 + core)
    z_mid = (me, (3 - z) * 2 + core)

    def group(d):
        return (peers[d], rep)

    names = {}

    def over(count, step, unroll):
        def run(body):
            @pl.loop(0, count // step, unroll=unroll)
            def _(i):
                body(pl.multiple_of(i * step, step))

        return run

    def remote(name, src, dst, device):
        i = names.setdefault(name, len(names))
        assert i < NSEM
        return pltpu.make_async_remote_copy(
            src_ref=src, dst_ref=dst, send_sem=send_sem.at[i], recv_sem=recv_sem.at[i],
            device_id=device, device_id_type=MESH,
        )

    pending = []

    def send(name, src, dst, device):
        copy = remote(name, src, dst, device)
        copy.start()
        pending.append(copy)
        return copy

    def at(start, size, multiple=None):
        return pl.ds(pl.multiple_of(start, multiple or size), size)

    barrier = pltpu.get_barrier_semaphore()
    everyone = [group(d) for d in (1, 2, 3)] + [twin, z_pair]
    for device in everyone:
        pl.semaphore_signal(barrier, inc=1, device_id=device, device_id_type=MESH)

    @pl.when(inner)
    def _():
        pl.semaphore_signal(barrier, inc=1, device_id=z_mid, device_id_type=MESH)

    locals_ = [
        pltpu.make_async_copy(ct_hbm, ct, local_sem.at[0]),
        pltpu.make_async_copy(wqkv_hbm, w_qkv_in, local_sem.at[1]),
        pltpu.make_async_copy(wdown_hbm, w_down, local_sem.at[2]),
        pltpu.make_async_copy(wout_hbm, w_out, local_sem.at[3]),
        pltpu.make_async_copy(
            wup_hbm.at[:, at(me * D, D, 128)], w_up.at[at(me * SHARD, SHARD)], local_sem.at[4]
        ),
    ]
    for copy in locals_:
        copy.start()

    small_all[me] = jnp.zeros((16, 256), f32)
    row640[...] = jnp.zeros((1, 640), f32)
    row640[:, : 3 * SHARD] = bqkv_ref[...].astype(f32).reshape(1, 3 * SHARD)
    for r in range(3):
        small_all[me, r : r + 1, :] = block_of(row640[...], r)
    for r, ref in enumerate((bout_ref, bdown_ref, ga_ref, sa_ref, gm_ref, sm_ref)):
        small_all[me, 3 + r : 4 + r, 0:SHARD] = ref[...].astype(f32).reshape(1, SHARD)
    mine = at(me * 128, 128)
    x_all[mine, :] = x_ref[...]
    bias_up = bup_ref[...].astype(f32).reshape(1, D)
    pl.semaphore_wait(barrier, len(everyone) + inner.astype(jnp.int32))

    half = at(me * SHARD + core * ROWS, ROWS)
    small_in = {d: send(("small", d), small_all.at[me], small_all.at[me], group(d)) for d in (3, 1, 2)}

    def spread_rows(name, buffer):
        copies = {}
        for h in (0, 1):
            for d in (1, 2):
                part = h if d == 1 else 1 - h
                rows = at(me * 128 + part * 64, 64)
                copies[d, part] = send((name, d, part), buffer.at[rows], buffer.at[rows], group(d))
        return copies

    def forward_rows(name, buffer, copies):
        onward = []
        for d in (1, 2):
            part = d - 1
            copies[d, part].wait_recv()
            rows = at(peers[d] * 128 + part * 64, 64)
            onward.append(send((name, "on", part), buffer.at[rows], buffer.at[rows], group(3 - d)))
        return onward

    def spread_columns(name, source, way, buffer):
        copies = {}
        for d in (1, 2):
            part = d - 1
            copies["way", part] = send(
                (name, "way", part), source(3, core * ROWS + part * 48, 48), way.at[part], group(d)
            )
        for d in (1, 2):
            copies[d] = send((name, d), source(d, core * ROWS, ROWS), buffer.at[half], group(d))
        return copies

    def forward_columns(name, way, buffer, copies):
        onward = []
        for d in (1, 2):
            part = d - 1
            copies["way", part].wait_recv()
            rows = at(peers[d] * SHARD + core * ROWS + part * 48, 48)
            onward.append(send((name, "on", part), way.at[part], buffer.at[rows], group(3 - d)))
        return onward

    def share_weight(name, buffer, copies, onward):
        twins = []
        for d in (1, 2, 3):
            if d == 3:
                for copy in onward:
                    copy.wait_recv()
            else:
                copies[d].wait_recv()
            rows = at(peers[d] * SHARD + core * ROWS, ROWS)
            twins.append(send((name, "twin", d), buffer.at[rows], buffer.at[rows], twin))
        return twins

    def up_source(d, start, size):
        return wup_hbm.at[at(start, size, 16), at(peers[d] * D, D, 128)]

    def qkv_source(d, start, size):
        return w_pack.at[peers[d], at(start, size, 16)]

    x_in = spread_rows("x", x_all)
    up_in = spread_columns("up", up_source, up_way, w_up)
    locals_[0].wait()
    g_all[mine, :] = ct[...].astype(bf16)

    for d in (1, 2, 3):
        small_in[d].wait_recv()

    def vector(r):
        rows = [small_all[i, r : r + 1] for i in range(4)]
        return jnp.concatenate([pair_of(rows[0], rows[1]), pair_of(rows[2], rows[3])], axis=1)

    gain_attn, shift_attn, gain_mlp, shift_mlp = vector(5), vector(6), vector(7), vector(8)
    bias = vector(3) + vector(4)
    bias_qkv = jnp.zeros((1, 640), f32)
    for j in range(4):
        a, b, c = (
            small_all[(4 * t + j) // 3, (4 * t + j) % 3 : (4 * t + j) % 3 + 1] for t in range(3)
        )
        bias_qkv = jnp.where(me == j, jnp.concatenate([pair_of(a, b), c], axis=1), bias_qkv)

    def norm_rows(start):
        @over(128, RL, UL)
        def _(i):
            rows = pl.ds(pl.multiple_of(start + i, RL), RL)
            t = x_all[rows, :].astype(f32)
            centered = t - jnp.mean(t, axis=1, keepdims=True)
            inverse = lax.rsqrt(jnp.mean(centered * centered, axis=1, keepdims=True) + eps)
            n = centered * inverse
            normed[rows, :] = n
            attn_in[rows, :] = (n * gain_attn + shift_attn).astype(bf16)
            mlp_in[rows, :] = (n * gain_mlp + shift_mlp).astype(bf16)

    norm_rows(me * 128)
    x_on = forward_rows("x", x_all, x_in)
    g_in = spread_rows("g", g_all)
    for d in (1, 2):
        x_in[d, 2 - d].wait_recv()
        norm_rows(peers[d] * 128)
    up_on = forward_columns("up", up_way, w_up, up_in)
    locals_[1].wait()

    @over(SHARD, 32, UP)
    def _(start):
        rows = pl.ds(start, 32)
        wide = w_qkv_in[rows, :].astype(f32)
        for j in range(4):
            a, b, c = (block_of(wide[:, t * D : (t + 1) * D], j) for t in range(3))
            w_pack[j, rows, :] = jnp.concatenate([pair_of(a, b), c], axis=1).astype(bf16)

    w_qkv[at(me * SHARD, SHARD), :] = w_pack[me]
    for copy in x_on:
        copy.wait_recv()
    norm_rows(peers[3] * 128)

    up_twins = share_weight("up", w_up, up_in, up_on)
    g_on = forward_rows("g", g_all, g_in)
    qkv_in = spread_columns("qkv", qkv_source, qkv_way, w_qkv)
    locals_[4].wait()
    for copy in up_twins:
        copy.wait_recv()

    acc_a[...] = mm(mlp_in[...], w_up[...])

    @over(512, 16, UM)
    def _(start):
        rows = pl.ds(start, 16)
        activation, slope = gelu_with_slope(acc_a[rows, :] + bias_up)
        act_b[rows, :] = activation.astype(bf16)
        acc_a[rows, :] = slope

    locals_[2].wait()
    locals_[3].wait()
    acc_b[...] = mm(act_b[...], w_down[...])

    items = [(k, 0, ROWS) for k in range(11)] + [(11, 32 * t, 32) for t in range(3)]

    def rows_of(buffer, n):
        k, start, size = items[n]
        return buffer.at[k, pl.ds(start, size)]

    def total_of(refs, n, which):
        gqkv, gout, gup, gdown = refs
        k, start, size = items[n]
        rows = at(which * ROWS + start, size, 16)
        if k < 4:
            return gdown.at[at(which * 384 + k * ROWS, ROWS)]
        if k < 8:
            return gup.at[rows, (k - 4) * D : (k - 3) * D]
        if k == 8:
            return gout.at[rows]
        return gqkv.at[rows, (k - 9) * D : (k - 8) * D]

    def total_ref(n, which):
        return total_of((gqkv_ref, gout_ref, gup_ref, gdown_ref), n, which)

    def store_total(n, which, i):
        return pltpu.make_async_copy(
            total_ref(n, which),
            total_of((qkv_hbm, out_hbm, up_hbm, down_hbm), n, which),
            local_sem.at[5 + 2 * n + i],
        )

    def hop_1(n):
        return remote(("z1", n), rows_of(chunk, n), rows_of(z_in, n), z_pair)

    def hop_2(n):
        return remote(("z2", n), rows_of(z_sum, n), rows_of(z_other, n), z_mid)

    def hop_3(n):
        own = total_ref(n, core)
        return remote(("z3", n), own, own, z_pair)

    def z_first(n):
        @pl.when(outer)
        def _():
            hop_1(n).start()

    def z_second(n):
        @pl.when(inner)
        def _():
            hop_1(n).wait_recv()
            rows_of(z_sum, n)[...] = (
                rows_of(chunk, n)[...].astype(f32) + rows_of(z_in, n)[...].astype(f32)
            ).astype(bf16)
            hop_2(n).start()

    def hand_over(n):
        own = total_ref(n, core)
        remote(("last", n), own, own, twin).start()
        store_total(n, core, 0).start()

    def z_third(n):
        @pl.when(inner)
        def _():
            hop_2(n).wait_recv()
            total_ref(n, core)[...] = (
                rows_of(z_sum, n)[...].astype(f32) + rows_of(z_other, n)[...].astype(f32)
            ).astype(bf16)
            hop_3(n).start()
            hand_over(n)

    def z_late(n):
        @pl.when(outer)
        def _():
            hop_3(n).wait_recv()
            hand_over(n)

    def z_fourth(n):
        theirs = total_ref(n, 1 - core)
        remote(("last", n), theirs, theirs, twin).wait_recv()
        store_total(n, 1 - core, 1).start()

    def z_finish(n):
        own = total_ref(n, core)
        remote(("last", n), own, own, twin).wait_send()
        store_total(n, core, 0).wait()
        store_total(n, 1 - core, 1).wait()

        @pl.when(inner)
        def _():
            hop_2(n).wait_send()
            hop_3(n).wait_send()

        @pl.when(outer)
        def _():
            hop_1(n).wait_send()

    for d in (1, 2):
        g_in[d, 2 - d].wait_recv()
    for copy in g_on:
        copy.wait_recv()
    g = g_all[...]
    other_cols = at((1 - core) * 384, 384)
    own_cols = at(core * 384, 384)

    part_send[0:384, :] = mm_tn(act_b[:, other_cols], g).astype(bf16)
    down_part = send("part_down", part_send.at[0:384], part_recv.at[0:384], twin)
    down_own[...] = mm_tn(act_b[:, own_cols], g)
    acc_c[...] = mm_nt(g, w_down[...])
    down_part.wait_recv()
    for k in range(4):
        rows = pl.ds(k * ROWS, ROWS)
        chunk[k] = (down_own[rows, :] + part_recv[rows, :].astype(f32)).astype(bf16)
        z_first(k)


    def slope_rows(i, total):
        rows = at(i * 16, 16)
        pg = acc_c[rows, :] * acc_a[rows, :]
        preact_b[rows, :] = pg.astype(bf16)
        return total + pg[:8] + pg[8:]

    up_bias_part = lax.fori_loop(0, 512 // 16, slope_rows, jnp.zeros((8, D), f32), unroll=US)
    up_bias_part = jnp.sum(up_bias_part, axis=0, keepdims=True)

    up_full[...] = mm_tn(mlp_in[...], preact_b[...])
    for j in range(4):
        part_send[384 + j * ROWS : 384 + (j + 1) * ROWS, :] = up_full[
            at(j * SHARD + (1 - core) * ROWS, ROWS), :
        ].astype(bf16)
    up_part = send("part_up", part_send.at[384:768], part_recv.at[384:768], twin)

    cg_b[...] = jnp.zeros_like(cg_b)
    cg_b[:, :SHARD] = mm_nt(g, w_out[...]).astype(bf16)

    up_part.wait_recv()
    for j in range(4):
        tu_send[j] = (
            up_full[at(j * SHARD + core * ROWS, ROWS), :]
            + part_recv[384 + j * ROWS : 384 + (j + 1) * ROWS, :].astype(f32)
        ).astype(bf16)
    chunk[4 + me] = tu_send[me]
    tu_in = {d: send(("tu", d), tu_send.at[peers[d]], chunk.at[4 + me], group(d)) for d in (3, 1, 2)}

    z_second(0)
    qkv_on = forward_columns("qkv", qkv_way, w_qkv, qkv_in)
    qkv_twins = share_weight("qkv", w_qkv, qkv_in, qkv_on)
    for copy in qkv_twins:
        copy.wait_recv()
    qkv_full[...] = mm(attn_in[...], w_qkv[...])
    z_second(1)

    def turn(t, cos, lo, hi):
        return t * cos + pltpu.roll(t, 376, 1) * lo + pltpu.roll(t, 8, 1) * hi

    def tables(rows):
        return tuple(
            jnp.concatenate([ref[rows, :]] * 3, axis=1) for ref in (cos_ref, sin_lo_ref, sin_hi_ref)
        )

    @over(512, RR, UR)
    def _(start):
        rows = pl.ds(start, RR)
        t = qkv_full[rows, :] + bias_qkv
        cos, lo, hi = tables(rows)
        qk = turn(t[:, :384], cos, lo, hi)
        q_b[rows, :] = (keep_192(qk[:, :256]) * 0.125).astype(bf16)
        k_b[rows, :] = keep_192(pltpu.roll(qk[:, 128:384], 192, 1)).astype(bf16)
        v_b[rows, :] = keep_192(t[:, 384:640]).astype(bf16)

    ctx_f[...] = jnp.zeros_like(ctx_f)
    dq_f[...] = jnp.zeros_like(dq_f)
    dk_f[...] = jnp.zeros_like(dk_f)
    dv_f[...] = jnp.zeros_like(dv_f)
    lane256 = lax.broadcasted_iota(jnp.int32, (1, 256), 1)
    for h in range(3):
        mask = ((lane256 >= h * 64) & (lane256 < (h + 1) * 64)).astype(bf16)
        for block in range(2):
            keys = (block + 1) * 256
            rows_q = slice(block * 256, (block + 1) * 256)
            q_h = q_b[rows_q, :] * mask
            cg_h = cg_b[rows_q, :] * mask
            s_buf[:, :keys] = mm_nt(q_h, k_b[:keys, :])
            dp_buf[:, :keys] = mm_nt(cg_h, v_b[:keys, :])

            @over(256, RA, UA)
            def _(start, keys=keys, block=block):
                rows = pl.ds(start, RA)
                s = s_buf[rows, :keys]
                key_at = lax.broadcasted_iota(jnp.int32, (RA, keys), 1)
                query_at = lax.broadcasted_iota(jnp.int32, (RA, keys), 0) + (block * 256 + start)
                s = jnp.where(key_at <= query_at, s, -jnp.inf)
                e = jnp.exp(s - jnp.max(s, axis=1, keepdims=True))
                dp = dp_buf[rows, :keys]
                share = 1.0 / jnp.sum(e, axis=1, keepdims=True)
                row_dot = jnp.sum(e * dp, axis=1, keepdims=True) * share
                p = e * share
                p_b[rows, :keys] = p.astype(bf16)
                ds_b[rows, :keys] = (p * (dp - row_dot)).astype(bf16)

            ctx_f[rows_q, :] += mm(p_b[:, :keys], v_b[:keys, :] * mask)
            dq_f[rows_q, :] += mm(ds_b[:, :keys], k_b[:keys, :] * mask)
            dk_f[:keys, :] += mm_tn(ds_b[:, :keys], q_h)
            dv_f[:keys, :] += mm_tn(p_b[:, :keys], cg_h)
            if (h, block) == (0, 0):
                z_second(2)
                z_third(0)
            elif (h, block) == (0, 1):
                for d in (1, 2, 3):
                    tu_in[d].wait_recv()
                for k in range(4, 8):
                    z_first(k)
                z_third(1)
            elif (h, block) == (1, 0):
                z_second(3)
            elif (h, block) == (1, 1):
                z_third(2)
            elif (h, block) == (2, 1):
                z_second(4)

    ctx_b[...] = ctx_f[...].astype(bf16)
    out_full[...] = mm_tn(ctx_b[:, :SHARD], g)
    part_send[768 : 768 + ROWS, :] = out_full[at((1 - core) * ROWS, ROWS), :].astype(bf16)
    out_part = send("part_out", part_send.at[768:864], part_recv.at[768:864], twin)


    def unturn_rows(i, totals):
        rows = at(i * 16, 16)
        cos, lo, hi = tables(rows)
        qk = pair_of(dq_f[rows, :] * 0.125, dk_f[rows, :])
        qk = turn(qk, cos, -lo, -hi)
        full = jnp.concatenate([qk, dv_f[rows, :]], axis=1)
        rows_b[rows, :] = full.astype(bf16)
        return totals + full[:8] + full[8:]

    qkv_bias_part = lax.fori_loop(0, 512 // 16, unturn_rows, jnp.zeros((8, 640), f32), unroll=UU)
    qkv_bias_part = jnp.sum(qkv_bias_part, axis=0, keepdims=True)

    up_full[:, :640] = mm_tn(attn_in[...], rows_b[...])
    for j in range(4):
        tq_send[4 + j] = up_full[at(j * SHARD + (1 - core) * ROWS, ROWS), :640].astype(bf16)
    qkv_part = send("part_qkv", tq_send.at[4:8], tq_recv.at[4:8], twin)
    z_third(3)
    out_part.wait_recv()
    chunk[8] = (out_full[at(core * ROWS, ROWS), :] + part_recv[768:864, :].astype(f32)).astype(bf16)
    z_first(8)
    qkv_part.wait_recv()
    for j in range(4):
        tq_send[j] = (
            up_full[at(j * SHARD + core * ROWS, ROWS), :640] + tq_recv[4 + j].astype(f32)
        ).astype(bf16)
    tq_recv[me] = tq_send[me]
    tq_in = {d: send(("tq", d), tq_send.at[peers[d]], tq_recv.at[me], group(d)) for d in (3, 1, 2)}

    z_second(5)
    z_third(4)
    acc_c[...] = mm_nt(preact_b[...], w_up[...])
    acc_b_in = mm_nt(rows_b[...], w_qkv[...])
    z_second(6)
    up_full[0:512, :] = acc_b_in

    def norm_grad_rows(i, totals):
        rows = at(i * 16, 16)
        ag, mg, n = up_full[rows, :], acc_c[rows, :], normed[rows, :]
        both = ag * gain_attn + mg * gain_mlp
        acc_c[rows, :] = both
        rs_in[rows, :] = both.astype(bf16)
        new = (ag * n, ag, mg * n, mg)
        return tuple(t + v[:8] + v[8:] for t, v in zip(totals, new))

    sums = lax.fori_loop(0, 512 // 16, norm_grad_rows, (jnp.zeros((8, D), f32),) * 4, unroll=UN)

    z_third(5)
    z_second(7)

    def rows_sum(t):
        return jnp.sum(t, axis=0, keepdims=True)

    wide = jnp.concatenate(
        [rows_sum(ct[...])] + [rows_sum(t) for t in sums] + [jnp.zeros((3, D), f32)], axis=0
    )
    types = [
        keep_192(qkv_bias_part[:, :256]),
        keep_192(pltpu.roll(qkv_bias_part[:, 128:384], 192, 1)),
        keep_192(qkv_bias_part[:, 384:640]),
    ]
    for j in range(4):
        vec_send[j] = block_of(wide, j)
        for t in range(3):
            b = 3 * j + t
            vec_send[j, 5 + t : 6 + t, :] = jnp.where(me == b % 4, types[b // 4], 0.0)
    vec_in = {d: send(("vec", d), vec_send.at[peers[d]], vec_recv.at[d - 1], group(d)) for d in (3, 1, 2)}
    acc_b[...] += mm(ctx_b[:, :SHARD], w_out[...])
    rs_out[...] = acc_b[...].astype(bf16)
    z_third(6)

    for d in (1, 2, 3):
        tq_in[d].wait_recv()

    @over(ROWS, 16, UC)
    def _(start):
        rows = pl.ds(start, 16)
        parts = [tq_recv[j, rows, :].astype(f32) for j in range(4)]
        for t in range(3):
            if t == 0:
                blocks = [keep_192(v[:, :256]) for v in parts]
            elif t == 1:
                blocks = [keep_192(pltpu.roll(v[:, 128:384], 192, 1)) for v in parts]
            else:
                blocks = [keep_192(v[:, 384:640]) for v in parts]
            chunk[9 + t, rows, :] = jnp.concatenate(
                [pair_of(blocks[0], blocks[1]), pair_of(blocks[2], blocks[3])], axis=1
            ).astype(bf16)

    for k in range(9, 14):
        z_first(k)
    out_in = {
        d: send(("rs_out", d), rs_out.at[at(peers[d] * 128, 128)], rs_out_in.at[d - 1], group(d))
        for d in (3, 1, 2)
    }
    in_in = {
        d: send(("rs_in", d), rs_in.at[at(peers[d] * 128, 128)], rs_in_in.at[d - 1], group(d))
        for d in (3, 1, 2)
    }
    z_second(8)
    z_third(7)
    for n in range(5):
        z_late(n)


    for d in (1, 2, 3):
        vec_in[d].wait_recv()
    vec_core[core, 0:8, :] = vec_send[me] + (vec_recv[0] + vec_recv[1] + vec_recv[2])
    vec_core[core, 8:16, :] = jnp.concatenate(
        [up_bias_part[:, t * 256 : (t + 1) * 256] for t in range(3)] + [jnp.zeros((5, 256), f32)], axis=0
    )
    vec_twin = send("vec_twin", vec_core.at[core], vec_core.at[core], twin)
    z_second(9)
    z_third(8)
    vec_twin.wait_recv()
    vec_z[0] = vec_core[0] + vec_core[1]
    vec_first = remote("vec_z1", vec_z.at[0], vec_z.at[1], z_pair)
    vec_second = remote("vec_z2", vec_z.at[2], vec_z.at[3], z_mid)
    vec_third = remote("vec_z3", vec_ref, vec_ref, z_pair)

    @pl.when(outer)
    def _():
        vec_first.start()

    z_second(10)
    for n in range(5):
        z_fourth(n)
    z_third(9)

    @pl.when(inner)
    def _():
        vec_first.wait_recv()
        vec_z[2] = vec_z[0] + vec_z[1]
        vec_second.start()

    z_second(11)
    for n in range(5, 8):
        z_late(n)
    z_third(10)
    z_second(12)
    z_second(13)

    @pl.when(inner)
    def _():
        vec_second.wait_recv()
        vec_ref[...] = vec_z[2] + vec_z[3]
        vec_third.start()

    for d in (1, 2, 3):
        out_in[d].wait_recv()

    @over(128, 16, UB)
    def _(start):
        rows = pl.ds(start, 16)
        total = acc_b[pl.ds(pl.multiple_of(me * 128 + start, 16), 16), :]
        for d in range(3):
            total = total + rs_out_in[d, rows, :].astype(f32)
        block_ref[rows, :] = x_ref[rows, :].astype(f32) + bias + total


    block_store = pltpu.make_async_copy(block_ref, block_hbm, local_sem.at[33])
    block_store.start()
    z_third(11)
    z_third(12)
    z_third(13)

    for d in (1, 2, 3):
        in_in[d].wait_recv()

    @over(128, 16, UB)
    def _(start):
        rows = pl.ds(start, 16)
        my_rows = pl.ds(pl.multiple_of(me * 128 + start, 16), 16)
        ng = acc_c[my_rows, :]
        for d in range(3):
            ng = ng + rs_in_in[d, rows, :].astype(f32)
        t = x_ref[rows, :].astype(f32)
        centered = t - jnp.mean(t, axis=1, keepdims=True)
        inverse = lax.rsqrt(jnp.mean(centered * centered, axis=1, keepdims=True) + eps)
        n = normed[my_rows, :]
        igrad_ref[rows, :] = ct[rows, :] + inverse * (
            ng - jnp.mean(ng, axis=1, keepdims=True) - n * jnp.mean(ng * n, axis=1, keepdims=True)
        )

    igrad_store = pltpu.make_async_copy(igrad_ref, igrad_hbm, local_sem.at[34])
    igrad_store.start()
    z_late(8)
    for n in range(5, 9):
        z_fourth(n)
    for n in range(9, 14):
        z_late(n)
    for n in range(9, 14):
        z_fourth(n)

    @pl.when(inner)
    def _():
        vec_second.wait_send()
        vec_third.wait_send()

    @pl.when(outer)
    def _():
        vec_first.wait_send()
        vec_third.wait_recv()

    block_store.wait()
    igrad_store.wait()
    for k in range(14):
        z_finish(k)
    for copy in pending:
        copy.wait_send()


def finish_kernel(*refs):
    vec_in, vec_refs, held, wide, in_sems, out_sems = (
        refs[6], refs[13:21], refs[21:27], refs[27:31], refs[31], refs[32],
    )
    pieces = []
    for n, parts in ((3, 1), (5, 4), (4, 4), (2, 4), (0, 1), (1, 1)):
        size = refs[n].shape[0] // parts
        for p in range(parts):
            rows = pl.ds(p * size, size)
            staged = wide[n - 2] if n >= 2 else held[n]
            pieces.append((
                n, rows,
                pltpu.make_async_copy(refs[n].at[rows], held[n].at[rows], in_sems.at[len(pieces)]),
                pltpu.make_async_copy(staged.at[rows], refs[7 + n].at[rows], out_sems.at[len(pieces)]),
            ))
    for piece in pieces:
        piece[2].start()
    for r, target in enumerate(vec_refs[:6]):
        target[...] = vec_in[max(r - 1, 0), :][:SHARD]
    rows = [vec_in[r : r + 1, :] for r in (5, 6, 7)]
    full = jnp.concatenate([pair_of(rows[0], rows[1]), rows[2]], axis=1)
    vec_refs[6][...] = full[:, : 3 * SHARD].reshape(3 * SHARD)
    vec_refs[7][...] = jnp.concatenate([vec_in[r : r + 1, :] for r in (8, 9, 10)], axis=1).reshape(4 * SHARD)
    for n, rows, arrives, leaves in pieces:
        arrives.wait()
        if n >= 2:
            wide[n - 2][rows, :] = held[n][rows, :].astype(jnp.float32)
        leaves.start()
    for piece in pieces:
        piece[3].wait()


def rope_tables(length):
    half_rot = ROT // 2
    lane = np.arange(128) % HD
    frequency = 10000.0 ** (-(lane % half_rot).astype(np.float64) * (2.0 / ROT))
    angles = np.arange(length, dtype=np.float64)[:, None] * frequency[None, :]
    turned = lane < ROT
    cos = np.where(turned, np.cos(angles), 1.0)
    lo = np.where(lane < half_rot, -np.sin(angles), 0.0)
    hi = np.where(turned & (lane >= half_rot), np.sin(angles), 0.0)
    return tuple(t.astype(np.float32) for t in (cos, lo, hi))


def local_fused(
    inputs, qkv_weight, qkv_bias, out_weight, out_bias, up_weight, up_bias, down_weight, down_bias,
    attn_gain, attn_shift, mlp_gain, mlp_shift, cotangent,
):
    f32, bf16 = jnp.float32, jnp.bfloat16
    length = 512
    def vmem(shape, dtype):
        return pltpu.VMEM(shape, dtype)

    inside = pl.BlockSpec(memory_space=pltpu.VMEM)
    anywhere = pl.BlockSpec(memory_space=pl.ANY)
    big = (length, D)
    outs = pl.pallas_call(
        block_kernel,
        out_shape=(
            jax.ShapeDtypeStruct((128, D), f32),
            jax.ShapeDtypeStruct((128, D), f32),
            jax.ShapeDtypeStruct((SHARD, 3 * D), bf16),
            jax.ShapeDtypeStruct((SHARD, D), bf16),
            jax.ShapeDtypeStruct((SHARD, 4 * D), bf16),
            jax.ShapeDtypeStruct((D, D), bf16),
            jax.ShapeDtypeStruct((16, 256), f32),
        ),
        in_specs=[inside] * 12 + [anywhere] * 5,
        out_specs=(anywhere,) * 6 + (inside,),
        scratch_shapes=[
            vmem((128, D), f32), vmem((128, D), f32),
            vmem((SHARD, 3 * D), bf16), vmem((SHARD, D), bf16), vmem((SHARD, 4 * D), bf16), vmem((D, D), bf16),
            vmem((128, D), f32), vmem((SHARD, 3 * D), bf16), vmem((D, D), bf16), vmem((SHARD, D), bf16),
            vmem((4, SHARD, 640), bf16), vmem((D, 640), bf16), vmem((D, D), bf16),
            vmem(big, bf16), vmem(big, bf16), vmem((4, 16, 256), f32), vmem((1, 640), f32), vmem((2, 48, D), bf16),
            vmem((2, 48, 640), bf16), vmem(big, f32), vmem(big, bf16),
            vmem(big, bf16),
            vmem(big, f32), vmem(big, f32), vmem(big, f32), vmem(big, bf16), vmem(big, bf16),
            vmem((length, 256), bf16), vmem((length, 256), bf16), vmem((length, 256), bf16),
            vmem((length, 256), bf16), vmem((length, 256), f32), vmem((length, 256), bf16),
            vmem((256, length), f32), vmem((256, length), f32), vmem((256, length), bf16),
            vmem((256, length), bf16), vmem((length, 256), f32), vmem((length, 256), f32),
            vmem((length, 256), f32), vmem((length, 640), bf16),
            vmem((384, D), f32), vmem((D, D), f32), vmem((length, 640), f32), vmem((SHARD, D), f32),
            vmem((864, D), bf16), vmem((864, D), bf16), vmem((8, ROWS, 640), bf16), vmem((8, ROWS, 640), bf16),
            vmem((4, ROWS, D), bf16), vmem((12, ROWS, D), bf16), vmem((12, ROWS, D), bf16),
            vmem((12, ROWS, D), bf16), vmem((12, ROWS, D), bf16),
            vmem(big, bf16), vmem((3, 128, D), bf16), vmem(big, bf16), vmem((3, 128, D), bf16),
            vmem((4, 8, 256), f32), vmem((3, 8, 256), f32), vmem((2, 16, 256), f32), vmem((4, 16, 256), f32),
            pltpu.SemaphoreType.DMA((NSEM,)), pltpu.SemaphoreType.DMA((NSEM,)), pltpu.SemaphoreType.DMA((35,)),
        ],
        compiler_params=pltpu.CompilerParams(
            collective_id=0, has_side_effects=True, vmem_limit_bytes=56 * 1024 * 1024
        ),
    )(
        inputs[0], qkv_bias, out_bias, down_bias, attn_gain, attn_shift, mlp_gain, mlp_shift, up_bias,
        *(jnp.asarray(t) for t in rope_tables(length)),
        cotangent[0], qkv_weight, up_weight, down_weight, out_weight,
    )
    widths = [SHARD] * 6 + [3 * SHARD, 4 * SHARD]
    (
        block_out, input_grad, gqkv, gout, gup, gdown,
        out_bias_sum, down_bias_sum, gain_attn, shift_attn, gain_mlp, shift_mlp, bqkv, bup,
    ) = pl.pallas_call(
        finish_kernel,
        out_shape=tuple(jax.ShapeDtypeStruct(t.shape, f32) for t in outs[:6])
        + tuple(jax.ShapeDtypeStruct((n,), f32) for n in widths),
        in_specs=[anywhere] * 6 + [inside],
        out_specs=(anywhere,) * 6 + (inside,) * 8,
        scratch_shapes=[vmem(t.shape, t.dtype) for t in outs[:6]]
        + [vmem(t.shape, f32) for t in outs[2:6]]
        + [pltpu.SemaphoreType.DMA((15,)), pltpu.SemaphoreType.DMA((15,))],
        compiler_params=pltpu.CompilerParams(vmem_limit_bytes=56 * 1024 * 1024),
    )(*outs)
    return (
        block_out[None], input_grad[None], gqkv, bqkv, gout, out_bias_sum, gup, bup, gdown, down_bias_sum,
        gain_attn, shift_attn, gain_mlp, shift_mlp,
    )


def solution(mesh):
    fused = (mesh.shape["grp"], mesh.shape["rep"]) == (4, 8)
    local = local_fused if fused else local_by_tokens
    placed = (
        P("rep", "grp", None),
        P("grp", None),
        P("grp"),
        P("grp", None),
        P("grp"),
        P("grp", None),
        P("grp"),
        P("grp", None),
        P("grp"),
        P("grp"),
        P("grp"),
        P("grp"),
        P("grp"),
        P("rep", "grp", None),
    )
    return jax.shard_map(
        local,
        mesh=mesh,
        in_specs=placed,
        out_specs=(
            P("rep", "grp", None),
            P("rep", "grp", None),
            P("grp", None),
            P("grp"),
            P("grp", None),
            P("grp"),
            P("grp", None),
            P("grp"),
            P("grp", None),
            P("grp"),
            P("grp"),
            P("grp"),
            P("grp"),
            P("grp"),
        ),
        check_vma=False,
    )
```
